32 devices in a mesh: dp: 16 (over z, x, core), mp: 2 (over y).
Axes of the slice: x: 2, y: 2, z: 4, core: 2. Of those that a mesh axis runs over, the one named last changes fastest.
Arguments:
- text_states: bfloat16 [32768, 768], P(('dp', 'mp')), may hold values from -6 to 6
- layout_states: bfloat16 [32768, 192], P(('dp', 'mp')), may hold values from -6 to 6
- box_counts: int32 [64], P('dp'), may hold values from 17 to 512, as said below
- text_qkv: bfloat16 [768, 3, 768], P(None, None, 'mp'), may hold values from -0.21875 to 0.21875
- text_qv_bias: float32 [2, 768], P(None, 'mp'), may hold values from -3 to 3
- text_out: bfloat16 [768, 768], P('mp'), may hold values from -1.75 to 1.75
- text_up: bfloat16 [768, 3072], P(None, 'mp'), may hold values from -0.21875 to 0.21875
- text_up_bias: float32 [3072], P('mp'), may hold values from -3 to 3
- text_down: bfloat16 [3072, 768], P('mp'), may hold values from -0.109375 to 0.109375
- text_gains: float32 [2, 768], replicated, may hold values from 0.25 to 1.75
- text_shifts: float32 [4, 768], replicated, may hold values from -3 to 3
- layout_qkv: bfloat16 [192, 3, 192], P(None, None, 'mp'), may hold values from -0.4375 to 0.4375
- layout_qv_bias: float32 [2, 192], P(None, 'mp'), may hold values from -3 to 3
- layout_out: bfloat16 [192, 192], P('mp'), may hold values from -1.75 to 1.75
- layout_up: bfloat16 [192, 768], P(None, 'mp'), may hold values from -0.4375 to 0.4375
- layout_up_bias: float32 [768], P('mp'), may hold values from -3 to 3
- layout_down: bfloat16 [768, 192], P('mp'), may hold values from -0.21875 to 0.21875
- layout_gains: float32 [2, 192], replicated, may hold values from 0.25 to 1.75
- layout_shifts: float32 [4, 192], replicated, may hold values from -3 to 3
- cot_text: bfloat16 [32768, 768], P(('dp', 'mp')), may hold values from -6 to 6
- cot_layout: bfloat16 [32768, 192], P(('dp', 'mp')), may hold values from -6 to 6
Outputs:
- out_text: bfloat16 [32768, 768], P(('dp', 'mp'))
- out_layout: bfloat16 [32768, 192], P(('dp', 'mp'))
- grad_text_states: float32 [32768, 768], P(('dp', 'mp'))
- grad_layout_states: float32 [32768, 192], P(('dp', 'mp'))
- grad_text_qkv: float32 [768, 3, 768], P(None, None, 'mp')
- grad_text_qv_bias: float32 [2, 768], P(None, 'mp')
- grad_text_out: float32 [768, 768], P('mp')
- grad_text_up: float32 [768, 3072], P(None, 'mp')
- grad_text_up_bias: float32 [3072], P('mp')
- grad_text_down: float32 [3072, 768], P('mp')
- grad_text_gains: float32 [2, 768], replicated
- grad_text_shifts: float32 [4, 768], replicated
- grad_layout_qkv: float32 [192, 3, 192], P(None, None, 'mp')
- grad_layout_qv_bias: float32 [2, 192], P(None, 'mp')
- grad_layout_out: float32 [192, 192], P('mp')
- grad_layout_up: float32 [192, 768], P(None, 'mp')
- grad_layout_up_bias: float32 [768], P('mp')
- grad_layout_down: float32 [768, 192], P('mp')
- grad_layout_gains: float32 [2, 192], replicated
- grad_layout_shifts: float32 [4, 192], replicated
The draws below stay inside these ranges and needn't reach their ends.
Inputs may be any that keep to these rules, and one draw needn't show every extreme that they name: `box_counts`: some page is full (512) in every draw, and some page has the fewest that the range allows.
All inputs are finite; a program needn't handle non-finite values.
Results may differ from the reference program's by a relative error of at most 0.023.
Values may be sent and summed in bfloat16 or wider, within the bound.
A program may use at most 192 MiB of HBM per device.

```python
import math
import jax
import jax.numpy as jnp
from jax import lax

HEADS = 12
HD = 64
HDL = 16
D = 768
DL = 192
FF = 3072
FFL = 768
SEQ = 512
PAGES = 64
TOKENS = 32768
N_MP = 2


def draw_box_counts(key, part):
    key_level, key_jitter, key_full, key_few = jax.random.split(jax.random.fold_in(key, 17), 4)
    jitter_span = max(SEQ // 32, 1)
    octave = jax.random.randint(key_level, (PAGES,), 0, 5)
    base_count = SEQ // jnp.left_shift(jnp.int32(1), octave)
    jitter = jax.random.randint(key_jitter, (PAGES,), 0, jitter_span)
    counts = jnp.maximum(base_count - jitter, 2)
    chosen = jax.random.randint(key_full, (), 0, PAGES)
    fewest = (chosen + 1 + jax.random.randint(key_few, (), 0, PAGES - 1)) % PAGES
    least = max(SEQ // 16 - jitter_span + 1, 2)
    positions = jnp.arange(PAGES)
    counts = jnp.where(positions == fewest, least, counts)
    return jnp.where(positions == chosen, SEQ, counts).astype(jnp.int32)


def block_levels(rng, dims, cuts, low, largest):
    def one(dim, shards_of):
        steps = jax.random.uniform(jax.random.fold_in(jax.random.fold_in(rng, 6), dim), (shards_of,), jnp.float32, low / len(cuts), largest / len(cuts))
        return jnp.repeat(jnp.exp(steps), dims[dim] // shards_of).reshape((-1,) + (1,) * (len(dims) - dim - 1))

    level = one(*cuts[0])
    for cut in cuts[1:]:
        level = level * one(*cut)
    return level


def gaussian(rng, dims, width, bound, shards=(), kind=jnp.bfloat16):
    entries = jax.random.normal(rng, dims, jnp.float32) * width
    if len(shards) > 0:
        entries = block_levels(rng, dims, shards, -0.22, 0.18) * entries
    return jnp.clip(entries, min=-bound, max=bound).astype(kind)


def setup_inputs(seed: int = 0) -> dict:
    seeds = jax.random.split(jax.random.key(seed), 22)
    text_states = gaussian(seeds[0], (TOKENS, D), 1.0, 6.0, ((0, 32),))
    layout_states = gaussian(seeds[1], (TOKENS, DL), 1.0, 6.0, ((0, 32),))
    box_counts = draw_box_counts(jax.random.fold_in(seeds[21], 71), 0)
    text_qkv = gaussian(seeds[3], (D, 3, D), D ** -0.5, 0.21875, ((2, 2),))
    text_qv_bias = gaussian(seeds[4], (2, D), 0.5, 3.0, ((1, 2),), jnp.float32)
    text_out = gaussian(seeds[5], (D, D), (D // 64) ** -0.5, 1.75, ((0, 2),))
    text_up = gaussian(seeds[6], (D, FF), D ** -0.5, 0.21875, ((1, 2),))
    text_up_bias = gaussian(seeds[7], (FF,), 0.5, 3.0, ((0, 2),), jnp.float32)
    text_down = gaussian(seeds[8], (FF, D), FF ** -0.5, 0.109375, ((0, 2),))
    text_gains = jnp.clip(1.0 + 0.15 * jax.random.normal(seeds[9], (2, D), jnp.float32), 0.25, 1.75)
    text_shifts = gaussian(seeds[10], (4, D), 0.5, 3.0, (), jnp.float32)
    layout_qkv = gaussian(seeds[11], (DL, 3, DL), DL ** -0.5, 0.4375, ((2, 2),))
    layout_qv_bias = gaussian(seeds[12], (2, DL), 0.5, 3.0, ((1, 2),), jnp.float32)
    layout_out = gaussian(seeds[13], (DL, DL), (DL // 16) ** -0.5, 1.75, ((0, 2),))
    layout_up = gaussian(seeds[14], (DL, FFL), DL ** -0.5, 0.4375, ((1, 2),))
    layout_up_bias = gaussian(seeds[15], (FFL,), 0.5, 3.0, ((0, 2),), jnp.float32)
    layout_down = gaussian(seeds[16], (FFL, DL), FFL ** -0.5, 0.21875, ((0, 2),))
    layout_gains = jnp.clip(1.0 + 0.15 * jax.random.normal(seeds[17], (2, DL), jnp.float32), 0.25, 1.75)
    layout_shifts = gaussian(seeds[18], (4, DL), 0.5, 3.0, (), jnp.float32)
    cot_text = gaussian(seeds[19], (TOKENS, D), 1.0, 6.0, ((0, 32),))
    cot_layout = gaussian(seeds[20], (TOKENS, DL), 1.0, 6.0, ((0, 32),))
    return {"text_states": text_states, "layout_states": layout_states, "box_counts": box_counts, "text_qkv": text_qkv, "text_qv_bias": text_qv_bias, "text_out": text_out, "text_up": text_up, "text_up_bias": text_up_bias, "text_down": text_down, "text_gains": text_gains, "text_shifts": text_shifts, "layout_qkv": layout_qkv, "layout_qv_bias": layout_qv_bias, "layout_out": layout_out, "layout_up": layout_up, "layout_up_bias": layout_up_bias, "layout_down": layout_down, "layout_gains": layout_gains, "layout_shifts": layout_shifts, "cot_text": cot_text, "cot_layout": cot_layout}


epsilon = 1e-05
masked_value = -1e+30
highest = lax.Precision.HIGHEST

@jax.custom_vjp
def low(v):
    return lax.optimization_barrier(v.astype(jnp.bfloat16)).astype(jnp.float32)

@jax.custom_vjp
def low_back(v):
    return v

def low_keep(v):
    return (low(v), None)

def low_pass(kept, grad):
    return (grad,)

def back_keep(v):
    return (v, None)

def back_low(kept, grad):
    return (low(grad),)
low.defvjp(low_keep, low_pass)
low_back.defvjp(back_keep, back_low)

def layer_norm(residual, gain_row, shift_row):
    row_mean = lax.optimization_barrier(jnp.mean(residual, -1, keepdims=True))
    centred = residual - row_mean
    spread = lax.optimization_barrier(jnp.mean(centred * centred, -1, keepdims=True))
    return centred * lax.rsqrt(spread + epsilon) * gain_row + shift_row

def project(states, weight, bias_pair):
    group_width = weight.shape[2] // N_MP
    pieces = []
    for member in range(N_MP):
        columns = weight[:, :, member * group_width:(member + 1) * group_width]
        pieces.append(jnp.einsum('td,dkf->tkf', low_back(states), columns, precision=highest))
    mixed = jnp.concatenate(pieces, 2)
    zero_row = jnp.zeros_like(bias_pair[0])
    mixed = mixed + jnp.stack([bias_pair[0], zero_row, bias_pair[1]])[None]
    return low_back(low(mixed))

def group_sum(left, right_weight):
    group_width = right_weight.shape[0] // N_MP
    summed = None
    for member in range(N_MP):
        unit_span = slice(member * group_width, (member + 1) * group_width)
        term = low(jnp.dot(left[:, unit_span], right_weight[unit_span], precision=highest))
        summed = term if summed is None else summed + term
    return low_back(summed)

def attend(page_block):
    text_page, layout_page, is_live = page_block
    text_scores = jnp.einsum('qhd,khd->hqk', text_page[:, 0], text_page[:, 1], precision=highest)
    layout_scores = jnp.einsum('qhd,khd->hqk', layout_page[:, 0], layout_page[:, 1], precision=highest)
    scores = low_back(text_scores / math.sqrt(HD) + layout_scores / math.sqrt(HDL))
    scores = jnp.where(is_live[None, None, :], scores, masked_value)
    row_top = lax.optimization_barrier(jnp.max(scores, -1, keepdims=True))
    log_total = row_top + jnp.log(lax.optimization_barrier(jnp.sum(jnp.exp(scores - row_top), -1, keepdims=True)))
    attend_weight = low(jnp.exp(scores - log_total))
    text_context = jnp.einsum('hqk,khd->qhd', attend_weight, text_page[:, 2], precision=highest)
    layout_context = jnp.einsum('hqk,khd->qhd', attend_weight, layout_page[:, 2], precision=highest)
    return (text_context, layout_context)

def finish(states, context, out_weight, up_weight, up_bias, down_weight, gains, shifts):
    attention = group_sum(context, out_weight)
    normed = layer_norm(states + attention + shifts[2], gains[0], shifts[0])
    normed_low = low(normed)
    group_width = up_weight.shape[1] // N_MP
    summed = None
    for member in range(N_MP):
        unit_span = slice(member * group_width, (member + 1) * group_width)
        preact = low_back(jnp.dot(low_back(normed_low), up_weight[:, unit_span], precision=highest) + up_bias[unit_span])
        activation = low(jax.nn.gelu(preact, approximate=False))
        term = low(jnp.dot(activation, down_weight[unit_span], precision=highest))
        summed = term if summed is None else summed + term
    feed_forward = low_back(summed)
    return layer_norm(normed + feed_forward + shifts[3], gains[1], shifts[1])

def whole_layer(params, text_rows, layout_rows, box_group):
    token_count = text_rows.shape[0]
    page_count = token_count // SEQ
    text_mixed = project(text_rows, params[0], params[1]).reshape(page_count, SEQ, 3, HEADS, HD)
    layout_mixed = project(layout_rows, params[8], params[9]).reshape(page_count, SEQ, 3, HEADS, HDL)
    is_live = jnp.arange(SEQ)[None, :] < box_group[:, None]
    text_context, layout_context = lax.map(jax.checkpoint(attend), (text_mixed, layout_mixed, is_live))
    text_context = low_back(low(text_context.reshape(token_count, HEADS * HD)))
    layout_context = low_back(low(layout_context.reshape(token_count, HEADS * HDL)))
    text_result = finish(text_rows, text_context, params[2], params[3], params[4], params[5], params[6], params[7])
    layout_result = finish(layout_rows, layout_context, params[10], params[11], params[12], params[13], params[14], params[15])
    return (text_result, layout_result)

def reference(text_states, layout_states, box_counts, text_qkv, text_qv_bias, text_out, text_up, text_up_bias, text_down, text_gains, text_shifts, layout_qkv, layout_qv_bias, layout_out, layout_up, layout_up_bias, layout_down, layout_gains, layout_shifts, cot_text, cot_layout):
    params = tuple((argument.astype(jnp.float32) for argument in (text_qkv, text_qv_bias, text_out, text_up, text_up_bias, text_down, text_gains, text_shifts, layout_qkv, layout_qv_bias, layout_out, layout_up, layout_up_bias, layout_down, layout_gains, layout_shifts)))
    group_pages = min(8, PAGES)
    group_count = PAGES // group_pages
    group_rows = group_pages * SEQ

    def regroup(source):
        return source.astype(jnp.float32).reshape(group_count, group_rows, source.shape[1])
    inputs = (regroup(text_states), regroup(layout_states), box_counts.reshape(group_count, group_pages), regroup(cot_text), regroup(cot_layout))

    def one_group(running, page_block):
        text_rows, layout_rows, box_group, text_cot, layout_cot = page_block

        def forward(weights, text_part, layout_part):
            return whole_layer(weights, text_part, layout_part, box_group)
        results, pullback = jax.vjp(forward, params, text_rows, layout_rows)
        grad_parts, text_grad, layout_grad = pullback((text_cot, layout_cot))
        running = jax.tree.map(lambda left, right: left + right, running, grad_parts)
        return (running, (results[0].astype(jnp.bfloat16), results[1].astype(jnp.bfloat16), text_grad, layout_grad))
    summed, (text_outs, layout_outs, text_grads, layout_grads) = lax.scan(one_group, jax.tree.map(jnp.zeros_like, params), inputs)
    return (text_outs.reshape(TOKENS, D), layout_outs.reshape(TOKENS, DL), text_grads.reshape(TOKENS, D), layout_grads.reshape(TOKENS, DL), summed[0], summed[1], summed[2], summed[3], summed[4], summed[5], summed[6], summed[7], summed[8], summed[9], summed[10], summed[11], summed[12], summed[13], summed[14], summed[15])
```

```python
import functools

import jax
import jax.numpy as jnp
from jax import lax
from jax.experimental import pallas as pl
from jax.experimental.pallas import tpu as pltpu
from jax.sharding import Mesh, PartitionSpec as P

f32 = jnp.float32
bf16 = jnp.bfloat16
SEQ = 512
NT = (((1,), (1,)), ((), ()))
TN = (((0,), (0,)), ((), ()))

def head_masks(h):
    lane=lax.broadcasted_iota(jnp.int32,(1,256),1)
    t=(lane>=64*(h%2))&(lane<64*(h%2)+64)
    l=(lane>=128+16*h)&(lane<128+16*h+16)
    return t|l, t|l|(lane==224)

def k1t_body(cnt, xt, xl, wt, bt, wl, bl, qkvt, qkvl, lse_o, ctxt, ctxl, cT, clT):
    n=cnt[pl.program_id(0)]
    lane=lax.broadcasted_iota(jnp.int32,(SEQ,128),1)
    row=lax.broadcasted_iota(jnp.int32,(SEQ,128),0)
    for c in range(3):
        r=jnp.dot(xt[...],wt[c],preferred_element_type=f32)+bt[c:c+1]
        s=jnp.dot(xl[...],wl[c],preferred_element_type=f32)+bl[c:c+1]
        if c==0:
            r=r*0.125; s=jnp.where(lane==96,1.0,s*0.25)
        if c==1:
            s=jnp.where((lane==96)&(row>=n),-1e30,s)
        qkvt[c]=r.astype(bf16); qkvl[c]=s.astype(bf16)
    vlT=qkvl[2].T
    for p in range(3):
        ps=pl.ds(128*p,128)
        qc=jnp.concatenate([qkvt[0,:,ps],qkvl[0]],axis=1)
        kc=jnp.concatenate([qkvt[1,:,ps],qkvl[1]],axis=1)
        vtT=qkvt[2,:,ps].T
        for hh in range(2):
            h=2*p+hh
            mv,mk=head_masks(h)
            km=jnp.where(mk,kc,jnp.zeros_like(kc))
            S=lax.dot_general(km,qc,NT,preferred_element_type=f32)
            m=jnp.max(S,axis=0,keepdims=True)
            e=jnp.exp(S-m)
            l=jnp.sum(e,axis=0,keepdims=True)
            vT=jnp.concatenate([vtT[64*hh:64*hh+64],vlT[16*h:16*h+16]],axis=0)
            o=jnp.dot(vT,e.astype(bf16),preferred_element_type=f32)*(1.0/l)
            cT[64*hh:64*hh+64,:]=o[:64]
            clT[16*h:16*h+16,:]=o[64:]
            lse_o[0,h:h+1,:]=m+jnp.log(l)
        ctxt[:,ps]=cT[...].T.astype(bf16)
    clT[96:,:]=jnp.zeros((32,SEQ),f32)
    ctxl[...]=clT[...].T.astype(bf16)
    lse_o[0,6:8,:]=jnp.zeros((2,SEQ),f32)

def attn_fwd2(cnt, xt, xl, wt, bt, wl, bl):
    T=xt.shape[0]; n=T//SEQ
    full=lambda s: pl.BlockSpec(s,lambda i,*_:(0,)*len(s),pipeline_mode=pl.Buffered(1))
    return pl.pallas_call(k1t_body,
        grid_spec=pltpu.PrefetchScalarGridSpec(num_scalar_prefetch=1,grid=(n,),
          in_specs=[pl.BlockSpec((SEQ,768),lambda i,*_:(i,0)),pl.BlockSpec((SEQ,192),lambda i,*_:(i,0)),
            full((3,768,384)),full((3,384)),full((3,192,128)),full((3,128))],
          out_specs=[pl.BlockSpec((3,SEQ,384),lambda i,*_:(0,i,0)),pl.BlockSpec((3,SEQ,128),lambda i,*_:(0,i,0)),
            pl.BlockSpec((1,8,SEQ),lambda i,*_:(i,0,0)),pl.BlockSpec((SEQ,384),lambda i,*_:(i,0)),pl.BlockSpec((SEQ,128),lambda i,*_:(i,0))],
          scratch_shapes=[pltpu.VMEM((128,SEQ),f32),pltpu.VMEM((128,SEQ),f32)]),
        out_shape=[jax.ShapeDtypeStruct((3,T,384),bf16),jax.ShapeDtypeStruct((3,T,128),bf16),jax.ShapeDtypeStruct((n,8,SEQ),f32),
            jax.ShapeDtypeStruct((T,384),bf16),jax.ShapeDtypeStruct((T,128),bf16)],
        compiler_params=pltpu.CompilerParams(vmem_limit_bytes=56<<20),
        name="attend_forward",
    )(cnt,xt,xl,wt,bt,wl,bl)

def k6_body(dat, dal, wot, wol, qkvt, qkvl, lse, dqkvt, dqkvl, dqT, dqlT, dcl, *, unused=0):
    dct=lax.dot_general(dat[...],wot[...],NT,preferred_element_type=f32).astype(bf16)
    dcl_=lax.dot_general(dal[...],wol[...],NT,preferred_element_type=f32).astype(bf16)
    accvl=jnp.zeros((SEQ,128),f32); acckl=jnp.zeros((SEQ,128),f32)
    klT=qkvl[1].T
    for p in range(3):
        ps=pl.ds(128*p,128)
        qc=jnp.concatenate([qkvt[0,:,ps],qkvl[0]],axis=1)
        kc=jnp.concatenate([qkvt[1,:,ps],qkvl[1]],axis=1)
        vc=jnp.concatenate([qkvt[2,:,ps],qkvl[2]],axis=1)
        dc=jnp.concatenate([dct[:,128*p:128*p+128],dcl_],axis=1)
        ktT=qkvt[1,:,ps].T
        accv=jnp.zeros((SEQ,128),f32); acck=jnp.zeros((SEQ,128),f32)
        for hh in range(2):
            h=2*p+hh
            mv,mk=head_masks(h)
            z=jnp.zeros_like(kc)
            km=jnp.where(mk,kc,z); vm=jnp.where(mv,vc,z); dm=jnp.where(mv,dc,z); qm=jnp.where(mv,qc,z)
            ST=lax.dot_general(km,qc,NT,preferred_element_type=f32)
            E=jnp.exp(ST-lse[0,h:h+1,:])
            dPT=lax.dot_general(vm,dc,NT,preferred_element_type=f32)
            X=E*dPT
            delta=jnp.sum(X,axis=0,keepdims=True)
            dS=(X-E*delta).astype(bf16)
            ov=jnp.dot(E.astype(bf16),dm,preferred_element_type=f32)
            ok=jnp.dot(dS,qm,preferred_element_type=f32)
            accv=accv+ov[:,:128]; accvl=accvl+ov[:,128:]
            acck=acck+ok[:,:128]; acckl=acckl+ok[:,128:]
            kT=jnp.concatenate([ktT[64*hh:64*hh+64],klT[16*h:16*h+16]],axis=0)
            oq=jnp.dot(kT,dS,preferred_element_type=f32)
            dqT[64*hh:64*hh+64,:]=oq[:64]*0.125
            dqlT[16*h:16*h+16,:]=oq[64:]*0.25
        dqkvt[0,:,ps]=dqT[...].T.astype(bf16)
        dqkvt[1,:,ps]=acck.astype(bf16)
        dqkvt[2,:,ps]=accv.astype(bf16)
    dqlT[96:,:]=jnp.zeros((32,SEQ),f32)
    dqkvl[0]=dqlT[...].T.astype(bf16)
    dqkvl[1]=acckl.astype(bf16)
    dqkvl[2]=accvl.astype(bf16)

def attn_bwd(dat,dal,wot,wol,qkvt,qkvl,lse):
    T=dat.shape[0]; n=T//SEQ
    full=lambda s: pl.BlockSpec(s,lambda i:(0,)*len(s),pipeline_mode=pl.Buffered(1))
    return pl.pallas_call(k6_body,grid=(n,),
        in_specs=[pl.BlockSpec((SEQ,768),lambda i:(i,0)),pl.BlockSpec((SEQ,192),lambda i:(i,0)),full((384,768)),full((128,192)),
          pl.BlockSpec((3,SEQ,384),lambda i:(0,i,0)),pl.BlockSpec((3,SEQ,128),lambda i:(0,i,0)),pl.BlockSpec((1,8,SEQ),lambda i:(i,0,0))],
        out_specs=[pl.BlockSpec((3,SEQ,384),lambda i:(0,i,0)),pl.BlockSpec((3,SEQ,128),lambda i:(0,i,0))],
        out_shape=[jax.ShapeDtypeStruct((3,T,384),bf16),jax.ShapeDtypeStruct((3,T,128),bf16)],
        scratch_shapes=[pltpu.VMEM((128,SEQ),f32),pltpu.VMEM((128,SEQ),f32),pltpu.VMEM((SEQ,128),f32)],
        compiler_params=pltpu.CompilerParams(vmem_limit_bytes=56<<20),
        name="attend_backward",
    )(dat,dal,wot,wol,qkvt,qkvl,lse)

GC=[0.11609199498651965, 0.07018864201817518, 0.2621979336040309, -0.22868178430415115, 0.38476147983842124, -0.10455825070574547]
GP=0.28
def gelu_pair(v):
    t=1.0/(1.0+GP*jnp.abs(v))
    g=jnp.exp(v*v*-0.5)
    q=GC[5]
    for c in GC[4::-1]: q=q*t+c
    q=q*t*g
    phi=jnp.where(v<0,q,1.0-q)
    return v*phi, phi+v*g*0.3989422804014327

def norm_stats(r):
    mean=jnp.mean(r,-1,keepdims=True)
    cen=r-mean
    rstd=lax.rsqrt(jnp.mean(cen*cen,-1,keepdims=True)+1e-5)
    return cen*rstd, rstd

def norm_back(e,n,rstd):
    return (e-jnp.mean(e,-1,keepdims=True)-n*jnp.mean(e*n,-1,keepdims=True))*rstd

def m_body(x, co, cp, wo, wp, upo, upp, dno, dnp, bo, bp, gains, shifts, cot,
           out, dr1o, dao, h1o, act, dpre, dfo, sums, bsum, gp_s, n1_s, *, CH):
    W=upo.shape[1]; nc=W//CH
    colsum=lambda v: jnp.sum(v,axis=0,keepdims=True)
    attn=jnp.dot(co[...],wo[...],preferred_element_type=f32)+jnp.dot(cp[...],wp[...],preferred_element_type=f32)
    n1,rstd1=norm_stats(x[...].astype(f32)+attn+shifts[2:3])
    n1_s[...]=n1
    h1=n1*gains[0:1]+shifts[0:1]
    h1b=h1.astype(bf16); h1o[...]=h1b
    ffn=None
    for hf,(up,dn,b) in enumerate(((upo,dno,bo),(upp,dnp,bp))):
        for c in range(nc):
            cs=slice(c*CH,(c+1)*CH)
            pre=jnp.dot(h1b,up[:,cs],preferred_element_type=f32)+b[:,cs]
            a,g=gelu_pair(pre)
            ab=a.astype(bf16)
            act[hf,:,cs]=ab; gp_s[hf,:,cs]=g.astype(gp_s.dtype)
            t=jnp.dot(ab,dn[cs,:],preferred_element_type=f32)
            ffn=t if ffn is None else ffn+t
    n2,rstd2=norm_stats(n1_s[...]*gains[0:1]+shifts[0:1]+ffn+shifts[3:4])
    out[...]=(n2*gains[1:2]+shifts[1:2]).astype(bf16)
    ct=cot[...].astype(f32)
    dr2=norm_back(ct*gains[1:2],n2,rstd2)
    df=dr2.astype(bf16); dfo[...]=df
    s_g2=colsum(ct*n2); s_s2=colsum(ct); s_r2=colsum(dr2)
    dh1=dr2
    first=pl.program_id(0)==0
    for hf,(up,dn) in enumerate(((upo,dno),(upp,dnp))):
        for c in range(nc):
            cs=slice(c*CH,(c+1)*CH)
            da_=lax.dot_general(df,dn[cs,:],NT,preferred_element_type=f32)
            dp=(da_*gp_s[hf,:,cs].astype(f32)).astype(bf16)
            dpre[hf,:,cs]=dp
            bs=colsum(dp.astype(f32))
            bsum[hf,:,cs]=jnp.where(first,bs,bsum[hf,:,cs]+bs)
            dh1=dh1+lax.dot_general(dp,up[:,cs],NT,preferred_element_type=f32)
    n1=n1_s[...]
    s_g1=colsum(dh1*n1); s_s1=colsum(dh1)
    dr1=norm_back(dh1*gains[0:1],n1,rstd1)
    dr1o[...]=dr1; dao[...]=dr1.astype(bf16)
    tot=jnp.concatenate([s_g1,s_g2,s_s1,s_s2,colsum(dr1),s_r2,jnp.zeros((2,s_g1.shape[1]),f32)],axis=0)
    sums[...]=jnp.where(first,tot,sums[...]+tot)

def middle(x,co,cp,wo,wp,upo,upp,dno,dnp,bo,bp,gains,shifts,cot,*,CH,R=512,GD=f32,name):
    T,D=x.shape; W=upo.shape[1]
    full=lambda a: pl.BlockSpec(a.shape,lambda i:(0,)*a.ndim,pipeline_mode=pl.Buffered(1))
    rows=lambda w: pl.BlockSpec((R,w),lambda i:(i,0))
    rows3=lambda w: pl.BlockSpec((2,R,w),lambda i:(0,i,0))
    const=lambda s: pl.BlockSpec(s,lambda i:(0,)*len(s))
    sd=jax.ShapeDtypeStruct
    return pl.pallas_call(functools.partial(m_body,CH=CH),grid=(T//R,),
        in_specs=[rows(D),rows(co.shape[1]),rows(co.shape[1])]+[full(a) for a in (wo,wp,upo,upp,dno,dnp,bo,bp,gains,shifts)]+[rows(D)],
        out_specs=[rows(D),rows(D),rows(D),rows(D),rows3(W),rows3(W),rows(D),const((8,D)),const((2,1,W))],
        out_shape=[sd((T,D),bf16),sd((T,D),f32),sd((T,D),bf16),sd((T,D),bf16),sd((2,T,W),bf16),sd((2,T,W),bf16),sd((T,D),bf16),sd((8,D),f32),sd((2,1,W),f32)],
        scratch_shapes=[pltpu.VMEM((2,R,W),GD),pltpu.VMEM((R,D),f32)],
        compiler_params=pltpu.CompilerParams(vmem_limit_bytes=62<<20),name=name,
    )(x,co,cp,wo,wp,upo,upp,dno,dnp,bo,bp,gains,shifts,cot)


AX = ("group", "chip", "core", "mp")
SWAP = [(0, 1), (1, 0)]


def fetch(w):
    core = lax.axis_index("core")
    n = w.shape[0] // 2
    mine = lax.dynamic_slice_in_dim(w, core * n, n, 0)
    got = lax.ppermute(mine, "mp", SWAP)
    sib = lax.ppermute(got, "core", SWAP)
    return jnp.where(core == 0, jnp.concatenate([got, sib], 0), jnp.concatenate([sib, got], 0))


def bit_pairs(n, bit):
    return [(i, i ^ bit) for i in range(n)]


def reduce_all(own, other, n_group, n_chip):
    core = lax.axis_index("core")
    chip = lax.axis_index("chip")
    take = lambda a, i, n: lax.dynamic_slice_in_dim(a, i * n, n, 0)
    n = own.shape[0] // 2
    oth = take(other, core, n) + lax.ppermute(take(other, 1 - core, n), "core", SWAP)
    mine = take(own, core, n) + lax.ppermute(take(own, 1 - core, n), "core", SWAP)
    v = mine + lax.ppermute(oth, "mp", SWAP)
    bits = []
    b = 1
    while b < n_chip:
        bits.append(b)
        b *= 2
    for b in bits:
        n = v.shape[0] // 2
        k = (chip // b) % 2
        v = take(v, k, n) + lax.ppermute(take(v, 1 - k, n), "chip", bit_pairs(n_chip, b))
    if n_group > 1:
        v = lax.psum(v, "group")
    for b in bits[::-1]:
        k = (chip // b) % 2
        r = lax.ppermute(v, "chip", bit_pairs(n_chip, b))
        v = jnp.where(k == 0, jnp.concatenate([v, r], 0), jnp.concatenate([r, v], 0))
    r = lax.ppermute(v, "core", SWAP)
    return jnp.where(core == 0, jnp.concatenate([v, r], 0), jnp.concatenate([r, v], 0))


def body(n_group, n_chip, text_states, layout_states, box_counts, text_qkv, text_qv_bias, text_out, text_up, text_up_bias,
         text_down, text_gains, text_shifts, layout_qkv, layout_qv_bias, layout_out, layout_up, layout_up_bias,
         layout_down, layout_gains, layout_shifts, cot_text, cot_layout):
    mp = lax.axis_index("mp")
    other = lambda a: lax.ppermute(a, "mp", SWAP)
    tq = jnp.transpose(text_qkv, (1, 0, 2))
    lq = jnp.pad(jnp.transpose(layout_qkv, (1, 0, 2)), ((0, 0), (0, 0), (0, 32)))
    lo = jnp.pad(layout_out, ((0, 32), (0, 0)))
    small = jnp.concatenate([text_qv_bias.reshape(-1), layout_qv_bias.reshape(-1), text_up_bias, layout_up_bias])
    small_o = other(small)

    def split_small(s):
        z = jnp.zeros((1, 384), f32)
        tb = jnp.concatenate([s[None, :384], z, s[None, 384:768]], 0)
        lb = jnp.concatenate([s[None, 768:864], z[:, :96], s[None, 864:960]], 0)
        return tb, jnp.pad(lb, ((0, 0), (0, 32))), s[None, 960:2496], s[None, 2496:2880]

    bq, blq, bu, blu = split_small(small)
    obq, oblq, obu, oblu = split_small(small_o)
    wq = fetch(tq.reshape(2304, 384)).reshape(3, 768, 384)
    olq = other(lq)
    wo = fetch(text_out)
    olo = other(lo)
    wu = fetch(text_up)
    olu = other(layout_up)
    wd = fetch(text_down)
    old = other(layout_down)
    counts = lax.dynamic_slice_in_dim(box_counts, mp * 2, 2, 0)
    qkv1, qkvl1, lse1, ct1, cl1 = attn_fwd2(counts, text_states, layout_states, tq, bq, lq, blq)
    qkv2, qkvl2, lse2, ct2, cl2 = attn_fwd2(counts, text_states, layout_states, wq, obq, olq, oblq)
    out_t, dr1, da, h1, act, dpre, df, sums, bsum = middle(
        text_states, ct1, ct2, text_out, wo, text_up, wu, text_down, wd, bu, obu, text_gains, text_shifts, cot_text,
        CH=768, R=256, name="text_middle")
    out_l, ldr1, lda, lh1, lact, ldpre, ldf, lsums, lbsum = middle(
        layout_states, cl1, cl2, lo, olo, layout_up, olu, layout_down, old, blu, oblu, layout_gains, layout_shifts,
        cot_layout, CH=384, R=512, name="layout_middle")
    tn = lambda a, b: lax.dot_general(a, b, TN, preferred_element_type=f32).astype(bf16)
    red = lambda a, b: reduce_all(a, b, n_group, n_chip)
    g_up = red(tn(h1, dpre[0]), tn(h1, dpre[1]))
    g_dn = red(tn(act[0], df), tn(act[1], df))
    gl_up = red(tn(lh1, ldpre[0]), tn(lh1, ldpre[1]))
    gl_dn = red(tn(lact[0], ldf), tn(lact[1], ldf))
    dq2, dql2 = attn_bwd(da, lda, wo, olo, qkv2, qkvl2, lse2)
    dq1, dql1 = attn_bwd(da, lda, text_out, lo, qkv1, qkvl1, lse1)

    def wg(dq, dql, ct, cl):
        gq = jnp.einsum("td,ctf->cdf", text_states, dq, preferred_element_type=f32).astype(bf16)
        glq = jnp.einsum("td,ctf->cdf", layout_states, dql, preferred_element_type=f32).astype(bf16)
        bt = jnp.sum(dq[0::2].astype(f32), 1).reshape(-1)
        bl = jnp.sum(dql[0::2].astype(f32), 1)[:, :96].reshape(-1)
        return gq.reshape(2304, 384), tn(ct, da), glq.reshape(576, 128), tn(cl, lda), bt, bl

    gq2, go2, glq2, glo2, bt2, bl2 = wg(dq2, dql2, ct2, cl2)
    gq1, go1, glq1, glo1, bt1, bl1 = wg(dq1, dql1, ct1, cl1)
    g_q = red(gq1, gq2)
    g_o = red(go1, go2)
    gl_q = red(glq1, glq2)
    gl_o = red(glo1, glo2)
    nt = lambda a, b: lax.dot_general(a, b, NT, preferred_element_type=f32)
    gx = dr1 + sum(nt(dq1[c], tq[c]) + nt(dq2[c], wq[c]) for c in range(3))
    gxl = ldr1 + sum(nt(dql1[c], lq[c]) + nt(dql2[c], olq[c]) for c in range(3))
    vec = lambda bt, bl, b, lb: jnp.concatenate([bt, bl, b.reshape(-1), lb.reshape(-1)])
    own_v = vec(bt1, bl1, bsum[0], lbsum[0])
    oth_v = vec(bt2, bl2, bsum[1], lbsum[1])
    norm_v = jnp.concatenate([sums[:6].reshape(-1), lsums[:6].reshape(-1)])
    z = jnp.zeros_like(own_v)
    first = jnp.where(mp == 0, own_v, oth_v)
    second = jnp.where(mp == 0, oth_v, own_v)
    tot = lax.psum(jnp.concatenate([norm_v, first, second]), AX)
    k = norm_v.shape[0]
    s6 = tot[:4608].reshape(6, 768)
    l6 = tot[4608:k].reshape(6, 192)
    bt, blq_, b_up, bl_up = (lambda s: (s[:768].reshape(2, 384), s[768:960].reshape(2, 96), s[960:2496], s[2496:]))(
        lax.dynamic_slice_in_dim(tot[k:].reshape(2, -1), mp, 1, 0)[0])
    back = lambda g, w: jnp.transpose(g.astype(f32).reshape(3, -1, g.shape[1])[:, :, :w], (1, 0, 2))
    return (out_t, out_l, gx, gxl, back(g_q, 384), bt, g_o.astype(f32), g_up.astype(f32), b_up, g_dn.astype(f32),
            s6[0:2], s6[2:6], back(gl_q, 96), blq_, gl_o[:96].astype(f32), gl_up.astype(f32), bl_up,
            gl_dn.astype(f32), l6[0:2], l6[2:6])


def solution(mesh):
    dp = mesh.shape["dp"]
    n_chip = min(dp // 2, 8)
    n_group = dp // (2 * n_chip)
    fine = Mesh(mesh.devices.reshape(n_group, n_chip, 2, 2), AX)
    rows = P(AX, None)
    half2 = P(None, "mp")
    half1 = P("mp", None)
    qkv = P(None, None, "mp")
    rep = P()
    return jax.shard_map(
        functools.partial(body, n_group, n_chip),
        mesh=fine,
        in_specs=(rows, rows, P(("group", "chip", "core")), qkv, half2, half1, half2, P("mp"), half1, rep, rep,
                  qkv, half2, half1, half2, P("mp"), half1, rep, rep, rows, rows),
        out_specs=(rows, rows, rows, rows, qkv, half2, half1, half2, P("mp"), half1, rep, rep,
                   qkv, half2, half1, half2, P("mp"), half1, rep, rep),
        check_vma=False,
    )
```

```python
import functools

import jax
import jax.numpy as jnp
from jax import lax
from jax.experimental import pallas as pl
from jax.experimental.pallas import tpu as pltpu
from jax.sharding import Mesh, PartitionSpec as P

f32 = jnp.float32
bf16 = jnp.bfloat16
SEQ = 512
NT = (((1,), (1,)), ((), ()))
TN = (((0,), (0,)), ((), ()))

def head_masks(h):
    lane=lax.broadcasted_iota(jnp.int32,(1,256),1)
    t=(lane>=64*(h%2))&(lane<64*(h%2)+64)
    l=(lane>=128+16*h)&(lane<128+16*h+16)
    return t|l, t|l|(lane==224)

def k1t_body(cnt, xt, xl, wt, bt, wl, bl, qkvt, qkvl, lse_o, ctxt, ctxl, cT, clT):
    n=cnt[pl.program_id(0)]
    lane=lax.broadcasted_iota(jnp.int32,(SEQ,128),1)
    row=lax.broadcasted_iota(jnp.int32,(SEQ,128),0)
    for c in range(3):
        r=jnp.dot(xt[...],wt[c],preferred_element_type=f32)+bt[c:c+1]
        s=jnp.dot(xl[...],wl[c],preferred_element_type=f32)+bl[c:c+1]
        if c==0:
            r=r*0.125; s=jnp.where(lane==96,1.0,s*0.25)
        if c==1:
            s=jnp.where((lane==96)&(row>=n),-1e30,s)
        qkvt[c]=r.astype(bf16); qkvl[c]=s.astype(bf16)
    vlT=qkvl[2].T
    for p in range(3):
        ps=pl.ds(128*p,128)
        qc=jnp.concatenate([qkvt[0,:,ps],qkvl[0]],axis=1)
        kc=jnp.concatenate([qkvt[1,:,ps],qkvl[1]],axis=1)
        vtT=qkvt[2,:,ps].T
        for hh in range(2):
            h=2*p+hh
            mv,mk=head_masks(h)
            km=jnp.where(mk,kc,jnp.zeros_like(kc))
            S=lax.dot_general(km,qc,NT,preferred_element_type=f32)
            m=jnp.max(S,axis=0,keepdims=True)
            e=jnp.exp(S-m)
            l=jnp.sum(e,axis=0,keepdims=True)
            vT=jnp.concatenate([vtT[64*hh:64*hh+64],vlT[16*h:16*h+16]],axis=0)
            o=jnp.dot(vT,e.astype(bf16),preferred_element_type=f32)*(1.0/l)
            cT[64*hh:64*hh+64,:]=o[:64]
            clT[16*h:16*h+16,:]=o[64:]
            lse_o[0,h:h+1,:]=m+jnp.log(l)
        ctxt[:,ps]=cT[...].T.astype(bf16)
    clT[96:,:]=jnp.zeros((32,SEQ),f32)
    ctxl[...]=clT[...].T.astype(bf16)
    lse_o[0,6:8,:]=jnp.zeros((2,SEQ),f32)

def attn_fwd2(cnt, xt, xl, wt, bt, wl, bl):
    T=xt.shape[0]; n=T//SEQ
    full=lambda s: pl.BlockSpec(s,lambda i,*_:(0,)*len(s),pipeline_mode=pl.Buffered(1))
    return pl.pallas_call(k1t_body,
        grid_spec=pltpu.PrefetchScalarGridSpec(num_scalar_prefetch=1,grid=(n,),
          in_specs=[pl.BlockSpec((SEQ,768),lambda i,*_:(i,0)),pl.BlockSpec((SEQ,192),lambda i,*_:(i,0)),
            full((3,768,384)),full((3,384)),full((3,192,128)),full((3,128))],
          out_specs=[pl.BlockSpec((3,SEQ,384),lambda i,*_:(0,i,0)),pl.BlockSpec((3,SEQ,128),lambda i,*_:(0,i,0)),
            pl.BlockSpec((1,8,SEQ),lambda i,*_:(i,0,0)),pl.BlockSpec((SEQ,384),lambda i,*_:(i,0)),pl.BlockSpec((SEQ,128),lambda i,*_:(i,0))],
          scratch_shapes=[pltpu.VMEM((128,SEQ),f32),pltpu.VMEM((128,SEQ),f32)]),
        out_shape=[jax.ShapeDtypeStruct((3,T,384),bf16),jax.ShapeDtypeStruct((3,T,128),bf16),jax.ShapeDtypeStruct((n,8,SEQ),f32),
            jax.ShapeDtypeStruct((T,384),bf16),jax.ShapeDtypeStruct((T,128),bf16)],
        compiler_params=pltpu.CompilerParams(vmem_limit_bytes=56<<20),
        name="attend_forward",
    )(cnt,xt,xl,wt,bt,wl,bl)

def k6_body(dat, dal, wot, wol, qkvt, qkvl, lse, dqkvt, dqkvl, dqT, dqlT, dcl, *, unused=0):
    dct=lax.dot_general(dat[...],wot[...],NT,preferred_element_type=f32).astype(bf16)
    dcl_=lax.dot_general(dal[...],wol[...],NT,preferred_element_type=f32).astype(bf16)
    accvl=jnp.zeros((SEQ,128),f32); acckl=jnp.zeros((SEQ,128),f32)
    klT=qkvl[1].T
    for p in range(3):
        ps=pl.ds(128*p,128)
        qc=jnp.concatenate([qkvt[0,:,ps],qkvl[0]],axis=1)
        kc=jnp.concatenate([qkvt[1,:,ps],qkvl[1]],axis=1)
        vc=jnp.concatenate([qkvt[2,:,ps],qkvl[2]],axis=1)
        dc=jnp.concatenate([dct[:,128*p:128*p+128],dcl_],axis=1)
        ktT=qkvt[1,:,ps].T
        accv=jnp.zeros((SEQ,128),f32); acck=jnp.zeros((SEQ,128),f32)
        for hh in range(2):
            h=2*p+hh
            mv,mk=head_masks(h)
            z=jnp.zeros_like(kc)
            km=jnp.where(mk,kc,z); vm=jnp.where(mv,vc,z); dm=jnp.where(mv,dc,z); qm=jnp.where(mv,qc,z)
            ST=lax.dot_general(km,qc,NT,preferred_element_type=f32)
            E=jnp.exp(ST-lse[0,h:h+1,:])
            dPT=lax.dot_general(vm,dc,NT,preferred_element_type=f32)
            X=E*dPT
            delta=jnp.sum(X,axis=0,keepdims=True)
            dS=(X-E*delta).astype(bf16)
            ov=jnp.dot(E.astype(bf16),dm,preferred_element_type=f32)
            ok=jnp.dot(dS,qm,preferred_element_type=f32)
            accv=accv+ov[:,:128]; accvl=accvl+ov[:,128:]
            acck=acck+ok[:,:128]; acckl=acckl+ok[:,128:]
            kT=jnp.concatenate([ktT[64*hh:64*hh+64],klT[16*h:16*h+16]],axis=0)
            oq=jnp.dot(kT,dS,preferred_element_type=f32)
            dqT[64*hh:64*hh+64,:]=oq[:64]*0.125
            dqlT[16*h:16*h+16,:]=oq[64:]*0.25
        dqkvt[0,:,ps]=dqT[...].T.astype(bf16)
        dqkvt[1,:,ps]=acck.astype(bf16)
        dqkvt[2,:,ps]=accv.astype(bf16)
    dqlT[96:,:]=jnp.zeros((32,SEQ),f32)
    dqkvl[0]=dqlT[...].T.astype(bf16)
    dqkvl[1]=acckl.astype(bf16)
    dqkvl[2]=accvl.astype(bf16)

def attn_bwd(dat,dal,wot,wol,qkvt,qkvl,lse):
    T=dat.shape[0]; n=T//SEQ
    full=lambda s: pl.BlockSpec(s,lambda i:(0,)*len(s),pipeline_mode=pl.Buffered(1))
    return pl.pallas_call(k6_body,grid=(n,),
        in_specs=[pl.BlockSpec((SEQ,768),lambda i:(i,0)),pl.BlockSpec((SEQ,192),lambda i:(i,0)),full((384,768)),full((128,192)),
          pl.BlockSpec((3,SEQ,384),lambda i:(0,i,0)),pl.BlockSpec((3,SEQ,128),lambda i:(0,i,0)),pl.BlockSpec((1,8,SEQ),lambda i:(i,0,0))],
        out_specs=[pl.BlockSpec((3,SEQ,384),lambda i:(0,i,0)),pl.BlockSpec((3,SEQ,128),lambda i:(0,i,0))],
        out_shape=[jax.ShapeDtypeStruct((3,T,384),bf16),jax.ShapeDtypeStruct((3,T,128),bf16)],
        scratch_shapes=[pltpu.VMEM((128,SEQ),f32),pltpu.VMEM((128,SEQ),f32),pltpu.VMEM((SEQ,128),f32)],
        compiler_params=pltpu.CompilerParams(vmem_limit_bytes=56<<20),
        name="attend_backward",
    )(dat,dal,wot,wol,qkvt,qkvl,lse)

GC=[0.11609199498651965, 0.07018864201817518, 0.2621979336040309, -0.22868178430415115, 0.38476147983842124, -0.10455825070574547]
GP=0.28
def gelu_pair(v):
    t=1.0/(1.0+GP*jnp.abs(v))
    g=jnp.exp(v*v*-0.5)
    q=GC[5]
    for c in GC[4::-1]: q=q*t+c
    q=q*t*g
    phi=jnp.where(v<0,q,1.0-q)
    return v*phi, phi+v*g*0.3989422804014327

def norm_stats(r):
    mean=jnp.mean(r,-1,keepdims=True)
    cen=r-mean
    rstd=lax.rsqrt(jnp.mean(cen*cen,-1,keepdims=True)+1e-5)
    return cen*rstd, rstd

def norm_back(e,n,rstd):
    return (e-jnp.mean(e,-1,keepdims=True)-n*jnp.mean(e*n,-1,keepdims=True))*rstd

def m_body(x, co, cp, wo, wp, upo, upp, dno, dnp, bo, bp, gains, shifts, cot,
           out, dr1o, dao, h1o, act, dpre, dfo, sums, bsum, gp_s, n1_s, *, CH):
    W=upo.shape[1]; nc=W//CH
    colsum=lambda v: jnp.sum(v,axis=0,keepdims=True)
    attn=jnp.dot(co[...],wo[...],preferred_element_type=f32)+jnp.dot(cp[...],wp[...],preferred_element_type=f32)
    n1,rstd1=norm_stats(x[...].astype(f32)+attn+shifts[2:3])
    n1_s[...]=n1
    h1=n1*gains[0:1]+shifts[0:1]
    h1b=h1.astype(bf16); h1o[...]=h1b
    ffn=None
    for hf,(up,dn,b) in enumerate(((upo,dno,bo),(upp,dnp,bp))):
        for c in range(nc):
            cs=slice(c*CH,(c+1)*CH)
            pre=jnp.dot(h1b,up[:,cs],preferred_element_type=f32)+b[:,cs]
            a,g=gelu_pair(pre)
            ab=a.astype(bf16)
            act[hf,:,cs]=ab; gp_s[hf,:,cs]=g.astype(gp_s.dtype)
            t=jnp.dot(ab,dn[cs,:],preferred_element_type=f32)
            ffn=t if ffn is None else ffn+t
    n2,rstd2=norm_stats(n1_s[...]*gains[0:1]+shifts[0:1]+ffn+shifts[3:4])
    out[...]=(n2*gains[1:2]+shifts[1:2]).astype(bf16)
    ct=cot[...].astype(f32)
    dr2=norm_back(ct*gains[1:2],n2,rstd2)
    df=dr2.astype(bf16); dfo[...]=df
    s_g2=colsum(ct*n2); s_s2=colsum(ct); s_r2=colsum(dr2)
    dh1=dr2
    first=pl.program_id(0)==0
    for hf,(up,dn) in enumerate(((upo,dno),(upp,dnp))):
        for c in range(nc):
            cs=slice(c*CH,(c+1)*CH)
            da_=lax.dot_general(df,dn[cs,:],NT,preferred_element_type=f32)
            dp=(da_*gp_s[hf,:,cs].astype(f32)).astype(bf16)
            dpre[hf,:,cs]=dp
            bs=colsum(dp.astype(f32))
            bsum[hf,:,cs]=jnp.where(first,bs,bsum[hf,:,cs]+bs)
            dh1=dh1+lax.dot_general(dp,up[:,cs],NT,preferred_element_type=f32)
    n1=n1_s[...]
    s_g1=colsum(dh1*n1); s_s1=colsum(dh1)
    dr1=norm_back(dh1*gains[0:1],n1,rstd1)
    dr1o[...]=dr1; dao[...]=dr1.astype(bf16)
    tot=jnp.concatenate([s_g1,s_g2,s_s1,s_s2,colsum(dr1),s_r2,jnp.zeros((2,s_g1.shape[1]),f32)],axis=0)
    sums[...]=jnp.where(first,tot,sums[...]+tot)

def middle(x,co,cp,wo,wp,upo,upp,dno,dnp,bo,bp,gains,shifts,cot,*,CH,R=512,GD=f32,name):
    T,D=x.shape; W=upo.shape[1]
    full=lambda a: pl.BlockSpec(a.shape,lambda i:(0,)*a.ndim,pipeline_mode=pl.Buffered(1))
    rows=lambda w: pl.BlockSpec((R,w),lambda i:(i,0))
    rows3=lambda w: pl.BlockSpec((2,R,w),lambda i:(0,i,0))
    const=lambda s: pl.BlockSpec(s,lambda i:(0,)*len(s))
    sd=jax.ShapeDtypeStruct
    return pl.pallas_call(functools.partial(m_body,CH=CH),grid=(T//R,),
        in_specs=[rows(D),rows(co.shape[1]),rows(co.shape[1])]+[full(a) for a in (wo,wp,upo,upp,dno,dnp,bo,bp,gains,shifts)]+[rows(D)],
        out_specs=[rows(D),rows(D),rows(D),rows(D),rows3(W),rows3(W),rows(D),const((8,D)),const((2,1,W))],
        out_shape=[sd((T,D),bf16),sd((T,D),f32),sd((T,D),bf16),sd((T,D),bf16),sd((2,T,W),bf16),sd((2,T,W),bf16),sd((T,D),bf16),sd((8,D),f32),sd((2,1,W),f32)],
        scratch_shapes=[pltpu.VMEM((2,R,W),GD),pltpu.VMEM((R,D),f32)],
        compiler_params=pltpu.CompilerParams(vmem_limit_bytes=62<<20),name=name,
    )(x,co,cp,wo,wp,upo,upp,dno,dnp,bo,bp,gains,shifts,cot)


AXES = ("group", "z", "x", "core", "mp")
MESH = pl.DeviceIdType.MESH
CHUNK = 256
WIDE = 768


def reduce_kernel(n, part_o, part_p, res, P, RC, RY, RX, RZ, sends, rA, rB, rC, rD, rE, rF, rH, loc):
    k = pl.program_id(0)
    z, x, core, mp = (lax.axis_index(a) for a in ("z", "x", "core", "mp"))

    @pl.when(k == 0)
    def _():
        bar = pltpu.get_barrier_semaphore()
        for who in ({"core": 1 - core}, {"mp": 1 - mp}, {"x": 1 - x}):
            pl.semaphore_signal(bar, inc=1, device_id=who, device_id_type=MESH)
        for d in range(1, 4):
            pl.semaphore_signal(bar, inc=1, device_id={"z": (z + d) % 4}, device_id_type=MESH)
        pl.semaphore_wait(bar, 6)

    def remote(src, dst, s, r, who):
        return pltpu.make_async_remote_copy(src_ref=src, dst_ref=dst, send_sem=s, recv_sem=r, device_id=who,
                                            device_id_type=MESH)

    def cA(j):
        return remote(P.at[j % 2, 1 - core], RC.at[j], sends.at[0, j % 8], rA.at[j], {"core": 1 - core})

    def cB(j):
        return remote(RC.at[j, 0], RY.at[j], sends.at[1, j % 8], rB.at[j], {"mp": 1 - mp})

    def cC(j):
        return remote(RY.at[j, 1 - x], RX.at[j], sends.at[2, j % 8], rC.at[j], {"x": 1 - x})

    def cD(j, d):
        t = (z + d) % 4
        return remote(RX.at[j, t], RZ.at[j, 3 - d], sends.at[2 + d, j % 8], rD.at[j], {"z": t})

    def cE(j, d):
        return remote(RX.at[j, z], res.at[j, core, x, z], sends.at[5 + d, j % 8], rE.at[j], {"z": (z + d) % 4})

    def cF(j):
        return remote(res.at[j, core, x], res.at[j, core, x], sends.at[9, j % 8], rF.at[j], {"x": 1 - x})

    def cH(j):
        return remote(res.at[j, core], res.at[j, core], sends.at[10, j % 8], rH.at[j], {"core": 1 - core})

    def stage(lag):
        j = k - lag
        return j, (j >= 0) & (j < n)

    j, live = stage(0)

    @pl.when(live)
    def _():
        for h in range(2):
            P[j % 2, h, 0] = part_p[0, h]
            P[j % 2, h, 1] = part_o[0, h]
        cA(j).start()

    j1, live1 = stage(1)

    @pl.when(live1)
    def _():
        j = j1
        cA(j).wait_recv()
        for i in range(2):
            RC[j, i] = (RC[j, i].astype(f32) + P[j % 2, core, i].astype(f32)).astype(bf16)
        cB(j).start()
        cA(j).wait_send()

    j2, live2 = stage(2)

    @pl.when(live2)
    def _():
        j = j2
        cB(j).wait_recv()
        RY[j] = (RY[j].astype(f32) + RC[j, 1].astype(f32)).astype(bf16)
        cC(j).start()

    j3, live3 = stage(3)

    @pl.when(live3)
    def _():
        j = j3
        cC(j).wait_recv()
        RX[j] = (RX[j].astype(f32) + RY[j, x].astype(f32)).astype(bf16)
        for d in range(1, 4):
            cD(j, d).start()

    j4, live4 = stage(4)

    @pl.when(live4)
    def _():
        j = j4
        remote(RZ.at[j], RZ.at[j], sends.at[3, j % 8], rD.at[j], {"z": (z + 1) % 4}).wait_recv()
        tot = RX[j, z].astype(f32)
        for d in range(3):
            tot = tot + RZ[j, d].astype(f32)
        RX[j, z] = tot.astype(bf16)
        for d in range(1, 4):
            cE(j, d).start()
        pltpu.make_async_copy(RX.at[j, z], res.at[j, core, x, z], loc.at[j % 8]).start()

    j5, live5 = stage(5)

    @pl.when(live5)
    def _():
        j = j5
        remote(res.at[j, core, x, pl.ds(0, 3)], res.at[j, core, x, pl.ds(0, 3)], sends.at[6, j % 8], rE.at[j],
               {"z": (z + 1) % 4}).wait_recv()
        pltpu.make_async_copy(RX.at[j, z], res.at[j, core, x, z], loc.at[j % 8]).wait()
        cF(j).start()

    j6, live6 = stage(6)

    @pl.when(live6)
    def _():
        j = j6
        cF(j).wait_recv()
        cH(j).start()

    j7, live7 = stage(7)

    @pl.when(live7)
    def _():
        j = j7
        cH(j).wait_recv()
        cB(j).wait_send()
        cC(j).wait_send()
        for d in range(1, 4):
            cD(j, d).wait_send()
            cE(j, d).wait_send()
        cF(j).wait_send()
        cH(j).wait_send()


def reduce_packed(own, oth):
    n = own.shape[0] // CHUNK
    shp = (n, 2, 2, 4, 16, WIDE)
    blk = pl.BlockSpec((1, 2, 2, 4, 16, WIDE), lambda k: (jnp.minimum(k, n - 1), 0, 0, 0, 0, 0))
    D = pltpu.SemaphoreType.DMA
    out = pl.pallas_call(
        functools.partial(reduce_kernel, n),
        grid=(n + 7,),
        in_specs=[blk, blk],
        out_specs=pl.BlockSpec(memory_space=pl.ANY),
        out_shape=jax.ShapeDtypeStruct((n, 2, 2, 4, 16, WIDE), bf16),
        scratch_shapes=[
            pltpu.VMEM((2, 2, 2, 2, 4, 16, WIDE), bf16), pltpu.VMEM((n, 2, 2, 4, 16, WIDE), bf16),
            pltpu.VMEM((n, 2, 4, 16, WIDE), bf16), pltpu.VMEM((n, 4, 16, WIDE), bf16),
            pltpu.VMEM((n, 3, 16, WIDE), bf16), D((11, 8)), D((n,)), D((n,)), D((n,)), D((n,)), D((n,)), D((n,)),
            D((n,)), D((8,))],
        compiler_params=pltpu.CompilerParams(collective_id=0, has_side_effects=True, vmem_limit_bytes=60 << 20),
        name="reduce_gradients",
    )(own.reshape(shp), oth.reshape(shp))
    return out.reshape(n * CHUNK, WIDE)


SWAP = [(0, 1), (1, 0)]


def fetch(w):
    core = lax.axis_index("core")
    n = w.shape[0] // 2
    mine = lax.dynamic_slice_in_dim(w, core * n, n, 0)
    got = lax.ppermute(mine, "mp", SWAP)
    sib = lax.ppermute(got, "core", SWAP)
    return jnp.where(core == 0, jnp.concatenate([got, sib], 0), jnp.concatenate([sib, got], 0))


def body(n_group, text_states, layout_states, box_counts, text_qkv, text_qv_bias, text_out, text_up, text_up_bias,
         text_down, text_gains, text_shifts, layout_qkv, layout_qv_bias, layout_out, layout_up, layout_up_bias,
         layout_down, layout_gains, layout_shifts, cot_text, cot_layout):
    mp = lax.axis_index("mp")
    other = lambda a: lax.ppermute(a, "mp", SWAP)
    tq = jnp.transpose(text_qkv, (1, 0, 2))
    lq = jnp.pad(jnp.transpose(layout_qkv, (1, 0, 2)), ((0, 0), (0, 0), (0, 32)))
    lo = jnp.pad(layout_out, ((0, 32), (0, 0)))
    small = jnp.concatenate([text_qv_bias.reshape(-1), layout_qv_bias.reshape(-1), text_up_bias, layout_up_bias])
    small_o = other(small)

    def split_small(s):
        z = jnp.zeros((1, 384), f32)
        tb = jnp.concatenate([s[None, :384], z, s[None, 384:768]], 0)
        lb = jnp.concatenate([s[None, 768:864], z[:, :96], s[None, 864:960]], 0)
        return tb, jnp.pad(lb, ((0, 0), (0, 32))), s[None, 960:2496], s[None, 2496:2880]

    bq, blq, bu, blu = split_small(small)
    obq, oblq, obu, oblu = split_small(small_o)
    wq = fetch(tq.reshape(2304, 384)).reshape(3, 768, 384)
    olq = other(lq)
    wo = fetch(text_out)
    olo = other(lo)
    wu = fetch(text_up)
    olu = other(layout_up)
    wd = fetch(text_down)
    old = other(layout_down)
    counts = lax.dynamic_slice_in_dim(box_counts, mp * 2, 2, 0)
    qkv1, qkvl1, lse1, ct1, cl1 = attn_fwd2(counts, text_states, layout_states, tq, bq, lq, blq)
    qkv2, qkvl2, lse2, ct2, cl2 = attn_fwd2(counts, text_states, layout_states, wq, obq, olq, oblq)
    out_t, dr1, da, h1, act, dpre, df, sums, bsum = middle(
        text_states, ct1, ct2, text_out, wo, text_up, wu, text_down, wd, bu, obu, text_gains, text_shifts, cot_text,
        CH=768, R=256, name="text_middle")
    out_l, ldr1, lda, lh1, lact, ldpre, ldf, lsums, lbsum = middle(
        layout_states, cl1, cl2, lo, olo, layout_up, olu, layout_down, old, blu, oblu, layout_gains, layout_shifts,
        cot_layout, CH=384, R=512, name="layout_middle")
    tn = lambda a, b: lax.dot_general(a, b, TN, preferred_element_type=f32).astype(bf16)
    dq2, dql2 = attn_bwd(da, lda, wo, olo, qkv2, qkvl2, lse2)
    dq1, dql1 = attn_bwd(da, lda, text_out, lo, qkv1, qkvl1, lse1)


    def pack(dq, dql, ct, cl, h, bs, lbs):
        gq = jnp.einsum("td,ctf->cdf", text_states, dq, preferred_element_type=f32).astype(bf16)
        glq = jnp.einsum("td,ctf->cdf", layout_states, dql, preferred_element_type=f32).astype(bf16)
        bt = jnp.sum(dq[0::2].astype(f32), 1).reshape(1, 768)
        bl = jnp.sum(dql[0::2].astype(f32), 1)[:, :96].reshape(1, 192)
        up = tn(h1, dpre[h])
        lay = jnp.concatenate([glq[0], glq[1], glq[2], tn(lh1, ldpre[h])], 1)
        lay2 = jnp.concatenate([tn(ldf, lact[h]), tn(lda, cl), jnp.zeros((192, 256), bf16)], 1)
        row = lambda v: jnp.pad(v, ((0, 0), (0, 768 - v.shape[1])))
        small = jnp.concatenate([sums[:6], lsums[:6].reshape(1, -1)[:, :768], row(lsums[:6].reshape(1, -1)[:, 768:]),
                                 bt, row(jnp.concatenate([bl, lbs], 1)), bs.reshape(2, 768)], 0)
        small = jnp.pad(small, ((0, 116), (0, 0))).astype(bf16)
        return jnp.concatenate([up[:, :768], up[:, 768:], tn(act[h], df), jnp.concatenate([gq[0], gq[1]], 1),
                                jnp.concatenate([gq[2][:384], gq[2][384:]], 1), tn(ct, da), lay, lay2, small], 0)

    own = pack(dq1, dql1, ct1, cl1, 0, bsum[0], lbsum[0])
    oth = pack(dq2, dql2, ct2, cl2, 1, bsum[1], lbsum[1])
    tot = reduce_packed(own, oth)
    if n_group > 1:
        tot = lax.psum(tot, "group")
    nt = lambda a, b: lax.dot_general(a, b, NT, preferred_element_type=f32)
    gx = dr1 + sum(nt(dq1[c], tq[c]) + nt(dq2[c], wq[c]) for c in range(3))
    gxl = ldr1 + sum(nt(dql1[c], lq[c]) + nt(dql2[c], olq[c]) for c in range(3))
    F = lambda a, b, c=0, d=768: tot[a:b, c:d].astype(f32)
    g_up = jnp.concatenate([F(0, 768), F(768, 1536)], 1)
    g_dn = F(1536, 3072)
    v = F(3840, 4224)
    g_qkv = jnp.stack([F(3072, 3840, 0, 384), F(3072, 3840, 384, 768), jnp.concatenate([v[:, :384], v[:, 384:]], 0)], 1)
    g_o = F(4224, 4608)
    gl_qkv = jnp.stack([F(4608, 4800, 128 * c, 128 * c + 96) for c in range(3)], 1)
    gl_up = F(4608, 4800, 384, 768)
    gl_dn = F(4800, 4992, 0, 384).T
    gl_o = F(4800, 4992, 384, 480).T
    s6 = F(4992, 4998)
    l6 = jnp.concatenate([F(4998, 4999), F(4999, 5000, 0, 384)], 1).reshape(6, 192)
    return (out_t, out_l, gx, gxl, g_qkv, F(5000, 5001).reshape(2, 384), g_o, g_up, F(5002, 5004).reshape(1536), g_dn,
            s6[0:2], s6[2:6], gl_qkv, F(5001, 5002, 0, 192).reshape(2, 96), gl_o, gl_up,
            F(5001, 5002, 192, 576).reshape(384), gl_dn, l6[0:2], l6[2:6])


def solution(mesh):
    dp = mesh.shape["dp"]
    n_group = dp // 16
    fine = Mesh(mesh.devices.reshape(n_group, 4, 2, 2, 2), AXES)
    rows = P(AXES, None)
    half2 = P(None, "mp")
    half1 = P("mp", None)
    qkv = P(None, None, "mp")
    rep = P()
    return jax.shard_map(
        functools.partial(body, n_group),
        mesh=fine,
        in_specs=(rows, rows, P(AXES[:4]), qkv, half2, half1, half2, P("mp"), half1, rep, rep,
                  qkv, half2, half1, half2, P("mp"), half1, rep, rep, rows, rows),
        out_specs=(rows, rows, rows, rows, qkv, half2, half1, half2, P("mp"), half1, rep, rep,
                   qkv, half2, half1, half2, P("mp"), half1, rep, rep),
        check_vma=False,
    )
```

```python
import functools

import jax
import jax.numpy as jnp
from jax import lax
from jax.experimental import pallas as pl
from jax.experimental.pallas import tpu as pltpu
from jax.sharding import Mesh, PartitionSpec as P

f32 = jnp.float32
bf16 = jnp.bfloat16
SEQ = 512
NT = (((1,), (1,)), ((), ()))
TN = (((0,), (0,)), ((), ()))
AXES = ("group", "z", "x", "core", "mp")
MESH = pl.DeviceIdType.MESH
CHUNK = 256
WIDE = 768
STEPS = 20
LAGS = 7


def dot(a, b):
    return jnp.dot(a, b, preferred_element_type=f32)


def dot_nt(a, b):
    return lax.dot_general(a, b, NT, preferred_element_type=f32)


def dot_tn(a, b):
    return lax.dot_general(a, b, TN, preferred_element_type=f32)


def colsum(v):
    return jnp.sum(v, axis=0, keepdims=True)


def whole(a):
    return pl.BlockSpec(a.shape, lambda *i: (0,) * a.ndim, pipeline_mode=pl.Buffered(1))


def head_masks(h):
    lane = lax.broadcasted_iota(jnp.int32, (1, 256), 1)
    t = (lane >= 64 * (h % 2)) & (lane < 64 * (h % 2) + 64)
    l = (lane >= 128 + 16 * h) & (lane < 128 + 16 * h + 16)
    return t | l, t | l | (lane == 224)


def attend_kernel(cnt, xt, xl, wt, bt, wl, bl, qkvt, qkvl, lse_o, ctxt, ctxl, cT, clT):
    n = cnt[pl.program_id(1)]
    lane = lax.broadcasted_iota(jnp.int32, (SEQ, 128), 1)
    row = lax.broadcasted_iota(jnp.int32, (SEQ, 128), 0)
    for c in range(3):
        r = dot(xt[...], wt[0, c]) + bt[0, c:c + 1]
        s = dot(xl[...], wl[0, c]) + bl[0, c:c + 1]
        if c == 0:
            r = r * 0.125
            s = jnp.where(lane == 96, 1.0, s * 0.25)
        if c == 1:
            s = jnp.where((lane == 96) & (row >= n), -1e30, s)
        qkvt[0, c] = r.astype(bf16)
        qkvl[0, c] = s.astype(bf16)
    vlT = qkvl[0, 2].T
    for p in range(3):
        ps = pl.ds(128 * p, 128)
        qc = jnp.concatenate([qkvt[0, 0, :, ps], qkvl[0, 0]], axis=1)
        kc = jnp.concatenate([qkvt[0, 1, :, ps], qkvl[0, 1]], axis=1)
        vtT = qkvt[0, 2, :, ps].T
        for hh in range(2):
            h = 2 * p + hh
            mv, mk = head_masks(h)
            km = jnp.where(mk, kc, jnp.zeros_like(kc))
            S = dot_nt(km, qc)
            m = jnp.max(S, axis=0, keepdims=True)
            e = jnp.exp(S - m)
            l = colsum(e)
            vT = jnp.concatenate([vtT[64 * hh:64 * hh + 64], vlT[16 * h:16 * h + 16]], axis=0)
            o = dot(vT, e.astype(bf16)) * (1.0 / l)
            cT[64 * hh:64 * hh + 64, :] = o[:64]
            clT[16 * h:16 * h + 16, :] = o[64:]
            lse_o[0, 0, h:h + 1, :] = m + jnp.log(l)
        ctxt[0, :, ps] = cT[...].T.astype(bf16)
    clT[96:, :] = jnp.zeros((32, SEQ), f32)
    ctxl[0] = clT[...].T.astype(bf16)
    lse_o[0, 0, 6:8, :] = jnp.zeros((2, SEQ), f32)


def attend_forward(cnt, xt, xl, wt, bt, wl, bl):
    T = xt.shape[0]
    n = T // SEQ
    half = lambda *s: pl.BlockSpec((1,) + s, lambda h, i, *_: (h,) + (0,) * len(s))
    out3 = lambda w: pl.BlockSpec((1, 3, SEQ, w), lambda h, i, *_: (h, 0, i, 0))
    out2 = lambda w: pl.BlockSpec((1, SEQ, w), lambda h, i, *_: (h, i, 0))
    sd = jax.ShapeDtypeStruct
    return pl.pallas_call(
        attend_kernel,
        grid_spec=pltpu.PrefetchScalarGridSpec(
            num_scalar_prefetch=1, grid=(2, n),
            in_specs=[pl.BlockSpec((SEQ, 768), lambda h, i, *_: (i, 0)),
                      pl.BlockSpec((SEQ, 192), lambda h, i, *_: (i, 0)),
                      half(3, 768, 384), half(3, 384), half(3, 192, 128), half(3, 128)],
            out_specs=[out3(384), out3(128), pl.BlockSpec((1, 1, 8, SEQ), lambda h, i, *_: (h, i, 0, 0)),
                       out2(384), out2(128)],
            scratch_shapes=[pltpu.VMEM((128, SEQ), f32), pltpu.VMEM((128, SEQ), f32)]),
        out_shape=[sd((2, 3, T, 384), bf16), sd((2, 3, T, 128), bf16), sd((2, n, 8, SEQ), f32),
                   sd((2, T, 384), bf16), sd((2, T, 128), bf16)],
        compiler_params=pltpu.CompilerParams(vmem_limit_bytes=56 << 20),
        name="attend_forward",
    )(cnt, xt, xl, wt, bt, wl, bl)


GC = [0.11609199498651965, 0.07018864201817518, 0.2621979336040309, -0.22868178430415115, 0.38476147983842124,
      -0.10455825070574547]
GP = 0.28


def gelu_pair(v):
    t = 1.0 / (1.0 + GP * jnp.abs(v))
    g = jnp.exp(v * v * -0.5)
    q = GC[5]
    for c in GC[4::-1]:
        q = q * t + c
    q = q * t * g
    phi = jnp.where(v < 0, q, 1.0 - q)
    return v * phi, phi + v * g * 0.3989422804014327


def norm_stats(r):
    cen = r - jnp.mean(r, -1, keepdims=True)
    rstd = lax.rsqrt(jnp.mean(cen * cen, -1, keepdims=True) + 1e-5)
    return cen * rstd, rstd


def norm_back(e, n, rstd):
    return (e - jnp.mean(e, -1, keepdims=True) - n * jnp.mean(e * n, -1, keepdims=True)) * rstd


def middle_kernel(x, ctx, wo, wp, upo, upp, dno, dnp, bo, bp, gains, shifts, cot,
                  out, dr1o, dao, h1o, act, dpre, dfo, sums, bsum, gp_s, n1_s, *, CH):
    W = upo.shape[1]
    nc = W // CH
    attn = dot(ctx[0], wo[...]) + dot(ctx[1], wp[...])
    n1, rstd1 = norm_stats(x[...].astype(f32) + attn + shifts[2:3])
    n1_s[...] = n1
    h1b = (n1 * gains[0:1] + shifts[0:1]).astype(bf16)
    h1o[...] = h1b
    ffn = None
    for hf, (up, dn, b) in enumerate(((upo, dno, bo), (upp, dnp, bp))):
        for c in range(nc):
            cs = slice(c * CH, (c + 1) * CH)
            a, g = gelu_pair(dot(h1b, up[:, cs]) + b[:, cs])
            ab = a.astype(bf16)
            act[hf, :, cs] = ab
            gp_s[hf, :, cs] = g
            t = dot(ab, dn[cs, :])
            ffn = t if ffn is None else ffn + t
    n2, rstd2 = norm_stats(n1_s[...] * gains[0:1] + shifts[0:1] + ffn + shifts[3:4])
    out[...] = (n2 * gains[1:2] + shifts[1:2]).astype(bf16)
    ct = cot[...].astype(f32)
    dr2 = norm_back(ct * gains[1:2], n2, rstd2)
    df = dr2.astype(bf16)
    dfo[...] = df
    s_g2 = colsum(ct * n2)
    s_s2 = colsum(ct)
    s_r2 = colsum(dr2)
    dh1 = dr2
    first = pl.program_id(0) == 0
    for hf, (up, dn) in enumerate(((upo, dno), (upp, dnp))):
        for c in range(nc):
            cs = slice(c * CH, (c + 1) * CH)
            dp = (dot_nt(df, dn[cs, :]) * gp_s[hf, :, cs]).astype(bf16)
            dpre[hf, :, cs] = dp
            bs = colsum(dp.astype(f32))
            bsum[hf, :, cs] = jnp.where(first, bs, bsum[hf, :, cs] + bs)
            dh1 = dh1 + dot_nt(dp, up[:, cs])
    n1 = n1_s[...]
    s_g1 = colsum(dh1 * n1)
    s_s1 = colsum(dh1)
    dr1 = norm_back(dh1 * gains[0:1], n1, rstd1)
    dr1o[...] = dr1
    dao[...] = dr1.astype(bf16)
    tot = jnp.concatenate([s_g1, s_g2, s_s1, s_s2, colsum(dr1), s_r2, jnp.zeros((2, s_g1.shape[1]), f32)], axis=0)
    sums[...] = jnp.where(first, tot, sums[...] + tot)


def middle(x, ctx, wo, wp, upo, upp, dno, dnp, bo, bp, gains, shifts, cot, *, CH, R, name):
    T, D = x.shape
    W = upo.shape[1]
    rows = lambda w: pl.BlockSpec((R, w), lambda i: (i, 0))
    rows3 = lambda w: pl.BlockSpec((2, R, w), lambda i: (0, i, 0))
    const = lambda s: pl.BlockSpec(s, lambda i: (0,) * len(s))
    sd = jax.ShapeDtypeStruct
    return pl.pallas_call(
        functools.partial(middle_kernel, CH=CH), grid=(T // R,),
        in_specs=[rows(D), rows3(ctx.shape[2])] + [whole(a) for a in (wo, wp, upo, upp, dno, dnp, bo, bp, gains, shifts)]
        + [rows(D)],
        out_specs=[rows(D), rows(D), rows(D), rows(D), rows3(W), rows3(W), rows(D), const((8, D)), const((2, 1, W))],
        out_shape=[sd((T, D), bf16), sd((T, D), f32), sd((T, D), bf16), sd((T, D), bf16), sd((2, T, W), bf16),
                   sd((2, T, W), bf16), sd((T, D), bf16), sd((8, D), f32), sd((2, 1, W), f32)],
        scratch_shapes=[pltpu.VMEM((2, R, W), f32), pltpu.VMEM((R, D), f32)],
        compiler_params=pltpu.CompilerParams(vmem_limit_bytes=62 << 20), name=name,
    )(x, ctx, wo, wp, upo, upp, dno, dnp, bo, bp, gains, shifts, cot)


def finish_kernel(h1, dpre, act, df, qkvt, qkvl, lse, xblk, dablk, dr1, ldr1, da, lda, wout, woutl, wq, wql, ctx, ctxl,
                  xl, lh1, ldf, ldpre, lact, sums, lsums, bsum, lbsum,
                  res, gx, gxlT,
                  DQ, DQL, dct_s, dcl_s, klT_s, avl, akl, dqT, dqlT, small,
                  P, RC, RY, RX, RZ, sends, rA, rB, rC, rD, rE, rF, rH, loc):
    n = STEPS
    k = pl.program_id(0)
    z, x, core, mp = (lax.axis_index(a) for a in ("z", "x", "core", "mp"))

    @pl.when(k == 0)
    def _():
        bar = pltpu.get_barrier_semaphore()
        for who in ({"core": 1 - core}, {"mp": 1 - mp}, {"x": 1 - x}):
            pl.semaphore_signal(bar, inc=1, device_id=who, device_id_type=MESH)
        for d in range(1, 4):
            pl.semaphore_signal(bar, inc=1, device_id={"z": (z + d) % 4}, device_id_type=MESH)
        pl.semaphore_wait(bar, 6)

    def put(o, t):
        t = t.astype(bf16).reshape(2, 2, 4, 16, WIDE)
        P[k % 2, 0, o] = t[0]
        P[k % 2, 1, o] = t[1]

    @pl.when(k < 6)
    def _():
        hT = h1[...].T
        for h in range(2):
            put(1 - h, dot(hT, dpre[h]))

    @pl.when((k >= 6) & (k < 12))
    def _():
        for h in range(2):
            put(1 - h, dot_tn(act[h], df[...]))

    cat3 = lambda h, c: jnp.concatenate([DQ[h, c, 0], DQ[h, c, 1], DQ[h, c, 2]], axis=1)

    @pl.when((k >= 12) & (k < 15))
    def _():
        xT = xblk[...].T
        for h in range(2):
            put(1 - h, jnp.concatenate([dot(xT, cat3(h, 0)), dot(xT, cat3(h, 1))], axis=1))

    @pl.when((k >= 15) & (k < 18))
    def _():
        xT = xblk[...].T
        dT = dablk[...].T
        for h in range(2):
            put(1 - h, jnp.concatenate([dot(xT, cat3(h, 2)), dot(dT, ctx[h])], axis=1))

    @pl.when(k == 18)
    def _():
        xT = xl[...].T
        hT = lh1[...].T
        for h in range(2):
            t = jnp.concatenate([dot(xT, DQL[h, 0]), dot(xT, DQL[h, 1]), dot(xT, DQL[h, 2]), dot(hT, ldpre[h])], axis=1)
            small[...] = jnp.zeros_like(small)
            small[0:6, :] = sums[0:6, :]
            small[6:12, 0:192] = lsums[0:6, :]
            for i, c in enumerate((0, 2)):
                for p in range(3):
                    at = 384 * i + 128 * p
                    small[12:13, at:at + 128] = colsum(DQ[h, c, p].astype(f32))
                small[13:14, 128 * i:128 * i + 128] = colsum(DQL[h, c].astype(f32))
            small[14:15, :] = bsum[h, :, 0:768]
            small[15:16, :] = bsum[h, :, 768:1536]
            small[16:17, 0:384] = lbsum[h]
            put(1 - h, jnp.concatenate([t, small[...]], axis=0))

    @pl.when(k == 19)
    def _():
        fT = ldf[...].T
        aT = lda[...].T
        for h in range(2):
            t = jnp.concatenate([dot(fT, lact[h]), dot(aT, ctxl[h]), jnp.zeros((192, 256), f32)], axis=1)
            put(1 - h, jnp.concatenate([t, jnp.zeros((64, WIDE), f32)], axis=0))

    def remote(src, dst, s, r, who):
        return pltpu.make_async_remote_copy(src_ref=src, dst_ref=dst, send_sem=s, recv_sem=r, device_id=who,
                                            device_id_type=MESH)

    def cA(j):
        return remote(P.at[j % 2, 1 - core], RC.at[j], sends.at[0, j % 8], rA.at[j], {"core": 1 - core})

    def cB(j):
        return remote(RC.at[j, 0], RY.at[j], sends.at[1, j % 8], rB.at[j], {"mp": 1 - mp})

    def cC(j):
        return remote(RY.at[j, 1 - x], RX.at[j], sends.at[2, j % 8], rC.at[j], {"x": 1 - x})

    def cD(j, d):
        t = (z + d) % 4
        return remote(RX.at[j, t], RZ.at[j, 3 - d], sends.at[2 + d, j % 8], rD.at[j], {"z": t})

    def cE(j, d):
        return remote(RX.at[j, z], res.at[j, core, x, z], sends.at[5 + d, j % 8], rE.at[j], {"z": (z + d) % 4})

    def cF(j):
        return remote(res.at[j, core, x], res.at[j, core, x], sends.at[9, j % 8], rF.at[j], {"x": 1 - x})

    def cH(j):
        return remote(res.at[j, core], res.at[j, core], sends.at[10, j % 8], rH.at[j], {"core": 1 - core})

    def stage(lag):
        j = k - lag
        return j, (j >= 0) & (j < n)

    j0, live0 = stage(0)

    @pl.when(live0)
    def _():
        cA(j0).start()

    j1, live1 = stage(1)

    @pl.when(live1)
    def _():
        j = j1
        cA(j).wait_recv()
        for i in range(2):
            RC[j, i] = (RC[j, i].astype(f32) + P[j % 2, core, i].astype(f32)).astype(bf16)
        cB(j).start()
        cA(j).wait_send()

    @pl.when(k < 12)
    def _():
        hf = 1 - k // 6
        page = (k % 6) // 3
        pair = k % 3
        rs = pl.ds(pl.multiple_of(page * SEQ, SEQ), SEQ)

        @pl.when(pair == 0)
        def _():
            dct = dot_nt(da[rs, :], wout[hf]).astype(bf16)
            for p in range(3):
                dct_s[p] = dct[:, 128 * p:128 * p + 128]
            dcl_s[...] = dot_nt(lda[rs, :], woutl[hf]).astype(bf16)
            klT_s[...] = qkvl[0, 1].T
            avl[...] = jnp.zeros_like(avl)
            akl[...] = jnp.zeros_like(akl)
            dqlT[...] = jnp.zeros_like(dqlT)

        qc = jnp.concatenate([qkvt[0, 0], qkvl[0, 0]], axis=1)
        kc = jnp.concatenate([qkvt[0, 1], qkvl[0, 1]], axis=1)
        vc = jnp.concatenate([qkvt[0, 2], qkvl[0, 2]], axis=1)
        dc = jnp.concatenate([dct_s[pair], dcl_s[...]], axis=1)
        ktT = qkvt[0, 1].T
        zero = jnp.zeros_like(kc)
        av = ak = None
        for hh in range(2):
            h = 2 * pair + hh
            lane = lax.broadcasted_iota(jnp.int32, (1, 256), 1)
            mv = ((lane >= 64 * hh) & (lane < 64 * hh + 64)) | ((lane >= 128 + 16 * h) & (lane < 144 + 16 * h))
            mk = mv | (lane == 224)
            E = jnp.exp(dot_nt(jnp.where(mk, kc, zero), qc) - lse[0, 0, pl.ds(h, 1), :])
            dP = dot_nt(jnp.where(mv, vc, zero), dc)
            X = E * dP
            dS = (X - E * colsum(X)).astype(bf16)
            ov = dot(E.astype(bf16), jnp.where(mv, dc, zero))
            ok = dot(dS, jnp.where(mv, qc, zero))
            av = ov[:, :128] if av is None else av + ov[:, :128]
            ak = ok[:, :128] if ak is None else ak + ok[:, :128]
            avl[...] += ov[:, 128:]
            akl[...] += ok[:, 128:]
            ls = pl.ds(pl.multiple_of(16 * h, 16), 16)
            kT = jnp.concatenate([ktT[64 * hh:64 * hh + 64], klT_s[ls, :]], axis=0)
            oq = dot(kT, dS)
            dqT[64 * hh:64 * hh + 64, :] = oq[:64] * 0.125
            dqlT[ls, :] = oq[64:] * 0.25
        DQ[hf, 0, pair, rs, :] = dqT[...].T.astype(bf16)
        DQ[hf, 1, pair, rs, :] = ak.astype(bf16)
        DQ[hf, 2, pair, rs, :] = av.astype(bf16)

        @pl.when(pair == 2)
        def _():
            DQL[hf, 0, rs, :] = dqlT[...].T.astype(bf16)
            DQL[hf, 1, rs, :] = akl[...].astype(bf16)
            DQL[hf, 2, rs, :] = avl[...].astype(bf16)

    @pl.when((k >= STEPS) & (k < STEPS + 4))
    def _():
        rs = pl.ds(pl.multiple_of((k - STEPS) * 256, 256), 256)
        g = dr1[...]
        gl = ldr1[...]
        for h in range(2):
            for c in range(3):
                g = g + dot_nt(jnp.concatenate([DQ[h, c, p, rs, :] for p in range(3)], axis=1), wq[h, c])
                gl = gl + dot_nt(DQL[h, c, rs, :], wql[h, c])
        gx[...] = g
        gxlT[...] = gl.T

    j2, live2 = stage(2)

    @pl.when(live2)
    def _():
        j = j2
        cB(j).wait_recv()
        RY[j] = (RY[j].astype(f32) + RC[j, 1].astype(f32)).astype(bf16)
        cC(j).start()

    j3, live3 = stage(3)

    @pl.when(live3)
    def _():
        j = j3
        cC(j).wait_recv()
        RX[j] = (RX[j].astype(f32) + RY[j, x].astype(f32)).astype(bf16)
        for d in range(1, 4):
            cD(j, d).start()

    j4, live4 = stage(4)

    @pl.when(live4)
    def _():
        j = j4
        remote(RZ.at[j], RZ.at[j], sends.at[3, j % 8], rD.at[j], {"z": (z + 1) % 4}).wait_recv()
        tot = RX[j, z].astype(f32)
        for d in range(3):
            tot = tot + RZ[j, d].astype(f32)
        RX[j, z] = tot.astype(bf16)
        for d in range(1, 4):
            cE(j, d).start()
        pltpu.make_async_copy(RX.at[j, z], res.at[j, core, x, z], loc.at[j % 8]).start()

    j5, live5 = stage(5)

    @pl.when(live5)
    def _():
        j = j5
        remote(res.at[j, core, x, pl.ds(0, 3)], res.at[j, core, x, pl.ds(0, 3)], sends.at[6, j % 8], rE.at[j],
               {"z": (z + 1) % 4}).wait_recv()
        pltpu.make_async_copy(RX.at[j, z], res.at[j, core, x, z], loc.at[j % 8]).wait()
        cF(j).start()

    j6, live6 = stage(6)

    @pl.when(live6)
    def _():
        cF(j6).wait_recv()
        cH(j6).start()

    j7, live7 = stage(7)

    @pl.when(live7)
    def _():
        j = j7
        cH(j).wait_recv()
        cB(j).wait_send()
        cC(j).wait_send()
        for d in range(1, 4):
            cD(j, d).wait_send()
            cE(j, d).wait_send()
        cF(j).wait_send()
        cH(j).wait_send()


def finish(h1, dpre, act, df, qkvt, qkvl, lse, x, da, dr1, ldr1, lda, wout, woutl, wq, wql, ctx, ctxl,
           xl, lh1, ldf, ldpre, lact, sums, lsums, bsum, lbsum):
    n = STEPS
    T = x.shape[0]
    lim = lambda v, a, b: jnp.minimum(jnp.maximum(v, a), b)
    att = lambda k: lim(k, 0, 11)
    head = lambda k: (1 - att(k) // 6, (att(k) % 6) // 3, att(k) % 3)
    D = pltpu.SemaphoreType.DMA
    V = pltpu.VMEM
    sd = jax.ShapeDtypeStruct
    one = pl.Buffered(1)
    in_specs = [
        pl.BlockSpec((T, 256), lambda k: (0, lim(k, 0, 5) % 3)),
        pl.BlockSpec((2, T, WIDE), lambda k: (0, 0, lim(k, 0, 5) // 3), pipeline_mode=one),
        pl.BlockSpec((2, T, 256), lambda k: (0, 0, lim(k - 6, 0, 5))),
        whole(df),
        pl.BlockSpec((1, 3, SEQ, 128), lambda k: (head(k)[0], 0, head(k)[1], head(k)[2])),
        pl.BlockSpec((1, 3, SEQ, 128), lambda k: (head(k)[0], 0, head(k)[1], 0)),
        pl.BlockSpec((1, 1, 8, SEQ), lambda k: (head(k)[0], head(k)[1], 0, 0)),
        pl.BlockSpec((T, 256), lambda k: (0, lim(k - 12, 0, 5) % 3)),
        pl.BlockSpec((T, 256), lambda k: (0, lim(k - 15, 0, 2))),
        pl.BlockSpec((256, WIDE), lambda k: (lim(k - STEPS, 0, 3), 0)),
        pl.BlockSpec((256, 192), lambda k: (lim(k - STEPS, 0, 3), 0)),
    ] + [whole(a) for a in (da, lda, wout, woutl, wq, wql, ctx, ctxl, xl, lh1, ldf, ldpre, lact, sums, lsums, bsum, lbsum)]
    return pl.pallas_call(
        finish_kernel,
        grid=(n + LAGS,),
        in_specs=in_specs,
        out_specs=[pl.BlockSpec(memory_space=pl.ANY),
                   pl.BlockSpec((256, WIDE), lambda k: (lim(k - STEPS, 0, 3), 0)),
                   pl.BlockSpec((192, 256), lambda k: (0, lim(k - STEPS, 0, 3)))],
        out_shape=[sd((n, 2, 2, 4, 16, WIDE), bf16), sd((T, WIDE), f32), sd((192, T), f32)],
        scratch_shapes=[
            V((2, 3, 3, T, 128), bf16), V((2, 3, T, 128), bf16), V((3, SEQ, 128), bf16), V((SEQ, 128), bf16),
            V((128, SEQ), bf16), V((SEQ, 128), f32), V((SEQ, 128), f32), V((128, SEQ), f32), V((128, SEQ), f32),
            V((64, WIDE), f32),
            V((2, 2, 2, 2, 4, 16, WIDE), bf16), V((n, 2, 2, 4, 16, WIDE), bf16), V((n, 2, 4, 16, WIDE), bf16),
            V((n, 4, 16, WIDE), bf16), V((n, 3, 16, WIDE), bf16), D((11, 8)), D((n,)), D((n,)), D((n,)), D((n,)),
            D((n,)), D((n,)), D((n,)), D((8,))],
        compiler_params=pltpu.CompilerParams(collective_id=0, has_side_effects=True, vmem_limit_bytes=63 << 20),
        name="finish_backward",
    )(h1, dpre, act, df, qkvt, qkvl, lse, x, da, dr1, ldr1, da, lda, wout, woutl, wq, wql, ctx, ctxl,
      xl, lh1, ldf, ldpre, lact, sums, lsums, bsum, lbsum)


SWAP = [(0, 1), (1, 0)]


def fetch(w):
    core = lax.axis_index("core")
    n = w.shape[0] // 2
    mine = lax.dynamic_slice_in_dim(w, core * n, n, 0)
    got = lax.ppermute(mine, "mp", SWAP)
    sib = lax.ppermute(got, "core", SWAP)
    return jnp.where(core == 0, jnp.concatenate([got, sib], 0), jnp.concatenate([sib, got], 0))


def unpack_kernel(r, r2, up, dn, qkv, out, lqkv, lup, ldnT, lout, small):
    k = pl.program_id(0)
    for i in range(3):
        rows = slice(256 * i, 256 * i + 256)

        @pl.when(k == 0)
        def _():
            up[rows, 0:768] = r[rows, :].astype(f32)

        @pl.when(k == 1)
        def _():
            up[rows, 768:1536] = r[rows, :].astype(f32)

        @pl.when((k == 2) | (k == 3))
        def _():
            dn[rows, :] = r[rows, :].astype(f32)

        @pl.when(k == 4)
        def _():
            qkv[0, rows, :] = r[rows, 0:384].astype(f32)
            qkv[1, rows, :] = r[rows, 384:768].astype(f32)

        @pl.when(k == 5)
        def _():
            qkv[2, rows, :] = r[rows, 0:384].astype(f32)
            out[:, rows] = r[rows, 384:768].astype(f32).T

    @pl.when(k == 6)
    def _():
        for c in range(3):
            lqkv[c] = r2[0:192, 128 * c:128 * c + 96].astype(f32)
        lup[...] = r2[0:192, 384:768].astype(f32)
        small[...] = r2[192:224, :].astype(f32)
        ldnT[...] = r2[256:448, 0:384].astype(f32)
        lout[...] = r2[256:448, 384:512].astype(f32).T[:96, :]


def unpack(tot):
    const = lambda s: pl.BlockSpec(s, lambda k: (0,) * len(s))
    sd = jax.ShapeDtypeStruct
    lim = lambda v, a, b: jnp.minimum(jnp.maximum(v, a), b)
    shapes = [(768, 1536), (1536, 768), (3, 768, 384), (384, 768), (3, 192, 96), (192, 384), (192, 384), (96, 192),
              (32, 768)]
    specs = [const(s) for s in shapes]
    specs[1] = pl.BlockSpec((768, 768), lambda k: (lim(k - 2, 0, 1), 0))
    return pl.pallas_call(
        unpack_kernel, grid=(7,),
        in_specs=[pl.BlockSpec((768, 768), lambda k: (lim(k, 0, 5), 0)), pl.BlockSpec((512, 768), lambda k: (9, 0))],
        out_specs=specs, out_shape=[sd(s, f32) for s in shapes],
        compiler_params=pltpu.CompilerParams(vmem_limit_bytes=56 << 20), name="unpack_gradients",
    )(tot, tot)


def body(n_group, text_states, layout_states, box_counts, text_qkv, text_qv_bias, text_out, text_up, text_up_bias,
         text_down, text_gains, text_shifts, layout_qkv, layout_qv_bias, layout_out, layout_up, layout_up_bias,
         layout_down, layout_gains, layout_shifts, cot_text, cot_layout):
    mp = lax.axis_index("mp")
    other = lambda a: lax.ppermute(a, "mp", SWAP)
    tq = jnp.transpose(text_qkv, (1, 0, 2))
    lq = jnp.pad(jnp.transpose(layout_qkv, (1, 0, 2)), ((0, 0), (0, 0), (0, 32)))
    lo = jnp.pad(layout_out, ((0, 32), (0, 0)))
    small = jnp.concatenate([text_qv_bias.reshape(-1), layout_qv_bias.reshape(-1), text_up_bias, layout_up_bias])
    small_o = other(small)

    def split_small(s):
        z = jnp.zeros((1, 384), f32)
        tb = jnp.concatenate([s[None, :384], z, s[None, 384:768]], 0)
        lb = jnp.concatenate([s[None, 768:864], z[:, :96], s[None, 864:960]], 0)
        return tb, jnp.pad(lb, ((0, 0), (0, 32))), s[None, 960:2496], s[None, 2496:2880]

    bq, blq, bu, blu = split_small(small)
    obq, oblq, obu, oblu = split_small(small_o)
    wq = fetch(tq.reshape(2304, 384)).reshape(3, 768, 384)
    olq = other(lq)
    wo = fetch(text_out)
    olo = other(lo)
    wu = fetch(text_up)
    olu = other(layout_up)
    wd = fetch(text_down)
    old = other(layout_down)
    counts = lax.dynamic_slice_in_dim(box_counts, mp * 2, 2, 0)
    both = lambda a, b: jnp.stack([a, b])
    wq2 = both(tq, wq)
    lq2 = both(lq, olq)
    qkvt, qkvl, lse, ctx, ctxl = attend_forward(counts, text_states, layout_states, wq2, both(bq, obq), lq2,
                                                both(blq, oblq))
    out_t, dr1, da, h1, act, dpre, df, sums, bsum = middle(
        text_states, ctx, text_out, wo, text_up, wu, text_down, wd, bu, obu, text_gains, text_shifts, cot_text,
        CH=768, R=256, name="text_middle")
    out_l, ldr1, lda, lh1, lact, ldpre, ldf, lsums, lbsum = middle(
        layout_states, ctxl, lo, olo, layout_up, olu, layout_down, old, blu, oblu, layout_gains, layout_shifts,
        cot_layout, CH=384, R=512, name="layout_middle")
    tot, gx, gxlT = finish(h1, dpre, act, df, qkvt, qkvl, lse, text_states, da, dr1, ldr1, lda, both(text_out, wo),
                           both(lo, olo), wq2, lq2, ctx, ctxl, layout_states, lh1, ldf, ldpre, lact, sums, lsums, bsum,
                           lbsum)
    tot = tot.reshape(STEPS * CHUNK, WIDE)
    if n_group > 1:
        tot = lax.psum(tot, "group")
    g_up, g_dn, g_qkv, g_o, gl_qkv, gl_up, gl_dnT, gl_o, s = unpack(tot)
    l6 = s[6:12, :192]
    swap = lambda a: jnp.transpose(a, (1, 0, 2))
    return (out_t, out_l, gx, gxlT.T, swap(g_qkv), s[12].reshape(2, 384), g_o, g_up, s[14:16].reshape(1536), g_dn,
            s[0:2], s[2:6], swap(gl_qkv), s[13, :256].reshape(2, 128)[:, :96], gl_o, gl_up, s[16, :384], gl_dnT.T,
            l6[0:2], l6[2:6])


def solution(mesh):
    dp = mesh.shape["dp"]
    n_group = dp // 16
    fine = Mesh(mesh.devices.reshape(n_group, 4, 2, 2, 2), AXES)
    rows = P(AXES, None)
    half2 = P(None, "mp")
    half1 = P("mp", None)
    qkv = P(None, None, "mp")
    rep = P()
    return jax.shard_map(
        functools.partial(body, n_group),
        mesh=fine,
        in_specs=(rows, rows, P(AXES[:4]), qkv, half2, half1, half2, P("mp"), half1, rep, rep,
                  qkv, half2, half1, half2, P("mp"), half1, rep, rep, rows, rows),
        out_specs=(rows, rows, rows, rows, qkv, half2, half1, half2, P("mp"), half1, rep, rep,
                   qkv, half2, half1, half2, P("mp"), half1, rep, rep),
        check_vma=False,
    )
```

```python
import functools

import jax
import jax.numpy as jnp
from jax import lax
from jax.experimental import pallas as pl
from jax.experimental.pallas import tpu as pltpu
from jax.sharding import Mesh, PartitionSpec as P

f32 = jnp.float32
bf16 = jnp.bfloat16
SEQ = 512
NT = (((1,), (1,)), ((), ()))
TN = (((0,), (0,)), ((), ()))
AXES = ("group", "z", "x", "core", "mp")
MESH = pl.DeviceIdType.MESH
CHUNK = 256
WIDE = 768
STEPS = 20
LAGS = 7


def dot(a, b):
    return jnp.dot(a, b, preferred_element_type=f32)


def dot_nt(a, b):
    return lax.dot_general(a, b, NT, preferred_element_type=f32)


def dot_tn(a, b):
    return lax.dot_general(a, b, TN, preferred_element_type=f32)


def colsum(v):
    return jnp.sum(v, axis=0, keepdims=True)


def whole(a):
    return pl.BlockSpec(a.shape, lambda *i: (0,) * a.ndim, pipeline_mode=pl.Buffered(1))


GC = [0.11609199498651965, 0.07018864201817518, 0.2621979336040309, -0.22868178430415115, 0.38476147983842124,
      -0.10455825070574547]
GP = 0.28


def gelu_pair(v):
    t = 1.0 / (1.0 + GP * jnp.abs(v))
    g = jnp.exp(v * v * -0.5)
    q = GC[5]
    for c in GC[4::-1]:
        q = q * t + c
    q = q * t * g
    phi = jnp.where(v < 0, q, 1.0 - q)
    return v * phi, phi + v * g * 0.3989422804014327


def norm_stats(r):
    cen = r - jnp.mean(r, -1, keepdims=True)
    rstd = lax.rsqrt(jnp.mean(cen * cen, -1, keepdims=True) + 1e-5)
    return cen * rstd, rstd


def norm_back(e, n, rstd):
    return (e - jnp.mean(e, -1, keepdims=True) - n * jnp.mean(e * n, -1, keepdims=True)) * rstd


def middle_math(x, ctx0, ctx1, wo, wp, up, dn, dn_back, bias, gains, shifts, ct, act, dpre, gp_s, n1_s, nc, CH):
    attn = dot(ctx0, wo) + dot(ctx1, wp)
    n1, rstd1 = norm_stats(x + attn + shifts[2:3])
    n1_s[...] = n1
    h1b = (n1 * gains[0:1] + shifts[0:1]).astype(bf16)
    ffn = None
    for hf in range(2):
        for c in range(nc):
            cs = slice(c * CH, (c + 1) * CH)
            a, g = gelu_pair(dot(h1b, up(hf, cs)) + bias(hf, cs))
            ab = a.astype(bf16)
            act[hf, :, cs] = ab
            gp_s[hf, :, cs] = g
            t = dn(ab, hf, cs)
            ffn = t if ffn is None else ffn + t
    n2, rstd2 = norm_stats(n1_s[...] * gains[0:1] + shifts[0:1] + ffn + shifts[3:4])
    out = n2 * gains[1:2] + shifts[1:2]
    dr2 = norm_back(ct * gains[1:2], n2, rstd2)
    df = dr2.astype(bf16)
    s_g2 = colsum(ct * n2)
    s_s2 = colsum(ct)
    s_r2 = colsum(dr2)
    dh1 = dr2
    bs = {}
    for hf in range(2):
        for c in range(nc):
            cs = slice(c * CH, (c + 1) * CH)
            dp = (dn_back(df, hf, cs) * gp_s[hf, :, cs]).astype(bf16)
            dpre[hf, :, cs] = dp
            bs[hf, c] = colsum(dp.astype(f32))
            dh1 = dh1 + dot_nt(dp, up(hf, cs))
    n1 = n1_s[...]
    s_g1 = colsum(dh1 * n1)
    s_s1 = colsum(dh1)
    dr1 = norm_back(dh1 * gains[0:1], n1, rstd1)
    tot = jnp.concatenate([s_g1, s_g2, s_s1, s_s2, colsum(dr1), s_r2, jnp.zeros((2, s_g1.shape[1]), f32)], axis=0)
    return out, dr1, h1b, df, tot, bs


def row_of(b, at, n):
    return jnp.concatenate([b[i:i + 1, :] for i in range(at // 128, (at + n) // 128)], axis=1)


def text_kernel(x, ctx, wo, wp, upo, upp, dno, dnp, bo, bp, gains, shifts, cot,
                out, dr1o, dao, h1o, act, dpre, dfo, sums, bsum, gp_s, n1_s, *, CH):
    ups, dns, bs_ = (upo, upp), (dno, dnp), (bo, bp)
    nc = upo.shape[1] // CH
    o, dr1, h1b, df, tot, bs = middle_math(
        x[...].astype(f32), ctx[0], ctx[1], wo[...], wp[...], lambda h, c: ups[h][:, c],
        lambda a, h, c: dot(a, dns[h][c, :]), lambda d, h, c: dot_nt(d, dns[h][c, :]),
        lambda h, c: row_of(bs_[h], c.start, CH), gains[...], shifts[...], cot[...].astype(f32), act, dpre, gp_s, n1_s,
        nc, CH)
    out[...] = o.astype(bf16)
    dr1o[...] = dr1
    dao[...] = dr1.astype(bf16)
    h1o[...] = h1b
    dfo[...] = df
    first = pl.program_id(0) == 0
    sums[...] = jnp.where(first, tot, sums[...] + tot)
    for (h, c), v in bs.items():
        cs = slice(c * CH, (c + 1) * CH)
        bsum[h, :, cs] = jnp.where(first, v, bsum[h, :, cs] + v)


def text_middle(x, ctx, wo, wp, upo, upp, dno, dnp, bo, bp, gains, shifts, cot, *, CH, R):
    T, D = x.shape
    W = upo.shape[1]
    rows = lambda w: pl.BlockSpec((R, w), lambda i: (i, 0))
    rows3 = lambda w: pl.BlockSpec((2, R, w), lambda i: (0, i, 0))
    const = lambda s: pl.BlockSpec(s, lambda i: (0,) * len(s))
    sd = jax.ShapeDtypeStruct
    return pl.pallas_call(
        functools.partial(text_kernel, CH=CH), grid=(T // R,),
        in_specs=[rows(D), rows3(ctx.shape[2])] + [whole(a) for a in (wo, wp, upo, upp, dno, dnp, bo, bp, gains, shifts)]
        + [rows(D)],
        out_specs=[rows(D), rows(D), rows(D), rows(D), rows3(W), rows3(W), rows(D), const((8, D)), const((2, 1, W))],
        out_shape=[sd((T, D), bf16), sd((T, D), f32), sd((T, D), bf16), sd((T, D), bf16), sd((2, T, W), bf16),
                   sd((2, T, W), bf16), sd((T, D), bf16), sd((8, D), f32), sd((2, 1, W), f32)],
        scratch_shapes=[pltpu.VMEM((2, R, W), f32), pltpu.VMEM((R, D), f32)],
        compiler_params=pltpu.CompilerParams(vmem_limit_bytes=62 << 20), name="text_middle",
    )(x, ctx, wo, wp, upo, upp, dno, dnp, bo, bp, gains, shifts, cot)


def remote(src, dst, s, r, who):
    return pltpu.make_async_remote_copy(src_ref=src, dst_ref=dst, send_sem=s, recv_sem=r, device_id=who,
                                        device_id_type=MESH)


PIECES = 15
START = [0, 0, 0, 0, 1, 2, 3, 4, 6, 7, 9, 10, 12, 13, 13]
RELAY = [2, 3, 4, 5, 6, 7, 8, 9, 10, 11, 12, 13, 14, 14, 14]
AHEAD = [4, 5, 6, 6, 7, 8, 9, 10, 11, 12, 13, 14, 14, 14, 14]
BEGIN_STEPS = 15


def begin_kernel(cnt, xt, xlT, wq, lq, lo, lup, ldnT, bq, blq, bu, blu, gains, shifts, cotT,
                 a_wq, a_lq, a_wo, a_lup, a_ldnT, a_up, a_dn,
                 qkvt, qkvl, lse_o, ctxt, ctxl, outT, dr1, dao, h1o, act, dpre, dfo, sums, bsum, lqp, lop, obu_o,
                 o_wq, o_wo, o_up, o_dn,
                 cT, clT, ctl, xl_s, gp_s, n1_s, wq_v, lq_v, lup_v, ldnT_v, lo_p, lq_p, obq, oblq, obu, oblu,
                 sy, ry, sx, rx, sc, rc, sd, rd, ss, rs_, loc):
    k = pl.program_id(0)
    z, x, core, mp = (lax.axis_index(a) for a in ("z", "x", "core", "mp"))
    Y, X, C = {"mp": 1 - mp}, {"x": 1 - x}, {"core": 1 - core}
    q_me = 2 * x + core
    q_x = 2 * (1 - x) + core

    def cut(ref, q, n, sub, nsub):
        m = n // 4 // nsub
        return ref.at[pl.ds(pl.multiple_of(q * (n // 4) + sub * m, 16), m), :]

    def piece(i, q, own):
        if i < 3:
            return cut((a_wq if own else wq_v).at[i], q, 768, 0, 1)
        if i == 3:
            return (a_lq if own else lq_v).at[:, pl.ds(pl.multiple_of(q * 48, 16), 48), :]
        if i == 4:
            return cut(a_wo if own else o_wo, q, 384, 0, 1)
        if i == 5:
            return cut(a_lup if own else lup_v, q, 192, 0, 1)
        if i == 6:
            return cut(a_ldnT if own else ldnT_v, q, 192, 0, 1)
        if i < 11:
            return cut(a_up if own else o_up, q, 768, i - 7, 4)
        return cut(a_dn if own else o_dn, q, 1536, i - 11, 4)

    def over_y(i):
        return remote(piece(i, q_me, True), piece(i, q_me, False), sy.at[i], ry.at[i], Y)

    def over_x(i):
        return remote(piece(i, q_me, False), piece(i, q_me, False), sx.at[i], rx.at[i], X)

    def over_core(i):
        return remote(piece(i, q_me, False), piece(i, q_me, False), sc.at[i], rc.at[i], C)

    def over_core2(i):
        return remote(piece(i, q_x, False), piece(i, q_x, False), sd.at[i], rd.at[i], C)

    def small():
        pairs = ((bq, obq), (blq, oblq), (bu, obu), (blu, oblu), (lo, lo_p.at[1, 0:96]))
        return [remote(a, b, ss.at[i], rs_.at[i], Y) for i, (a, b) in enumerate(pairs)]

    @pl.when(k == 0)
    def _():
        lo_p[...] = jnp.zeros_like(lo_p)
        bar = pltpu.get_barrier_semaphore()
        for who in (C, Y, X):
            pl.semaphore_signal(bar, inc=1, device_id=who, device_id_type=MESH)
        pl.semaphore_wait(bar, 3)

    order = list(range(PIECES))
    for s in range(BEGIN_STEPS):
        @pl.when(k == s)
        def _(s=s):
            if s == 0:
                lq_p[...] = jnp.zeros_like(lq_p)
                for c in small():
                    c.start()
                lo_p[0, 0:96, :] = lo[...]
                for c in range(3):
                    lq_p[0, c, :, 0:96] = lq[c]
                sums[...] = jnp.zeros_like(sums)
                bsum[...] = jnp.zeros_like(bsum)
            for i in order:
                if START[i] == s:
                    over_y(i).start()
            for i in order:
                if RELAY[i] == s:
                    over_y(i).wait_recv()
                    over_x(i).start()
                    over_core(i).start()
                if AHEAD[i] == s:
                    over_x(i).wait_recv()
                    over_core2(i).start()
            if s == 6:
                for c in small():
                    c.wait_recv()
                for i in range(4):
                    over_core(i).wait_recv()
                    over_core2(i).wait_recv()
                for c in range(3):
                    lq_p[1, c, :, 0:96] = lq_v[c]
                pltpu.make_async_copy(wq_v, o_wq, loc).start()
            if s == 12:
                for i in (5, 6):
                    over_core(i).wait_recv()
                    over_core2(i).wait_recv()

    @pl.when(k < 12)
    def _():
        hf = k // 6
        page = (k % 6) // 3
        pair = k % 3

        def project(w, b, lb):
            n = cnt[page]
            lane = lax.broadcasted_iota(jnp.int32, (SEQ, 128), 1)
            row = lax.broadcasted_iota(jnp.int32, (SEQ, 128), 0)
            for c in range(3):
                r = dot(xt[...], w[c])
                s = dot(xl_s[page], lq_p[hf, c])
                if c != 1:
                    r = r + b[c // 2:c // 2 + 1]
                    s = s + jnp.concatenate([lb[c // 2:c // 2 + 1], jnp.zeros((1, 32), f32)], axis=1)
                if c == 0:
                    r = r * 0.125
                    s = jnp.where(lane == 96, 1.0, s * 0.25)
                if c == 1:
                    s = jnp.where((lane == 96) & (row >= n), -1e30, s)
                for p in range(3):
                    qkvt[0, c, p] = r[:, 128 * p:128 * p + 128].astype(bf16)
                qkvl[0, c] = s.astype(bf16)

        @pl.when((pair == 0) & (hf == 0))
        def _():
            xl_s[page] = xlT[...].T
            project(wq, bq, blq)

        @pl.when((pair == 0) & (hf == 1))
        def _():
            project(wq_v, obq, oblq)

        @pl.when(pair == 0)
        def _():
            clT[...] = jnp.zeros_like(clT)
            lse_o[...] = jnp.zeros_like(lse_o)

        qc = jnp.concatenate([qkvt[0, 0, pair], qkvl[0, 0]], axis=1)
        kc = jnp.concatenate([qkvt[0, 1, pair], qkvl[0, 1]], axis=1)
        vtT = qkvt[0, 2, pair].T
        vlT = qkvl[0, 2].T
        lane = lax.broadcasted_iota(jnp.int32, (1, 256), 1)
        for hh in range(2):
            h = 2 * pair + hh
            mk = ((lane >= 64 * hh) & (lane < 64 * hh + 64)) | ((lane >= 128 + 16 * h) & (lane < 144 + 16 * h))
            S = dot_nt(jnp.where(mk | (lane == 224), kc, jnp.zeros_like(kc)), qc)
            m = jnp.max(S, axis=0, keepdims=True)
            e = jnp.exp(S - m)
            l = colsum(e)
            o = dot(jnp.concatenate([vtT[64 * hh:64 * hh + 64], vlT], axis=0), e.astype(bf16)) * (1.0 / l)
            cT[64 * hh:64 * hh + 64, :] = o[:64]
            row = lax.broadcasted_iota(jnp.int32, (128, 1), 0)
            clT[...] += jnp.where((row >= 16 * h) & (row < 16 * h + 16), o[64:], 0.0)
            r8 = lax.broadcasted_iota(jnp.int32, (8, 1), 0)
            lse_o[0, 0] += jnp.where(r8 == h, m + jnp.log(l), 0.0)
        for p in range(3):
            @pl.when(pair == p)
            def _(p=p):
                ctxt[0, :, 128 * p:128 * p + 128] = cT[...].T.astype(bf16)

        @pl.when(pair == 2)
        def _():
            cl = clT[...].T.astype(bf16)
            ctxl[0] = cl
            ctl[hf, page] = cl

    @pl.when((k == 12) | (k == 13))
    def _():
        page = k - 12
        wops = lambda h: lo_p[h]
        ups, dns, bs_ = (lup, lup_v), (ldnT, ldnT_v), (blu, oblu)
        o, d1, h1b, df, tot, bs = middle_math(
            xl_s[page].astype(f32), ctl[0, page], ctl[1, page], lo_p[0], lo_p[1], lambda h, c: ups[h][...],
            lambda a, h, c: dot_nt(a, dns[h][...]), lambda d, h, c: dot(d, dns[h][...]),
            lambda h, c: row_of(bs_[h], 0, 384), gains[...], shifts[...], cotT[...].T.astype(f32), act, dpre, gp_s, n1_s,
            1, 384)
        outT[...] = o.T.astype(bf16)
        dr1[...] = d1
        dao[...] = d1.astype(bf16)
        h1o[...] = h1b
        dfo[...] = df
        sums[...] += tot
        for (h, c), v in bs.items():
            bsum[h] += v

    @pl.when(k == BEGIN_STEPS - 1)
    def _():
        for h in range(2):
            lop[h] = lo_p[h]
            for c in range(3):
                lqp[h, c] = lq_p[h, c]
        obu_o[...] = obu[...]
        for i in range(PIECES):
            if i in (4,) or i > 6:
                over_core(i).wait_recv()
                over_core2(i).wait_recv()
        for i in range(PIECES):
            over_y(i).wait_send()
            over_x(i).wait_send()
            over_core(i).wait_send()
            over_core2(i).wait_send()
        for c in small():
            c.wait_send()
        pltpu.make_async_copy(wq_v, o_wq, loc).wait()


def begin_forward(cnt, xt, xlT, wq, lq, wo, lo, lup, ldnT, up, dn, bq, blq, bu, blu, gains, shifts, cotT):
    T = xt.shape[0]
    n = T // SEQ
    lim = lambda v, a, b: jnp.minimum(jnp.maximum(v, a), b)
    hf = lambda k: lim(k, 0, 11) // 6
    pg = lambda k: (lim(k, 0, 11) % 6) // 3
    lp = lambda k: lim(k - 12, 0, 1)
    anyspec = pl.BlockSpec(memory_space=pl.ANY)
    const = lambda s: pl.BlockSpec(s, lambda k, *_: (0,) * len(s))
    V = pltpu.VMEM
    D = pltpu.SemaphoreType.DMA
    sds = jax.ShapeDtypeStruct
    lrows = pl.BlockSpec((SEQ, 192), lambda k, *_: (lp(k), 0))
    lrows3 = pl.BlockSpec((2, SEQ, 384), lambda k, *_: (0, lp(k), 0))
    return pl.pallas_call(
        begin_kernel,
        grid_spec=pltpu.PrefetchScalarGridSpec(
            num_scalar_prefetch=1, grid=(BEGIN_STEPS,),
            in_specs=[pl.BlockSpec((SEQ, 768), lambda k, *_: (pg(k), 0)),
                      pl.BlockSpec((192, SEQ), lambda k, *_: (0, pg(k)))]
            + [whole(a) for a in (wq, lq, lo, lup, ldnT, bq, blq, bu, blu, gains, shifts)]
            + [pl.BlockSpec((192, SEQ), lambda k, *_: (0, lp(k)))] + [anyspec] * 7,
            out_specs=[pl.BlockSpec((1, 3, 3, SEQ, 128), lambda k, *_: (hf(k), 0, 0, pg(k), 0)),
                       pl.BlockSpec((1, 3, SEQ, 128), lambda k, *_: (hf(k), 0, pg(k), 0)),
                       pl.BlockSpec((1, 1, 8, SEQ), lambda k, *_: (hf(k), pg(k), 0, 0)),
                       pl.BlockSpec((1, SEQ, 384), lambda k, *_: (hf(k), pg(k), 0)),
                       pl.BlockSpec((1, SEQ, 128), lambda k, *_: (hf(k), pg(k), 0)),
                       pl.BlockSpec((192, SEQ), lambda k, *_: (0, lp(k))),
                       lrows, lrows, lrows, lrows3, lrows3, lrows, const((8, 192)), const((2, 1, 384)),
                       const((2, 3, 192, 128)), const((2, 128, 192)), const((12, 128)),
                       anyspec, anyspec, anyspec, anyspec],
            scratch_shapes=[
                V((128, SEQ), f32), V((128, SEQ), f32), V((2, n, SEQ, 128), bf16), V((n, SEQ, 192), bf16),
                V((2, SEQ, 384), f32), V((SEQ, 192), f32), V((3, 768, 384), bf16), V((3, 192, 96), bf16),
                V((192, 384), bf16), V((192, 384), bf16), V((2, 128, 192), bf16), V((2, 3, 192, 128), bf16),
                V((2, 384), f32), V((2, 96), f32), V((12, 128), f32), V((3, 128), f32)]
            + [D((PIECES,))] * 8 + [D((5,)), D((5,)), D]),
        out_shape=[sds((2, 3, 3, T, 128), bf16), sds((2, 3, T, 128), bf16), sds((2, n, 8, SEQ), f32),
                   sds((2, T, 384), bf16), sds((2, T, 128), bf16), sds((192, T), bf16), sds((T, 192), f32),
                   sds((T, 192), bf16), sds((T, 192), bf16), sds((2, T, 384), bf16), sds((2, T, 384), bf16),
                   sds((T, 192), bf16), sds((8, 192), f32), sds((2, 1, 384), f32), sds((2, 3, 192, 128), bf16),
                   sds((2, 128, 192), bf16), sds((12, 128), f32), sds((3, 768, 384), bf16), sds((384, 768), bf16),
                   sds((768, 1536), bf16), sds((1536, 768), bf16)],
        compiler_params=pltpu.CompilerParams(collective_id=1, has_side_effects=True, vmem_limit_bytes=56 << 20),
        name="begin_forward",
    )(cnt, xt, xlT, wq, lq, lo, lup, ldnT, bq, blq, bu, blu, gains, shifts, cotT, wq, lq, wo, lup, ldnT, up, dn)


def finish_kernel(h1, dpre, act, df, qkvt, qkvl, lse, xblk, dablk, dr1, ldr1, da, lda, wout, woutp, woutl, wq, wqp, wql, ctx, ctxl,
                  xlT, lh1, ldf, ldpre, lact, sums, lsums, bsum, lbsum,
                  res, gx, gxlT,
                  DQ, DQL, dct_s, dcl_s, klT_s, avl, akl, dqT, dqlT, small,
                  P, RC, RY, RX, RZ, sends, rA, rB, rC, rD, rE, rF, rH, loc):
    n = STEPS
    k = pl.program_id(0)
    z, x, core, mp = (lax.axis_index(a) for a in ("z", "x", "core", "mp"))

    @pl.when(k == 0)
    def _():
        bar = pltpu.get_barrier_semaphore()
        for who in ({"core": 1 - core}, {"mp": 1 - mp}, {"x": 1 - x}):
            pl.semaphore_signal(bar, inc=1, device_id=who, device_id_type=MESH)
        for d in range(1, 4):
            pl.semaphore_signal(bar, inc=1, device_id={"z": (z + d) % 4}, device_id_type=MESH)
        pl.semaphore_wait(bar, 6)

    def put(o, t):
        t = t.astype(bf16).reshape(2, 2, 4, 16, WIDE)
        P[k % 2, 0, o] = t[0]
        P[k % 2, 1, o] = t[1]

    @pl.when(k < 6)
    def _():
        hT = h1[...].T
        for h in range(2):
            put(1 - h, dot(hT, dpre[h]))

    @pl.when((k >= 6) & (k < 12))
    def _():
        for h in range(2):
            put(1 - h, dot_tn(act[h], df[...]))

    cat3 = lambda h, c: jnp.concatenate([DQ[h, c, 0], DQ[h, c, 1], DQ[h, c, 2]], axis=1)

    @pl.when((k >= 12) & (k < 15))
    def _():
        xT = xblk[...].T
        for h in range(2):
            put(1 - h, jnp.concatenate([dot(xT, cat3(h, 0)), dot(xT, cat3(h, 1))], axis=1))

    @pl.when((k >= 15) & (k < 18))
    def _():
        xT = xblk[...].T
        dT = dablk[...].T
        for h in range(2):
            put(1 - h, jnp.concatenate([dot(xT, cat3(h, 2)), dot(dT, ctx[h])], axis=1))

    @pl.when(k == 18)
    def _():
        xT = xlT[...]
        hT = lh1[...].T
        for h in range(2):
            t = jnp.concatenate([dot(xT, DQL[h, 0]), dot(xT, DQL[h, 1]), dot(xT, DQL[h, 2]), dot(hT, ldpre[h])], axis=1)
            small[...] = jnp.zeros_like(small)
            small[0:6, :] = sums[0:6, :]
            small[6:12, 0:192] = lsums[0:6, :]
            for i, c in enumerate((0, 2)):
                for p in range(3):
                    at = 384 * i + 128 * p
                    small[12:13, at:at + 128] = colsum(DQ[h, c, p].astype(f32))
                small[13:14, 128 * i:128 * i + 128] = colsum(DQL[h, c].astype(f32))
            small[14:15, :] = bsum[h, :, 0:768]
            small[15:16, :] = bsum[h, :, 768:1536]
            small[16:17, 0:384] = lbsum[h]
            put(1 - h, jnp.concatenate([t, small[...]], axis=0))

    @pl.when(k == 19)
    def _():
        fT = ldf[...].T
        aT = lda[...].T
        for h in range(2):
            t = jnp.concatenate([dot(fT, lact[h]), dot(aT, ctxl[h]), jnp.zeros((192, 256), f32)], axis=1)
            put(1 - h, jnp.concatenate([t, jnp.zeros((64, WIDE), f32)], axis=0))

    def cA(j):
        return remote(P.at[j % 2, 1 - core], RC.at[j], sends.at[0, j % 8], rA.at[j], {"core": 1 - core})

    def cB(j):
        return remote(RC.at[j, 0], RY.at[j], sends.at[1, j % 8], rB.at[j], {"mp": 1 - mp})

    def cC(j):
        return remote(RY.at[j, 1 - x], RX.at[j], sends.at[2, j % 8], rC.at[j], {"x": 1 - x})

    def cD(j, d):
        t = (z + d) % 4
        return remote(RX.at[j, t], RZ.at[j, 3 - d], sends.at[2 + d, j % 8], rD.at[j], {"z": t})

    def cE(j, d):
        return remote(RX.at[j, z], res.at[j, core, x, z], sends.at[5 + d, j % 8], rE.at[j], {"z": (z + d) % 4})

    def cF(j):
        return remote(res.at[j, core, x], res.at[j, core, x], sends.at[9, j % 8], rF.at[j], {"x": 1 - x})

    def cH(j):
        return remote(res.at[j, core], res.at[j, core], sends.at[10, j % 8], rH.at[j], {"core": 1 - core})

    def stage(lag):
        j = k - lag
        return j, (j >= 0) & (j < n)

    j0, live0 = stage(0)

    @pl.when(live0)
    def _():
        cA(j0).start()

    j1, live1 = stage(1)

    @pl.when(live1)
    def _():
        j = j1
        cA(j).wait_recv()
        for i in range(2):
            RC[j, i] = (RC[j, i].astype(f32) + P[j % 2, core, i].astype(f32)).astype(bf16)
        cB(j).start()
        cA(j).wait_send()

    @pl.when(k < 12)
    def _():
        hf = 1 - k // 6
        page = (k % 6) // 3
        pair = k % 3
        rs = pl.ds(pl.multiple_of(page * SEQ, SEQ), SEQ)

        @pl.when(pair == 0)
        def _():
            for h, w in enumerate((wout, woutp)):
                @pl.when(hf == h)
                def _(w=w):
                    dct = dot_nt(da[rs, :], w[...]).astype(bf16)
                    for p in range(3):
                        dct_s[p] = dct[:, 128 * p:128 * p + 128]

            dcl_s[...] = dot_nt(lda[rs, :], woutl[hf]).astype(bf16)
            klT_s[...] = qkvl[0, 1].T
            avl[...] = jnp.zeros_like(avl)
            akl[...] = jnp.zeros_like(akl)
            dqlT[...] = jnp.zeros_like(dqlT)

        qc = jnp.concatenate([qkvt[0, 0, 0], qkvl[0, 0]], axis=1)
        kc = jnp.concatenate([qkvt[0, 1, 0], qkvl[0, 1]], axis=1)
        vc = jnp.concatenate([qkvt[0, 2, 0], qkvl[0, 2]], axis=1)
        dc = jnp.concatenate([dct_s[pair], dcl_s[...]], axis=1)
        ktT = qkvt[0, 1, 0].T
        zero = jnp.zeros_like(kc)
        av = ak = None
        for hh in range(2):
            h = 2 * pair + hh
            lane = lax.broadcasted_iota(jnp.int32, (1, 256), 1)
            mv = ((lane >= 64 * hh) & (lane < 64 * hh + 64)) | ((lane >= 128 + 16 * h) & (lane < 144 + 16 * h))
            mk = mv | (lane == 224)
            E = jnp.exp(dot_nt(jnp.where(mk, kc, zero), qc) - lse[0, 0, pl.ds(h, 1), :])
            dP = dot_nt(jnp.where(mv, vc, zero), dc)
            X = E * dP
            dS = (X - E * colsum(X)).astype(bf16)
            ov = dot(E.astype(bf16), jnp.where(mv, dc, zero))
            ok = dot(dS, jnp.where(mv, qc, zero))
            av = ov[:, :128] if av is None else av + ov[:, :128]
            ak = ok[:, :128] if ak is None else ak + ok[:, :128]
            avl[...] += ov[:, 128:]
            akl[...] += ok[:, 128:]
            ls = pl.ds(pl.multiple_of(16 * h, 16), 16)
            kT = jnp.concatenate([ktT[64 * hh:64 * hh + 64], klT_s[ls, :]], axis=0)
            oq = dot(kT, dS)
            dqT[64 * hh:64 * hh + 64, :] = oq[:64] * 0.125
            dqlT[ls, :] = oq[64:] * 0.25
        DQ[hf, 0, pair, rs, :] = dqT[...].T.astype(bf16)
        DQ[hf, 1, pair, rs, :] = ak.astype(bf16)
        DQ[hf, 2, pair, rs, :] = av.astype(bf16)

        @pl.when(pair == 2)
        def _():
            DQL[hf, 0, rs, :] = dqlT[...].T.astype(bf16)
            DQL[hf, 1, rs, :] = akl[...].astype(bf16)
            DQL[hf, 2, rs, :] = avl[...].astype(bf16)

    @pl.when((k >= STEPS) & (k < STEPS + 4))
    def _():
        rs = pl.ds(pl.multiple_of((k - STEPS) * 256, 256), 256)
        g = dr1[...]
        gl = ldr1[...]
        for h in range(2):
            for c in range(3):
                g = g + dot_nt(jnp.concatenate([DQ[h, c, p, rs, :] for p in range(3)], axis=1), (wq, wqp)[h][c])
                gl = gl + dot_nt(DQL[h, c, rs, :], wql[h, c])
        gx[...] = g
        gxlT[...] = gl.T

    j2, live2 = stage(2)

    @pl.when(live2)
    def _():
        j = j2
        cB(j).wait_recv()
        RY[j] = (RY[j].astype(f32) + RC[j, 1].astype(f32)).astype(bf16)
        cC(j).start()

    j3, live3 = stage(3)

    @pl.when(live3)
    def _():
        j = j3
        cC(j).wait_recv()
        RX[j] = (RX[j].astype(f32) + RY[j, x].astype(f32)).astype(bf16)
        for d in range(1, 4):
            cD(j, d).start()

    j4, live4 = stage(4)

    @pl.when(live4)
    def _():
        j = j4
        remote(RZ.at[j], RZ.at[j], sends.at[3, j % 8], rD.at[j], {"z": (z + 1) % 4}).wait_recv()
        tot = RX[j, z].astype(f32)
        for d in range(3):
            tot = tot + RZ[j, d].astype(f32)
        RX[j, z] = tot.astype(bf16)
        for d in range(1, 4):
            cE(j, d).start()
        pltpu.make_async_copy(RX.at[j, z], res.at[j, core, x, z], loc.at[j % 8]).start()

    j5, live5 = stage(5)

    @pl.when(live5)
    def _():
        j = j5
        remote(res.at[j, core, x, pl.ds(0, 3)], res.at[j, core, x, pl.ds(0, 3)], sends.at[6, j % 8], rE.at[j],
               {"z": (z + 1) % 4}).wait_recv()
        pltpu.make_async_copy(RX.at[j, z], res.at[j, core, x, z], loc.at[j % 8]).wait()
        cF(j).start()

    j6, live6 = stage(6)

    @pl.when(live6)
    def _():
        cF(j6).wait_recv()
        cH(j6).start()

    j7, live7 = stage(7)

    @pl.when(live7)
    def _():
        j = j7
        cH(j).wait_recv()
        cB(j).wait_send()
        cC(j).wait_send()
        for d in range(1, 4):
            cD(j, d).wait_send()
            cE(j, d).wait_send()
        cF(j).wait_send()
        cH(j).wait_send()


def finish(h1, dpre, act, df, qkvt, qkvl, lse, x, da, dr1, ldr1, lda, wout, woutp, woutl, wq, wqp, wql, ctx, ctxl,
           xlT, lh1, ldf, ldpre, lact, sums, lsums, bsum, lbsum):
    n = STEPS
    T = x.shape[0]
    lim = lambda v, a, b: jnp.minimum(jnp.maximum(v, a), b)
    att = lambda k: lim(k, 0, 11)
    head = lambda k: (1 - att(k) // 6, (att(k) % 6) // 3, att(k) % 3)
    D = pltpu.SemaphoreType.DMA
    V = pltpu.VMEM
    sd = jax.ShapeDtypeStruct
    one = pl.Buffered(1)
    in_specs = [
        pl.BlockSpec((T, 256), lambda k: (0, lim(k, 0, 5) % 3)),
        pl.BlockSpec((2, T, WIDE), lambda k: (0, 0, lim(k, 0, 5) // 3), pipeline_mode=one),
        pl.BlockSpec((2, T, 256), lambda k: (0, 0, lim(k - 6, 0, 5))),
        whole(df),
        pl.BlockSpec((1, 3, 1, SEQ, 128), lambda k: (head(k)[0], 0, head(k)[2], head(k)[1], 0)),
        pl.BlockSpec((1, 3, SEQ, 128), lambda k: (head(k)[0], 0, head(k)[1], 0)),
        pl.BlockSpec((1, 1, 8, SEQ), lambda k: (head(k)[0], head(k)[1], 0, 0)),
        pl.BlockSpec((T, 256), lambda k: (0, lim(k - 12, 0, 5) % 3)),
        pl.BlockSpec((T, 256), lambda k: (0, lim(k - 15, 0, 2))),
        pl.BlockSpec((256, WIDE), lambda k: (lim(k - STEPS, 0, 3), 0)),
        pl.BlockSpec((256, 192), lambda k: (lim(k - STEPS, 0, 3), 0)),
    ] + [whole(a) for a in (da, lda, wout, woutp, woutl, wq, wqp, wql, ctx, ctxl, xlT, lh1, ldf, ldpre, lact, sums, lsums,
                             bsum, lbsum)]
    return pl.pallas_call(
        finish_kernel,
        grid=(n + LAGS,),
        in_specs=in_specs,
        out_specs=[pl.BlockSpec(memory_space=pl.ANY),
                   pl.BlockSpec((256, WIDE), lambda k: (lim(k - STEPS, 0, 3), 0)),
                   pl.BlockSpec((192, 256), lambda k: (0, lim(k - STEPS, 0, 3)))],
        out_shape=[sd((n, 2, 2, 4, 16, WIDE), bf16), sd((T, WIDE), f32), sd((192, T), f32)],
        scratch_shapes=[
            V((2, 3, 3, T, 128), bf16), V((2, 3, T, 128), bf16), V((3, SEQ, 128), bf16), V((SEQ, 128), bf16),
            V((128, SEQ), bf16), V((SEQ, 128), f32), V((SEQ, 128), f32), V((128, SEQ), f32), V((128, SEQ), f32),
            V((64, WIDE), f32),
            V((2, 2, 2, 2, 4, 16, WIDE), bf16), V((n, 2, 2, 4, 16, WIDE), bf16), V((n, 2, 4, 16, WIDE), bf16),
            V((n, 4, 16, WIDE), bf16), V((n, 3, 16, WIDE), bf16), D((11, 8)), D((n,)), D((n,)), D((n,)), D((n,)),
            D((n,)), D((n,)), D((n,)), D((8,))],
        compiler_params=pltpu.CompilerParams(collective_id=0, has_side_effects=True, vmem_limit_bytes=63 << 20),
        name="finish_backward",
    )(h1, dpre, act, df, qkvt, qkvl, lse, x, da, dr1, ldr1, da, lda, wout, woutp, woutl, wq, wqp, wql, ctx, ctxl,
      xlT, lh1, ldf, ldpre, lact, sums, lsums, bsum, lbsum)


def unpack_kernel(r, r2, up, dn, qkv, out, lqkv, lup, ldnT, lout, small):
    k = pl.program_id(0)
    for i in range(3):
        rows = slice(256 * i, 256 * i + 256)

        @pl.when(k == 0)
        def _():
            up[rows, 0:768] = r[rows, :].astype(f32)

        @pl.when(k == 1)
        def _():
            up[rows, 768:1536] = r[rows, :].astype(f32)

        @pl.when((k == 2) | (k == 3))
        def _():
            dn[rows, :] = r[rows, :].astype(f32)

        @pl.when(k == 4)
        def _():
            qkv[0, rows, :] = r[rows, 0:384].astype(f32)
            qkv[1, rows, :] = r[rows, 384:768].astype(f32)

        @pl.when(k == 5)
        def _():
            qkv[2, rows, :] = r[rows, 0:384].astype(f32)
            out[:, rows] = r[rows, 384:768].astype(f32).T

    @pl.when(k == 6)
    def _():
        for c in range(3):
            lqkv[c] = r2[0:192, 128 * c:128 * c + 96].astype(f32)
        lup[...] = r2[0:192, 384:768].astype(f32)
        small[...] = r2[192:224, :].astype(f32)
        ldnT[...] = r2[256:448, 0:384].astype(f32)
        lout[...] = r2[256:448, 384:512].astype(f32).T[:96, :]


def unpack(tot):
    const = lambda s: pl.BlockSpec(s, lambda k: (0,) * len(s))
    sd = jax.ShapeDtypeStruct
    lim = lambda v, a, b: jnp.minimum(jnp.maximum(v, a), b)
    shapes = [(768, 1536), (1536, 768), (3, 768, 384), (384, 768), (3, 192, 96), (192, 384), (192, 384), (96, 192),
              (32, 768)]
    specs = [const(s) for s in shapes]
    specs[1] = pl.BlockSpec((768, 768), lambda k: (lim(k - 2, 0, 1), 0))
    return pl.pallas_call(
        unpack_kernel, grid=(7,),
        in_specs=[pl.BlockSpec((768, 768), lambda k: (lim(k, 0, 5), 0)), pl.BlockSpec((512, 768), lambda k: (9, 0))],
        out_specs=specs, out_shape=[sd(s, f32) for s in shapes],
        compiler_params=pltpu.CompilerParams(vmem_limit_bytes=56 << 20), name="unpack_gradients",
    )(tot, tot)


def body(n_group, text_states, layout_states, box_counts, text_qkv, text_qv_bias, text_out, text_up, text_up_bias,
         text_down, text_gains, text_shifts, layout_qkv, layout_qv_bias, layout_out, layout_up, layout_up_bias,
         layout_down, layout_gains, layout_shifts, cot_text, cot_layout):
    mp = lax.axis_index("mp")
    tq = jnp.transpose(text_qkv, (1, 0, 2))
    lq = jnp.transpose(layout_qkv, (1, 0, 2))
    xlT = layout_states.T
    counts = lax.dynamic_slice_in_dim(box_counts, mp * 2, 2, 0)
    bu = text_up_bias.reshape(12, 128)
    (qkvt, qkvl, lse, ctx, ctxl, out_lT, ldr1, lda, lh1, lact, ldpre, ldf, lsums, lbsum, lqp, lop, obu, wq, wo, wu,
     wd) = begin_forward(
        counts, text_states, xlT, tq, lq, text_out, layout_out, layout_up, layout_down.T, text_up, text_down,
        text_qv_bias, layout_qv_bias, bu, layout_up_bias.reshape(3, 128), layout_gains, layout_shifts, cot_layout.T)
    out_t, dr1, da, h1, act, dpre, df, sums, bsum = text_middle(
        text_states, ctx, text_out, wo, text_up, wu, text_down, wd, bu, obu, text_gains, text_shifts, cot_text,
        CH=768, R=256)
    tot, gx, gxlT = finish(h1, dpre, act, df, qkvt, qkvl, lse, text_states, da, dr1, ldr1, lda, text_out, wo, lop, tq, wq,
                           lqp, ctx, ctxl, xlT, lh1, ldf, ldpre, lact, sums, lsums, bsum, lbsum)
    tot = tot.reshape(STEPS * CHUNK, WIDE)
    if n_group > 1:
        tot = lax.psum(tot, "group")
    g_up, g_dn, g_qkv, g_o, gl_qkv, gl_up, gl_dnT, gl_o, s = unpack(tot)
    l6 = s[6:12, :192]
    swap = lambda a: jnp.transpose(a, (1, 0, 2))
    return (out_t, out_lT.T, gx, gxlT.T, swap(g_qkv), s[12].reshape(2, 384), g_o, g_up, s[14:16].reshape(1536), g_dn,
            s[0:2], s[2:6], swap(gl_qkv), s[13, :256].reshape(2, 128)[:, :96], gl_o, gl_up, s[16, :384], gl_dnT.T,
            l6[0:2], l6[2:6])


def solution(mesh):
    dp = mesh.shape["dp"]
    n_group = dp // 16
    fine = Mesh(mesh.devices.reshape(n_group, 4, 2, 2, 2), AXES)
    rows = P(AXES, None)
    half2 = P(None, "mp")
    half1 = P("mp", None)
    qkv = P(None, None, "mp")
    rep = P()
    return jax.shard_map(
        functools.partial(body, n_group),
        mesh=fine,
        in_specs=(rows, rows, P(AXES[:4]), qkv, half2, half1, half2, P("mp"), half1, rep, rep,
                  qkv, half2, half1, half2, P("mp"), half1, rep, rep, rows, rows),
        out_specs=(rows, rows, rows, rows, qkv, half2, half1, half2, P("mp"), half1, rep, rep,
                   qkv, half2, half1, half2, P("mp"), half1, rep, rep),
        check_vma=False,
    )
```

```python
import functools

import jax
import jax.numpy as jnp
from jax import lax
from jax.experimental import pallas as pl
from jax.experimental.pallas import tpu as pltpu
from jax.sharding import Mesh, PartitionSpec as P

f32 = jnp.float32
bf16 = jnp.bfloat16
SEQ = 512
NT = (((1,), (1,)), ((), ()))
TN = (((0,), (0,)), ((), ()))
AXES = ("group", "z", "x", "core", "mp")
MESH = pl.DeviceIdType.MESH
CHUNK = 256
WIDE = 768
N_CHUNK = 20


def dot(a, b):
    return jnp.dot(a, b, preferred_element_type=f32)


def dot_nt(a, b):
    return lax.dot_general(a, b, NT, preferred_element_type=f32)


def dot_tn(a, b):
    return lax.dot_general(a, b, TN, preferred_element_type=f32)


def colsum(v):
    return jnp.sum(v, axis=0, keepdims=True)


def whole(a):
    return pl.BlockSpec(a.shape, lambda *i: (0,) * a.ndim, pipeline_mode=pl.Buffered(1))


GC = [0.11609199498651965, 0.07018864201817518, 0.2621979336040309, -0.22868178430415115, 0.38476147983842124,
      -0.10455825070574547]
GP = 0.28


def gelu_pair(v):
    t = 1.0 / (1.0 + GP * jnp.abs(v))
    g = jnp.exp(v * v * -0.5)
    q = GC[5]
    for c in GC[4::-1]:
        q = q * t + c
    q = q * t * g
    phi = jnp.where(v < 0, q, 1.0 - q)
    return v * phi, phi + v * g * 0.3989422804014327


def norm_stats(r):
    cen = r - jnp.mean(r, -1, keepdims=True)
    rstd = lax.rsqrt(jnp.mean(cen * cen, -1, keepdims=True) + 1e-5)
    return cen * rstd, rstd


def norm_back(e, n, rstd):
    return (e - jnp.mean(e, -1, keepdims=True) - n * jnp.mean(e * n, -1, keepdims=True)) * rstd


def head_masks(h):
    lane = lax.broadcasted_iota(jnp.int32, (1, 256), 1)
    t = (lane >= 64 * (h % 2)) & (lane < 64 * (h % 2) + 64)
    l = (lane >= 128 + 16 * h) & (lane < 128 + 16 * h + 16)
    return t | l, t | l | (lane == 224)


def row_of(b, at, n):
    return jnp.concatenate([b[i:i + 1, :] for i in range(at // 128, (at + n) // 128)], axis=1)


def clip(v, a, b):
    return jnp.minimum(jnp.maximum(v, a), b)


def remote(src, dst, s, r, who):
    return pltpu.make_async_remote_copy(src_ref=src, dst_ref=dst, send_sem=s, recv_sem=r, device_id=who,
                                        device_id_type=MESH)


def forward_math(x, ctx0, ctx1, wo, wp, up, dn, bias, gains, shifts, ct, act, gp, nc, CH, hook):
    attn = dot(ctx0, wo) + dot(ctx1, wp)
    n1, rstd1 = norm_stats(x + attn + shifts[2:3])
    h1 = n1 * gains[0:1] + shifts[0:1]
    h1b = h1.astype(bf16)
    r2 = h1 + shifts[3:4]
    for hf in range(2):
        if hf == 1:
            hook()
        for c in range(nc):
            cs = slice(c * CH, (c + 1) * CH)
            a, g = gelu_pair(dot(h1b, up(hf, cs)) + bias(hf, cs))
            ab = a.astype(bf16)
            act[hf, :, cs] = ab
            gp[hf, :, cs] = g.astype(gp.dtype)
            r2 = r2 + dn(ab, hf, cs)
    n2, rstd2 = norm_stats(r2)
    out = n2 * gains[1:2] + shifts[1:2]
    dr2 = norm_back(ct * gains[1:2], n2, rstd2)
    return n1, rstd1, h1b, out, dr2, (colsum(ct * n2), colsum(ct), colsum(dr2))


PIECES = 15
START = [0, 0, 0, 0, 1, 2, 2, 3, 4, 6, 7, 8, 10, 11, 12]
RELAY = [2, 3, 4, 4, 6, 6, 6, 8, 9, 10, 12, 14, 15, 16, 17]
AHEAD = [4, 5, 6, 6, 8, 8, 8, 9, 11, 12, 14, 16, 16, 17, 17]
TEXT = 6
FWD_STEPS = 10


def forward_kernel(cnt, xt, xlT, wq, lq, lo, lup, ldnT, bq, blq, bu, blu, lgains, lshifts, lcotT, x2, gains, shifts, cot,
                   a_wq, a_lq, a_wo, a_lup, a_ldnT, a_up, a_dn,
                   qkvt, qkvl, lse_o, ctxt, outT, ldr1, dcl, lay1, lay2, lsums, lbsum, lqp,
                   out, act, gp, h1T, dfo, dr2o, n1o, rso, sums, o_wq, o_wo, o_up, o_dn,
                   cT, clT, ctx_s, ctl, xl_s, lact, lgp, ldpre, lh1, ldf, lda, wq_v, lq_v, lup_v, ldnT_v, lo_p, lq_p,
                   wo_v, up_v, dn_v, wo_s, up_s, dn_s, obq, oblq, obu, oblu,
                   sy, ry, sx, rx, sc, rc, sd, rd, ss, rs_, loc, own):
    k = pl.program_id(0)
    x, core, mp = (lax.axis_index(a) for a in ("x", "core", "mp"))
    Y, X, C = {"mp": 1 - mp}, {"x": 1 - x}, {"core": 1 - core}
    q_me = 2 * x + core
    q_x = 2 * (1 - x) + core

    def cut(ref, q, n, sub, nsub):
        m = n // 4 // nsub
        return ref.at[pl.ds(pl.multiple_of(q * (n // 4) + sub * m, 16), m), :]

    def piece(i, q, mine):
        if i < 3:
            return cut((a_wq if mine else wq_v).at[i], q, 768, 0, 1)
        if i == 3:
            return (a_lq if mine else lq_v).at[:, pl.ds(pl.multiple_of(q * 48, 16), 48), :]
        if i == 4:
            return cut(a_wo if mine else wo_v, q, 384, 0, 1)
        if i == 5:
            return cut(a_lup if mine else lup_v, q, 192, 0, 1)
        if i == 6:
            return cut(a_ldnT if mine else ldnT_v, q, 192, 0, 1)
        if i < 11:
            return cut(a_up if mine else up_v, q, 768, i - 7, 4)
        return cut(a_dn if mine else dn_v, q, 1536, i - 11, 4)

    def over_y(i):
        return remote(piece(i, q_me, True), piece(i, q_me, False), sy.at[i], ry.at[i], Y)

    def over_x(i):
        return remote(piece(i, q_me, False), piece(i, q_me, False), sx.at[i], rx.at[i], X)

    def over_core(i):
        return remote(piece(i, q_me, False), piece(i, q_me, False), sc.at[i], rc.at[i], C)

    def over_core2(i):
        return remote(piece(i, q_x, False), piece(i, q_x, False), sd.at[i], rd.at[i], C)

    def arrived(i):
        over_core(i).wait_recv()
        over_core2(i).wait_recv()

    def small():
        pairs = ((bq, obq), (blq, oblq), (bu, obu), (blu, oblu), (lo, lo_p.at[1, 0:96]))
        return [remote(a, b, ss.at[i], rs_.at[i], Y) for i, (a, b) in enumerate(pairs)]

    def keep(i):
        a, b = ((wq_v, o_wq), (wo_v, o_wo), (up_v, o_up), (dn_v, o_dn))[i]
        return pltpu.make_async_copy(a, b, loc.at[i])

    def load_own():
        return [pltpu.make_async_copy(a, b, own.at[i]) for i, (a, b) in enumerate(
            ((a_wo, wo_s), (a_up, up_s), (a_dn, dn_s)))]

    @pl.when(k == 0)
    def _():
        lo_p[...] = jnp.zeros_like(lo_p)
        bar = pltpu.get_barrier_semaphore()
        for who in (C, Y, X):
            pl.semaphore_signal(bar, inc=1, device_id=who, device_id_type=MESH)
        pl.semaphore_wait(bar, 3)
        for c in small():
            c.start()

    def slot(step, s):
        @pl.when(k == step)
        def _():
            for i in range(PIECES):
                if START[i] == s:
                    over_y(i).start()
            for i in range(PIECES):
                if RELAY[i] == s:
                    over_y(i).wait_recv()
                    over_x(i).start()
                    over_core(i).start()
            for i in range(PIECES):
                if AHEAD[i] == s:
                    over_x(i).wait_recv()
                    over_core2(i).start()

    for st in range(4):
        slot(st, 3 * st)

    @pl.when(k == 0)
    def _():
        for c in load_own():
            c.start()
        lq_p[...] = jnp.zeros_like(lq_p)
        lo_p[0, 0:96, :] = lo[...]
        for c in range(3):
            lq_p[0, c, :, 0:96] = lq[c]
        lsums[...] = jnp.zeros_like(lsums)
        lbsum[...] = jnp.zeros_like(lbsum)

    @pl.when(k == 2)
    def _():
        for c in small():
            c.wait_recv()
        for i in range(4):
            arrived(i)
        for c in range(3):
            lq_p[1, c, :, 0:96] = lq_v[c]
        keep(0).start()

    @pl.when(k < 4)
    def _():
        hf = k // 2
        page = k % 2

        def project(w, b, lb):
            n = cnt[page]
            lane = lax.broadcasted_iota(jnp.int32, (SEQ, 128), 1)
            row = lax.broadcasted_iota(jnp.int32, (SEQ, 128), 0)
            for c in range(3):
                r = dot(xt[...], w[c])
                s = dot(xl_s[page], lq_p[hf, c])
                if c != 1:
                    r = r + b[c // 2:c // 2 + 1]
                    s = s + jnp.concatenate([lb[c // 2:c // 2 + 1], jnp.zeros((1, 32), f32)], axis=1)
                if c == 0:
                    r = r * 0.125
                    s = jnp.where(lane == 96, 1.0, s * 0.25)
                if c == 1:
                    s = jnp.where((lane == 96) & (row >= n), -1e30, s)
                for p in range(3):
                    qkvt[0, c, p] = r[:, 128 * p:128 * p + 128].astype(bf16)
                qkvl[0, c] = s.astype(bf16)

        @pl.when(hf == 0)
        def _():
            xl_s[page] = xlT[...].T
            project(wq, bq, blq)

        @pl.when(hf == 1)
        def _():
            project(wq_v, obq, oblq)

        rows = pl.ds(pl.multiple_of(page * SEQ, SEQ), SEQ)
        vlT = qkvl[0, 2].T
        for p in range(3):
            if p > 0:
                for st in range(4):
                    slot(st, 3 * st + p)
            qc = jnp.concatenate([qkvt[0, 0, p], qkvl[0, 0]], axis=1)
            kc = jnp.concatenate([qkvt[0, 1, p], qkvl[0, 1]], axis=1)
            vtT = qkvt[0, 2, p].T
            for hh in range(2):
                h = 2 * p + hh
                mk = head_masks(h)[1]
                S = dot_nt(jnp.where(mk, kc, jnp.zeros_like(kc)), qc)
                m = jnp.max(S, axis=0, keepdims=True)
                e = jnp.exp(S - m)
                l = colsum(e)
                vT = jnp.concatenate([vtT[64 * hh:64 * hh + 64], vlT[16 * h:16 * h + 16]], axis=0)
                o = dot(vT, e.astype(bf16)) * (1.0 / l)
                cT[64 * hh:64 * hh + 64, :] = o[:64]
                clT[16 * h:16 * h + 16, :] = o[64:]
                lse_o[0, 0, h:h + 1, :] = m + jnp.log(l)
            cv = cT[...].T.astype(bf16)
            ctxt[0, :, 128 * p:128 * p + 128] = cv
            ctx_s[hf, rows, 128 * p:128 * p + 128] = cv
        clT[96:, :] = jnp.zeros((32, SEQ), f32)
        ctl[hf, rows, :] = clT[...].T.astype(bf16)
        lse_o[0, 0, 6:8, :] = jnp.zeros((2, SEQ), f32)

    slot(4, 12)
    slot(5, 14)

    @pl.when(k == 4)
    def _():
        arrived(5)
        arrived(6)

    @pl.when((k == 4) | (k == 5))
    def _():
        page = k - 4
        rows = pl.ds(pl.multiple_of(page * SEQ, SEQ), SEQ)
        ups, dns, bs_ = (lup, lup_v), (ldnT, ldnT_v), (blu, oblu)

        def hook():
            slot(4, 13)
            slot(5, 15)

        n1, rstd1, h1b, o, dr2, (s_g2, s_s2, s_r2) = forward_math(
            xl_s[page].astype(f32), ctl[0, rows, :], ctl[1, rows, :], lo_p[0], lo_p[1], lambda h, c: ups[h][...],
            lambda a, h, c: dot_nt(a, dns[h][...]), lambda h, c: row_of(bs_[h], 0, 384), lgains[...], lshifts[...],
            lcotT[...].T.astype(f32), lact.at[:, rows, :], lgp, 1, 384, hook)
        outT[...] = o.T.astype(bf16)
        df = dr2.astype(bf16)
        dh1 = dr2
        for h in range(2):
            dp = (dot(df, dns[h][...]) * lgp[h]).astype(bf16)
            ldpre[h, rows, :] = dp
            lbsum[h] += colsum(dp.astype(f32))
            dh1 = dh1 + dot_nt(dp, ups[h][...])
        d1 = norm_back(dh1 * lgains[0:1], n1, rstd1)
        ldr1[...] = d1
        db = d1.astype(bf16)
        lh1[rows, :] = h1b
        ldf[rows, :] = df
        lda[rows, :] = db
        for h in range(2):
            dcl[h] = dot_nt(db, lo_p[h]).astype(bf16)
        lsums[...] += jnp.concatenate([colsum(dh1 * n1), s_g2, colsum(dh1), s_s2, colsum(d1), s_r2,
                                       jnp.zeros((2, 192), f32)], axis=0)

    @pl.when(k == 5)
    def _():
        hT = lh1[...].T
        fT = ldf[...].T
        aT = lda[...].T
        for h in range(2):
            lay1[h] = dot(hT, ldpre[h])
            lay2[h, :, 0:384] = dot(fT, lact[h])
            lay2[h, :, 384:512] = dot(aT, ctl[h])
            for c in range(3):
                lqp[h, c] = lq_p[h, c]

    slot(TEXT, 16)

    @pl.when(k == TEXT)
    def _():
        for c in load_own():
            c.wait()
        arrived(4)
        sums[...] = jnp.zeros_like(sums)

    @pl.when(k >= TEXT)
    def _():
        rows = pl.ds(pl.multiple_of((k - TEXT) * 256, 256), 256)
        ups, dns, bs_ = (up_s, up_v), (dn_s, dn_v), (bu, obu)

        def hook():
            slot(TEXT, 17)

            @pl.when(k == TEXT)
            def _():
                for i in range(7, PIECES):
                    arrived(i)
                for i in range(1, 4):
                    keep(i).start()

        n1, rstd1, h1b, o, dr2, (s_g2, s_s2, s_r2) = forward_math(
            x2[...].astype(f32), ctx_s[0, rows, :], ctx_s[1, rows, :], wo_s[...], wo_v[...], lambda h, c: ups[h][:, c],
            lambda a, h, c: dot(a, dns[h][c, :]), lambda h, c: row_of(bs_[h], c.start, 768), gains[...], shifts[...],
            cot[...].astype(f32), act, gp, 2, 768, hook)
        out[...] = o.astype(bf16)
        h1T[...] = h1b.T
        dfo[...] = dr2.astype(bf16)
        dr2o[...] = dr2
        n1o[...] = n1.astype(bf16)
        rso[...] = jnp.broadcast_to(rstd1, (256, 128))
        sums[...] += jnp.concatenate([s_g2, s_s2, s_r2, jnp.zeros((5, 768), f32)], axis=0)

    @pl.when(k == FWD_STEPS - 1)
    def _():
        for i in range(PIECES):
            over_y(i).wait_send()
            over_x(i).wait_send()
            over_core(i).wait_send()
            over_core2(i).wait_send()
        for c in small():
            c.wait_send()
        for i in range(4):
            keep(i).wait()


def forward(cnt, xt, xlT, wq, lq, wo, lo, lup, ldnT, up, dn, bq, blq, bu, blu, lgains, lshifts, lcotT, gains, shifts, cot):
    T = xt.shape[0]
    n = T // SEQ
    hf = lambda k: clip(k, 0, 3) // 2
    pg = lambda k: clip(k, 0, 3) % 2
    lp = lambda k: clip(k - 4, 0, 1)
    tb = lambda k: clip(k - TEXT, 0, 3)
    anyspec = pl.BlockSpec(memory_space=pl.ANY)
    const = lambda s: pl.BlockSpec(s, lambda k, *_: (0,) * len(s))
    V = pltpu.VMEM
    D = pltpu.SemaphoreType.DMA
    sds = jax.ShapeDtypeStruct
    trow = pl.BlockSpec((256, 768), lambda k, *_: (tb(k), 0))
    trow3 = pl.BlockSpec((2, 256, 1536), lambda k, *_: (0, tb(k), 0))
    lcol = pl.BlockSpec((192, SEQ), lambda k, *_: (0, lp(k)))
    return pl.pallas_call(
        forward_kernel,
        grid_spec=pltpu.PrefetchScalarGridSpec(
            num_scalar_prefetch=1, grid=(FWD_STEPS,),
            in_specs=[pl.BlockSpec((SEQ, 768), lambda k, *_: (pg(k), 0)),
                      pl.BlockSpec((192, SEQ), lambda k, *_: (0, pg(k)))]
            + [whole(a) for a in (wq, lq, lo, lup, ldnT, bq, blq, bu, blu, lgains, lshifts)]
            + [lcol, trow, whole(gains), whole(shifts), trow] + [anyspec] * 7,
            out_specs=[pl.BlockSpec((1, 3, 3, SEQ, 128), lambda k, *_: (hf(k), 0, 0, pg(k), 0)),
                       pl.BlockSpec((1, 3, SEQ, 128), lambda k, *_: (hf(k), 0, pg(k), 0)),
                       pl.BlockSpec((1, 1, 8, SEQ), lambda k, *_: (hf(k), pg(k), 0, 0)),
                       pl.BlockSpec((1, SEQ, 384), lambda k, *_: (hf(k), pg(k), 0)),
                       lcol, pl.BlockSpec((SEQ, 192), lambda k, *_: (lp(k), 0)),
                       pl.BlockSpec((2, SEQ, 128), lambda k, *_: (0, lp(k), 0)),
                       const((2, 192, 384)), const((2, 192, 512)), const((8, 192)), const((2, 1, 384)),
                       const((2, 3, 192, 128)),
                       trow, trow3, trow3, pl.BlockSpec((768, 256), lambda k, *_: (0, tb(k))), trow, trow, trow,
                       pl.BlockSpec((256, 128), lambda k, *_: (tb(k), 0)), const((8, 768)),
                       anyspec, anyspec, anyspec, anyspec],
            scratch_shapes=[
                V((128, SEQ), f32), V((128, SEQ), f32), V((2, T, 384), bf16), V((2, T, 128), bf16),
                V((n, SEQ, 192), bf16), V((2, T, 384), bf16), V((2, SEQ, 384), f32), V((2, T, 384), bf16),
                V((T, 192), bf16), V((T, 192), bf16), V((T, 192), bf16),
                V((3, 768, 384), bf16), V((3, 192, 96), bf16), V((192, 384), bf16), V((192, 384), bf16),
                V((2, 128, 192), bf16), V((2, 3, 192, 128), bf16),
                V((384, 768), bf16), V((768, 1536), bf16), V((1536, 768), bf16),
                V((384, 768), bf16), V((768, 1536), bf16), V((1536, 768), bf16),
                V((2, 384), f32), V((2, 96), f32), V((12, 128), f32), V((3, 128), f32)]
            + [D((PIECES,))] * 8 + [D((5,)), D((5,)), D((4,)), D((3,))]),
        out_shape=[sds((2, 3, 3, T, 128), bf16), sds((2, 3, T, 128), bf16), sds((2, n, 8, SEQ), f32),
                   sds((2, T, 384), bf16), sds((192, T), bf16), sds((T, 192), f32), sds((2, T, 128), bf16),
                   sds((2, 192, 384), f32), sds((2, 192, 512), f32), sds((8, 192), f32), sds((2, 1, 384), f32),
                   sds((2, 3, 192, 128), bf16),
                   sds((T, 768), bf16), sds((2, T, 1536), bf16), sds((2, T, 1536), bf16), sds((768, T), bf16),
                   sds((T, 768), bf16), sds((T, 768), f32), sds((T, 768), bf16), sds((T, 128), f32), sds((8, 768), f32),
                   sds((3, 768, 384), bf16), sds((384, 768), bf16), sds((768, 1536), bf16), sds((1536, 768), bf16)],
        compiler_params=pltpu.CompilerParams(collective_id=1, has_side_effects=True, vmem_limit_bytes=62 << 20),
        name="forward",
    )(cnt, xt, xlT, wq, lq, lo, lup, ldnT, bq, blq, bu, blu, lgains, lshifts, lcotT, xt, gains, shifts, cot,
      wq, lq, wo, lup, ldnT, up, dn)


FEED = 12
ATT = FEED + 12
GRADS = ATT + 8
BWD_STEPS = GRADS + 7


def n_sent(k):
    return jnp.where(k < ATT, clip(k + 1, 0, FEED), FEED + clip(k - ATT + 1, 0, N_CHUNK - FEED))


def n_met(k):
    return jnp.where(k < ATT + 1, clip(((k - 3) * 4) // 7, 0, FEED), FEED + clip(k - ATT - 1, 0, N_CHUNK - FEED))


def backward_kernel(h1T, gp, act, df, dno, dnp, upo, upp, qkvt, qkvl, lse, xblk, n1, rs1, gains, dcl, ldr1, wout, woutp,
                    wq, wqp, wql, ctx, xlT, lay1, lay2, sums, lsums, lbsum, dr2,
                    res, gx, gxlT,
                    dh1, dab, dpre, bsum, sums1, DQ, DQL, dct_s, klT_s, avl, akl, dqT, dqlT, small,
                    P, RC, RY, RX, RZ, sends, rA, rB, rC, rD, rE, rF, rH, loc, ini):
    k = pl.program_id(0)
    z, x, core, mp = (lax.axis_index(a) for a in ("z", "x", "core", "mp"))

    @pl.when(k == 0)
    def _():
        pltpu.make_async_copy(dr2, dh1, ini).start()
        bar = pltpu.get_barrier_semaphore()
        for who in ({"core": 1 - core}, {"mp": 1 - mp}, {"x": 1 - x}):
            pl.semaphore_signal(bar, inc=1, device_id=who, device_id_type=MESH)
        for d in range(1, 4):
            pl.semaphore_signal(bar, inc=1, device_id={"z": (z + d) % 4}, device_id_type=MESH)
        pl.semaphore_wait(bar, 6)

    made = n_sent(k) - 1

    def put(o, t):
        t = t.astype(bf16).reshape(2, 2, 4, 16, WIDE)
        P[made % 2, 0, o] = t[0]
        P[made % 2, 1, o] = t[1]

    dns, ups = (dno, dnp), (upo, upp)

    @pl.when((k < FEED) & (k % 2 == 0))
    def _():
        b = k // 2
        for h in range(2):
            dp = (dot_nt(df[...], dns[h][...]) * gp[h].astype(f32)).astype(bf16)
            dpre[h] = dp
            bsum[h, pl.ds(b, 1), :] = colsum(dp.astype(f32))
            t = dot(h1T[...], dp)
            put(1 - h, jnp.concatenate([t[0:256], t[256:512], t[512:768]], axis=1))

    @pl.when((k < FEED) & (k % 2 == 1))
    def _():
        for h in range(2):
            put(1 - h, dot_tn(act[h], df[...]))

    cat3 = lambda h, c: jnp.concatenate([DQ[h, c, 0], DQ[h, c, 1], DQ[h, c, 2]], axis=1)

    @pl.when((k >= ATT) & (k < ATT + 3))
    def _():
        xT = xblk[...].T
        for h in range(2):
            put(1 - h, jnp.concatenate([dot(xT, cat3(h, 0)), dot(xT, cat3(h, 1))], axis=1))

    @pl.when((k >= ATT + 3) & (k < ATT + 6))
    def _():
        xT = xblk[...].T
        dT = dab[k - ATT - 3].T
        for h in range(2):
            put(1 - h, jnp.concatenate([dot(xT, cat3(h, 2)), dot(dT, ctx[h])], axis=1))

    @pl.when(k == ATT + 6)
    def _():
        xT = xlT[...]
        for h in range(2):
            t = jnp.concatenate([dot(xT, DQL[h, 0]), dot(xT, DQL[h, 1]), dot(xT, DQL[h, 2]), lay1[h]], axis=1)
            small[...] = jnp.zeros_like(small)
            small[0:1, :] = sums1[0:1, :]
            small[1:2, :] = sums[0:1, :]
            small[2:3, :] = sums1[1:2, :]
            small[3:4, :] = sums[1:2, :]
            small[4:5, :] = sums1[2:3, :]
            small[5:6, :] = sums[2:3, :]
            small[6:12, 0:192] = lsums[0:6, :]
            for i, c in enumerate((0, 2)):
                for p in range(3):
                    at = 384 * i + 128 * p
                    small[12:13, at:at + 128] = colsum(DQ[h, c, p].astype(f32))
                small[13:14, 128 * i:128 * i + 128] = colsum(DQL[h, c].astype(f32))
            for b in range(6):
                small[14 + b // 3:15 + b // 3, 256 * (b % 3):256 * (b % 3) + 256] = bsum[h, b:b + 1, :]
            small[16:17, 0:384] = lbsum[h]
            put(1 - h, jnp.concatenate([t, small[...]], axis=0))

    @pl.when(k == ATT + 7)
    def _():
        for h in range(2):
            t = jnp.concatenate([lay2[h], jnp.zeros((192, 256), f32)], axis=1)
            put(1 - h, jnp.concatenate([t, jnp.zeros((64, WIDE), f32)], axis=0))

    def cA(j):
        return remote(P.at[j % 2, 1 - core], RC.at[j], sends.at[0, j], rA.at[j], {"core": 1 - core})

    def cB(j):
        return remote(RC.at[j, 0], RY.at[j], sends.at[1, j], rB.at[j], {"mp": 1 - mp})

    def cC(j):
        return remote(RY.at[j, 1 - x], RX.at[j], sends.at[2, j], rC.at[j], {"x": 1 - x})

    def cD(j, d):
        t = (z + d) % 4
        return remote(RX.at[j, t], RZ.at[j, 3 - d], sends.at[2 + d, j], rD.at[j], {"z": t})

    def cE(j, d):
        return remote(RX.at[j, z], res.at[j, core, x, z], sends.at[5 + d, j], rE.at[j], {"z": (z + d) % 4})

    def cF(j):
        return remote(res.at[j, core, x], res.at[j, core, x], sends.at[9, j], rF.at[j], {"x": 1 - x})

    def cH(j):
        return remote(res.at[j, core], res.at[j, core], sends.at[10, j], rH.at[j], {"core": 1 - core})

    def stage(count, lag):
        now, before = count(k - lag), count(k - lag - 1)
        return now - 1, now > before

    j0, live0 = stage(n_sent, 0)

    @pl.when(live0)
    def _():
        cA(j0).start()

    j1, live1 = stage(n_sent, 1)

    @pl.when(live1)
    def _():
        j = j1
        cA(j).wait_recv()
        for i in range(2):
            RC[j, i] = (RC[j, i].astype(f32) + P[j % 2, core, i].astype(f32)).astype(bf16)
        cB(j).start()
        cA(j).wait_send()

    @pl.when((k < FEED) & (k % 2 == 1))
    def _():
        @pl.when(k == 1)
        def _():
            pltpu.make_async_copy(dr2, dh1, ini).wait()

        for r in range(2):
            rs = slice(512 * r, 512 * r + 512)
            dh1[rs, :] = dh1[rs, :] + dot_nt(dpre[0, rs, :], upo[...]) + dot_nt(dpre[1, rs, :], upp[...])

    @pl.when(k == FEED)
    def _():
        s1 = s2 = s3 = None
        for r in range(4):
            rs = slice(256 * r, 256 * r + 256)
            g = dh1[rs, :]
            n = n1[rs, :].astype(f32)
            d = norm_back(g * gains[0:1], n, rs1[rs, 0:1])
            dh1[rs, :] = d
            db = d.astype(bf16)
            for i in range(3):
                dab[i, rs, :] = db[:, 256 * i:256 * i + 256]
            t1, t2, t3 = colsum(g * n), colsum(g), colsum(d)
            s1, s2, s3 = (t1, t2, t3) if s1 is None else (s1 + t1, s2 + t2, s3 + t3)
        sums1[...] = jnp.concatenate([s1, s2, s3, jnp.zeros((5, WIDE), f32)], axis=0)

    @pl.when((k >= FEED) & (k < ATT))
    def _():
        a = k - FEED
        hf = 1 - a // 6
        page = (a % 6) // 3
        pair = a % 3
        rs = pl.ds(pl.multiple_of(page * SEQ, SEQ), SEQ)

        @pl.when(pair == 0)
        def _():
            da = jnp.concatenate([dab[0, rs, :], dab[1, rs, :], dab[2, rs, :]], axis=1)
            for h, w in enumerate((wout, woutp)):
                @pl.when(hf == h)
                def _(w=w):
                    dct = dot_nt(da, w[...]).astype(bf16)
                    for p in range(3):
                        dct_s[p] = dct[:, 128 * p:128 * p + 128]

            klT_s[...] = qkvl[0, 1].T
            avl[...] = jnp.zeros_like(avl)
            akl[...] = jnp.zeros_like(akl)
            dqlT[...] = jnp.zeros_like(dqlT)

        qc = jnp.concatenate([qkvt[0, 0, 0], qkvl[0, 0]], axis=1)
        kc = jnp.concatenate([qkvt[0, 1, 0], qkvl[0, 1]], axis=1)
        vc = jnp.concatenate([qkvt[0, 2, 0], qkvl[0, 2]], axis=1)
        dc = jnp.concatenate([dct_s[pair], dcl[0]], axis=1)
        ktT = qkvt[0, 1, 0].T
        zero = jnp.zeros_like(kc)
        av = ak = None
        for hh in range(2):
            h = 2 * pair + hh
            lane = lax.broadcasted_iota(jnp.int32, (1, 256), 1)
            mv = ((lane >= 64 * hh) & (lane < 64 * hh + 64)) | ((lane >= 128 + 16 * h) & (lane < 144 + 16 * h))
            mk = mv | (lane == 224)
            E = jnp.exp(dot_nt(jnp.where(mk, kc, zero), qc) - lse[0, 0, pl.ds(h, 1), :])
            dP = dot_nt(jnp.where(mv, vc, zero), dc)
            X = E * dP
            dS = (X - E * colsum(X)).astype(bf16)
            ov = dot(E.astype(bf16), jnp.where(mv, dc, zero))
            ok = dot(dS, jnp.where(mv, qc, zero))
            av = ov[:, :128] if av is None else av + ov[:, :128]
            ak = ok[:, :128] if ak is None else ak + ok[:, :128]
            avl[...] += ov[:, 128:]
            akl[...] += ok[:, 128:]
            ls = pl.ds(pl.multiple_of(16 * h, 16), 16)
            kT = jnp.concatenate([ktT[64 * hh:64 * hh + 64], klT_s[ls, :]], axis=0)
            oq = dot(kT, dS)
            dqT[64 * hh:64 * hh + 64, :] = oq[:64] * 0.125
            dqlT[ls, :] = oq[64:] * 0.25
        DQ[hf, 0, pair, rs, :] = dqT[...].T.astype(bf16)
        DQ[hf, 1, pair, rs, :] = ak.astype(bf16)
        DQ[hf, 2, pair, rs, :] = av.astype(bf16)

        @pl.when(pair == 2)
        def _():
            DQL[hf, 0, rs, :] = dqlT[...].T.astype(bf16)
            DQL[hf, 1, rs, :] = akl[...].astype(bf16)
            DQL[hf, 2, rs, :] = avl[...].astype(bf16)

    @pl.when((k >= GRADS) & (k < GRADS + 4))
    def _():
        rs = pl.ds(pl.multiple_of((k - GRADS) * 256, 256), 256)
        g = dh1[rs, :]
        gl = ldr1[...]
        for h in range(2):
            for c in range(3):
                g = g + dot_nt(jnp.concatenate([DQ[h, c, p, rs, :] for p in range(3)], axis=1), (wq, wqp)[h][c])
                gl = gl + dot_nt(DQL[h, c, rs, :], wql[h, c])
        gx[...] = g
        gxlT[...] = gl.T

    j2, live2 = stage(n_met, 0)

    @pl.when(live2)
    def _():
        j = j2
        cB(j).wait_recv()
        RY[j] = (RY[j].astype(f32) + RC[j, 1].astype(f32)).astype(bf16)
        cC(j).start()

    j3, live3 = stage(n_met, 1)

    @pl.when(live3)
    def _():
        j = j3
        cC(j).wait_recv()
        RX[j] = (RX[j].astype(f32) + RY[j, x].astype(f32)).astype(bf16)
        for d in range(1, 4):
            cD(j, d).start()

    j4, live4 = stage(n_met, 2)

    @pl.when(live4)
    def _():
        j = j4
        remote(RZ.at[j], RZ.at[j], sends.at[3, j], rD.at[j], {"z": (z + 1) % 4}).wait_recv()
        tot = RX[j, z].astype(f32)
        for d in range(3):
            tot = tot + RZ[j, d].astype(f32)
        RX[j, z] = tot.astype(bf16)
        for d in range(1, 4):
            cE(j, d).start()
        pltpu.make_async_copy(RX.at[j, z], res.at[j, core, x, z], loc.at[j]).start()

    j5, live5 = stage(n_met, 3)

    @pl.when(live5)
    def _():
        j = j5
        remote(res.at[j, core, x, pl.ds(0, 3)], res.at[j, core, x, pl.ds(0, 3)], sends.at[6, j], rE.at[j],
               {"z": (z + 1) % 4}).wait_recv()
        pltpu.make_async_copy(RX.at[j, z], res.at[j, core, x, z], loc.at[j]).wait()
        cF(j).start()

    j6, live6 = stage(n_met, 4)

    @pl.when(live6)
    def _():
        cF(j6).wait_recv()
        cH(j6).start()

    j7, live7 = stage(n_met, 5)

    @pl.when(live7)
    def _():
        j = j7
        cH(j).wait_recv()
        cB(j).wait_send()
        cC(j).wait_send()
        for d in range(1, 4):
            cD(j, d).wait_send()
            cE(j, d).wait_send()
        cF(j).wait_send()
        cH(j).wait_send()


def backward(h1T, gp, act, df, dno, dnp, upo, upp, qkvt, qkvl, lse, x, n1, rs1, gains, dcl, ldr1, wout, woutp, wq, wqp, wql,
             ctx, xlT, lay1, lay2, sums, lsums, lbsum, dr2):
    n = N_CHUNK
    T = x.shape[0]
    blk = lambda k: clip(k, 0, FEED - 1) // 2
    att = lambda k: clip(k - FEED, 0, 11)
    head = lambda k: (1 - att(k) // 6, (att(k) % 6) // 3, att(k) % 3)
    D = pltpu.SemaphoreType.DMA
    V = pltpu.VMEM
    sd = jax.ShapeDtypeStruct
    hid = pl.BlockSpec((2, T, 256), lambda k: (0, 0, blk(k)))
    rowb = pl.BlockSpec((256, WIDE), lambda k: (blk(k), 0))
    colb = pl.BlockSpec((WIDE, 256), lambda k: (0, blk(k)))
    grow = lambda k: clip(k - GRADS, 0, 3)
    in_specs = [
        whole(h1T), hid, hid, whole(df), rowb, rowb, colb, colb,
        pl.BlockSpec((1, 3, 1, SEQ, 128), lambda k: (head(k)[0], 0, head(k)[2], head(k)[1], 0)),
        pl.BlockSpec((1, 3, SEQ, 128), lambda k: (head(k)[0], 0, head(k)[1], 0)),
        pl.BlockSpec((1, 1, 8, SEQ), lambda k: (head(k)[0], head(k)[1], 0, 0)),
        pl.BlockSpec((T, 256), lambda k: (0, clip(k - ATT, 0, 5) % 3)),
        whole(n1), whole(rs1), whole(gains),
        pl.BlockSpec((1, SEQ, 128), lambda k: (head(k)[0], head(k)[1], 0)),
        pl.BlockSpec((256, 192), lambda k: (grow(k), 0)),
    ] + [whole(a) for a in (wout, woutp, wq, wqp, wql, ctx, xlT, lay1, lay2, sums, lsums, lbsum)] + [
        pl.BlockSpec(memory_space=pl.ANY)]
    return pl.pallas_call(
        backward_kernel,
        grid=(BWD_STEPS,),
        in_specs=in_specs,
        out_specs=[pl.BlockSpec(memory_space=pl.ANY),
                   pl.BlockSpec((256, WIDE), lambda k: (grow(k), 0)),
                   pl.BlockSpec((192, 256), lambda k: (0, grow(k)))],
        out_shape=[sd((n, 2, 2, 4, 16, WIDE), bf16), sd((T, WIDE), f32), sd((192, T), f32)],
        scratch_shapes=[
            V((T, WIDE), f32), V((3, T, 256), bf16), V((2, T, 256), bf16), V((2, 8, 256), f32), V((8, WIDE), f32),
            V((2, 3, 3, T, 128), bf16), V((2, 3, T, 128), bf16), V((3, SEQ, 128), bf16),
            V((128, SEQ), bf16), V((SEQ, 128), f32), V((SEQ, 128), f32), V((128, SEQ), f32), V((128, SEQ), f32),
            V((64, WIDE), f32),
            V((2, 2, 2, 2, 4, 16, WIDE), bf16), V((n, 2, 2, 4, 16, WIDE), bf16), V((n, 2, 4, 16, WIDE), bf16),
            V((n, 4, 16, WIDE), bf16), V((n, 3, 16, WIDE), bf16), D((11, n)), D((n,)), D((n,)), D((n,)), D((n,)),
            D((n,)), D((n,)), D((n,)), D((n,)), D],
        compiler_params=pltpu.CompilerParams(collective_id=0, has_side_effects=True, vmem_limit_bytes=63 << 20),
        name="backward",
    )(h1T, gp, act, df, dno, dnp, upo, upp, qkvt, qkvl, lse, x, n1, rs1, gains, dcl, ldr1, wout, woutp, wq, wqp, wql,
      ctx, xlT, lay1, lay2, sums, lsums, lbsum, dr2)


def unpack_kernel(r, up, dn, qkv, out, lqkv, lup, ldnT, lout, qvb, upb, gain, shift, lqvb, lupb, lgain, lshift):
    k = pl.program_id(0)

    @pl.when(k < 6)
    def _():
        for i in range(3):
            up[256 * i:256 * i + 256, :] = r[0:256, 256 * i:256 * i + 256].astype(f32)
        dn[...] = r[256:512, :].astype(f32)

    for j in range(6):
        @pl.when(k == 6 + j // 2)
        def _(j=j):
            rows = slice(256 * (j % 3), 256 * (j % 3) + 256)
            a = r[256 * (j % 2):256 * (j % 2) + 256, :].astype(f32)
            if j < 3:
                qkv[0, rows, :] = a[:, 0:384]
                qkv[1, rows, :] = a[:, 384:768]
            else:
                qkv[2, rows, :] = a[:, 0:384]
                out[:, rows] = a[:, 384:768].T

    @pl.when(k == 9)
    def _():
        for c in range(3):
            lqkv[c] = r[0:192, 128 * c:128 * c + 96].astype(f32)
        lup[...] = r[0:192, 384:768].astype(f32)
        s = r[192:224, :].astype(f32)
        ldnT[...] = r[256:448, 0:384].astype(f32)
        lout[...] = r[256:448, 384:512].astype(f32).T[:96, :]
        gain[...] = s[0:2]
        shift[...] = s[2:6]
        lgain[...] = s[6:8, 0:192]
        lshift[...] = s[8:12, 0:192]
        for i in range(2):
            qvb[i:i + 1, :] = s[12:13, 384 * i:384 * i + 384]
            lqvb[i:i + 1, :] = s[13:14, 128 * i:128 * i + 96]
            for j in range(6):
                upb[6 * i + j:6 * i + j + 1, :] = s[14 + i:15 + i, 128 * j:128 * j + 128]
        for j in range(3):
            lupb[j:j + 1, :] = s[16:17, 128 * j:128 * j + 128]


def unpack(tot):
    const = lambda s: pl.BlockSpec(s, lambda k: (0,) * len(s))
    sd = jax.ShapeDtypeStruct
    shapes = [(768, 1536), (1536, 768), (3, 768, 384), (384, 768), (3, 192, 96), (192, 384), (192, 384), (96, 192),
              (2, 384), (12, 128), (2, 768), (4, 768), (2, 96), (3, 128), (2, 192), (4, 192)]
    specs = [const(s) for s in shapes]
    specs[0] = pl.BlockSpec((768, 256), lambda k: (0, clip(k, 0, 5)))
    specs[1] = pl.BlockSpec((256, 768), lambda k: (clip(k, 0, 5), 0))
    return pl.pallas_call(
        unpack_kernel, grid=(10,),
        in_specs=[pl.BlockSpec((512, 768), lambda k: (k, 0))],
        out_specs=specs, out_shape=[sd(s, f32) for s in shapes],
        compiler_params=pltpu.CompilerParams(vmem_limit_bytes=56 << 20), name="unpack_gradients",
    )(tot)


def body(n_group, text_states, layout_states, box_counts, text_qkv, text_qv_bias, text_out, text_up, text_up_bias,
         text_down, text_gains, text_shifts, layout_qkv, layout_qv_bias, layout_out, layout_up, layout_up_bias,
         layout_down, layout_gains, layout_shifts, cot_text, cot_layout):
    mp = lax.axis_index("mp")
    tq = jnp.transpose(text_qkv, (1, 0, 2))
    lq = jnp.transpose(layout_qkv, (1, 0, 2))
    xlT = layout_states.T
    counts = lax.dynamic_slice_in_dim(box_counts, mp * 2, 2, 0)
    (qkvt, qkvl, lse, ctx, out_lT, ldr1, dcl, lay1, lay2, lsums, lbsum, lqp, out_t, act, gp, h1T, df, dr2, n1, rs1, sums,
     wq, wo, wu, wd) = forward(
        counts, text_states, xlT, tq, lq, text_out, layout_out, layout_up, layout_down.T, text_up, text_down,
        text_qv_bias, layout_qv_bias, text_up_bias.reshape(12, 128), layout_up_bias.reshape(3, 128), layout_gains,
        layout_shifts, cot_layout.T, text_gains, text_shifts, cot_text)
    tot, gx, gxlT = backward(h1T, gp, act, df, text_down, wd, text_up, wu, qkvt, qkvl, lse, text_states, n1, rs1,
                             text_gains, dcl, ldr1, text_out, wo, tq, wq, lqp, ctx, xlT, lay1, lay2, sums, lsums, lbsum,
                             dr2)
    tot = tot.reshape(N_CHUNK * CHUNK, WIDE)
    if n_group > 1:
        tot = lax.psum(tot, "group")
    (g_up, g_dn, g_qkv, g_o, gl_qkv, gl_up, gl_dnT, gl_o, qvb, upb, gain, shift, lqvb, lupb, lgain, lshift) = unpack(tot)
    swap = lambda a: jnp.transpose(a, (1, 0, 2))
    return (out_t, out_lT.T, gx, gxlT.T, swap(g_qkv), qvb, g_o, g_up, upb.reshape(1536), g_dn, gain, shift,
            swap(gl_qkv), lqvb, gl_o, gl_up, lupb.reshape(384), gl_dnT.T, lgain, lshift)


def solution(mesh):
    dp = mesh.shape["dp"]
    n_group = dp // 16
    fine = Mesh(mesh.devices.reshape(n_group, 4, 2, 2, 2), AXES)
    rows = P(AXES, None)
    half2 = P(None, "mp")
    half1 = P("mp", None)
    qkv = P(None, None, "mp")
    rep = P()
    return jax.shard_map(
        functools.partial(body, n_group),
        mesh=fine,
        in_specs=(rows, rows, P(AXES[:4]), qkv, half2, half1, half2, P("mp"), half1, rep, rep,
                  qkv, half2, half1, half2, P("mp"), half1, rep, rep, rows, rows),
        out_specs=(rows, rows, rows, rows, qkv, half2, half1, half2, P("mp"), half1, rep, rep,
                   qkv, half2, half1, half2, P("mp"), half1, rep, rep),
        check_vma=False,
    )
```

```python
import functools

import jax
import jax.numpy as jnp
from jax import lax
from jax.experimental import pallas as pl
from jax.experimental.pallas import tpu as pltpu
from jax.sharding import Mesh, PartitionSpec as P

f32 = jnp.float32
bf16 = jnp.bfloat16
SEQ = 512
NT = (((1,), (1,)), ((), ()))
TN = (((0,), (0,)), ((), ()))
AXES = ("group", "z", "x", "core", "mp")
MESH = pl.DeviceIdType.MESH
WIDE = 768


def dot(a, b):
    return jnp.dot(a, b, preferred_element_type=f32)


def dot_nt(a, b):
    return lax.dot_general(a, b, NT, preferred_element_type=f32)


def dot_tn(a, b):
    return lax.dot_general(a, b, TN, preferred_element_type=f32)


def colsum(v):
    return jnp.sum(v, axis=0, keepdims=True)


def whole(a):
    return pl.BlockSpec(a.shape, lambda *i: (0,) * a.ndim, pipeline_mode=pl.Buffered(1))


GC = [0.11609199498651965, 0.07018864201817518, 0.2621979336040309, -0.22868178430415115, 0.38476147983842124,
      -0.10455825070574547]
GP = 0.28


def gelu_pair(v):
    t = 1.0 / (1.0 + GP * jnp.abs(v))
    g = jnp.exp(v * v * -0.5)
    q = GC[5]
    for c in GC[4::-1]:
        q = q * t + c
    q = q * t * g
    phi = jnp.where(v < 0, q, 1.0 - q)
    return v * phi, phi + v * g * 0.3989422804014327


def norm_stats(r):
    cen = r - jnp.mean(r, -1, keepdims=True)
    rstd = lax.rsqrt(jnp.mean(cen * cen, -1, keepdims=True) + 1e-5)
    return cen * rstd, rstd


def norm_back(e, n, rstd):
    return (e - jnp.mean(e, -1, keepdims=True) - n * jnp.mean(e * n, -1, keepdims=True)) * rstd


def head_masks(h):
    lane = lax.broadcasted_iota(jnp.int32, (1, 256), 1)
    t = (lane >= 64 * (h % 2)) & (lane < 64 * (h % 2) + 64)
    l = (lane >= 128 + 16 * h) & (lane < 128 + 16 * h + 16)
    return t | l, t | l | (lane == 224)


def row_of(b, at, n):
    return jnp.concatenate([b[i:i + 1, :] for i in range(at // 128, (at + n) // 128)], axis=1)


def clip(v, a, b):
    return jnp.minimum(jnp.maximum(v, a), b)


def remote(src, dst, s, r, who):
    return pltpu.make_async_remote_copy(src_ref=src, dst_ref=dst, send_sem=s, recv_sem=r, device_id=who,
                                        device_id_type=MESH)


def second_norm(r2, gains, shifts, ct):
    n2, rstd2 = norm_stats(r2)
    dr2 = norm_back(ct * gains[1:2], n2, rstd2)
    return n2 * gains[1:2] + shifts[1:2], dr2, (colsum(ct * n2), colsum(ct), colsum(dr2))


PIECES = 15
START = [0, 0, 0, 0, 2, 3, 3, 4, 5, 6, 7, 8, 9, 10, 11]
RELAY = [2, 4, 5, 5, 6, 6, 6, 7, 8, 9, 10, 12, 14, 15, 16]
AHEAD = [5, 6, 6, 6, 9, 9, 9, 10, 11, 12, 14, 15, 17, 18, 19]
TEXT = 6
TEXT2 = 10
FWD_STEPS = 14


def forward_kernel(cnt, xt, xlT, wq, lq, lo, lup, ldnT, bq, blq, bu, blu, lgains, lshifts, lcotT, x2, gains, shifts, cot,
                   a_wq, a_lq, a_wo, a_lup, a_ldnT, a_up, a_dn,
                   qkvt, qkvl, lse_o, ctxt, outT, ldr1, dcl, lay1, lay2, lsums, lbsum, lqp,
                   out, act, gp, h1T, dfo, dr2o, n1o, rso, sums, o_wq, o_wo, o_up, o_dn,
                   cT, clT, ctx_s, ctl, xl_s, lact, lgp, ldpre, lh1, ldf, lda, wq_v, lq_v, lup_v, ldnT_v, lo_p, lq_p,
                   wo_v, up_v, dn_v, wo_s, up_s, dn_s, h1_s, r2_s, obq, oblq, obu, oblu,
                   sy, ry, sx, rx, sc, rc, sd, rd, ss, rs_, loc, own):
    k = pl.program_id(0)
    x, core, mp = (lax.axis_index(a) for a in ("x", "core", "mp"))
    Y, X, C = {"mp": 1 - mp}, {"x": 1 - x}, {"core": 1 - core}
    q_me = 2 * x + core
    q_x = 2 * (1 - x) + core

    def cut(ref, q, n, sub, nsub):
        m = n // 4 // nsub
        return ref.at[pl.ds(pl.multiple_of(q * (n // 4) + sub * m, 16), m), :]

    def piece(i, q, mine):
        if i < 3:
            return cut((a_wq if mine else wq_v).at[i], q, 768, 0, 1)
        if i == 3:
            return (a_lq if mine else lq_v).at[:, pl.ds(pl.multiple_of(q * 48, 16), 48), :]
        if i == 4:
            return cut(a_wo if mine else wo_v, q, 384, 0, 1)
        if i == 5:
            return cut(a_lup if mine else lup_v, q, 192, 0, 1)
        if i == 6:
            return cut(a_ldnT if mine else ldnT_v, q, 192, 0, 1)
        if i < 11:
            return cut(a_up if mine else up_v, q, 768, i - 7, 4)
        return cut(a_dn if mine else dn_v, q, 1536, i - 11, 4)

    def over_y(i):
        return remote(piece(i, q_me, True), piece(i, q_me, False), sy.at[i], ry.at[i], Y)

    def over_x(i):
        return remote(piece(i, q_me, False), piece(i, q_me, False), sx.at[i], rx.at[i], X)

    def over_core(i):
        return remote(piece(i, q_me, False), piece(i, q_me, False), sc.at[i], rc.at[i], C)

    def over_core2(i):
        return remote(piece(i, q_x, False), piece(i, q_x, False), sd.at[i], rd.at[i], C)

    def arrived(i):
        over_core(i).wait_recv()
        over_core2(i).wait_recv()

    def small():
        pairs = ((bq, obq), (blq, oblq), (bu, obu), (blu, oblu), (lo, lo_p.at[1, 0:96]))
        return [remote(a, b, ss.at[i], rs_.at[i], Y) for i, (a, b) in enumerate(pairs)]

    def keep(i):
        a, b = ((wq_v, o_wq), (wo_v, o_wo), (up_v, o_up), (dn_v, o_dn))[i]
        return pltpu.make_async_copy(a, b, loc.at[i])

    def load_own():
        return [pltpu.make_async_copy(a, b, own.at[i]) for i, (a, b) in enumerate(
            ((a_wo, wo_s), (a_up, up_s), (a_dn, dn_s)))]

    @pl.when(k == 0)
    def _():
        lo_p[...] = jnp.zeros_like(lo_p)
        bar = pltpu.get_barrier_semaphore()
        for who in (C, Y, X):
            pl.semaphore_signal(bar, inc=1, device_id=who, device_id_type=MESH)
        pl.semaphore_wait(bar, 3)
        for c in small():
            c.start()

    def slot(step, s):
        @pl.when(k == step)
        def _():
            for i in range(PIECES):
                if START[i] == s:
                    over_y(i).start()
            for i in range(PIECES):
                if RELAY[i] == s:
                    over_y(i).wait_recv()
                    over_x(i).start()
                    over_core(i).start()
            for i in range(PIECES):
                if AHEAD[i] == s:
                    over_x(i).wait_recv()
                    over_core2(i).start()

    for st in range(4):
        slot(st, 3 * st)

    @pl.when(k == 0)
    def _():
        for c in load_own():
            c.start()
        lq_p[...] = jnp.zeros_like(lq_p)
        lo_p[0, 0:96, :] = lo[...]
        for c in range(3):
            lq_p[0, c, :, 0:96] = lq[c]
        lsums[...] = jnp.zeros_like(lsums)
        lbsum[...] = jnp.zeros_like(lbsum)

    @pl.when(k == 2)
    def _():
        for c in small():
            c.wait_recv()
        for i in range(4):
            arrived(i)
        for c in range(3):
            lq_p[1, c, :, 0:96] = lq_v[c]
        keep(0).start()

    @pl.when(k < 4)
    def _():
        hf = k // 2
        page = k % 2

        def project(w, b, lb):
            n = cnt[page]
            lane = lax.broadcasted_iota(jnp.int32, (SEQ, 128), 1)
            row = lax.broadcasted_iota(jnp.int32, (SEQ, 128), 0)
            for c in range(3):
                r = dot(xt[...], w[c])
                s = dot(xl_s[page], lq_p[hf, c])
                if c != 1:
                    r = r + b[c // 2:c // 2 + 1]
                    s = s + jnp.concatenate([lb[c // 2:c // 2 + 1], jnp.zeros((1, 32), f32)], axis=1)
                if c == 0:
                    r = r * 0.125
                    s = jnp.where(lane == 96, 1.0, s * 0.25)
                if c == 1:
                    s = jnp.where((lane == 96) & (row >= n), -1e30, s)
                for p in range(3):
                    qkvt[0, c, p] = r[:, 128 * p:128 * p + 128].astype(bf16)
                qkvl[0, c] = s.astype(bf16)

        @pl.when(hf == 0)
        def _():
            xl_s[page] = xlT[...].T
            project(wq, bq, blq)

        @pl.when(hf == 1)
        def _():
            project(wq_v, obq, oblq)

        rows = pl.ds(pl.multiple_of(page * SEQ, SEQ), SEQ)
        vlT = qkvl[0, 2].T
        for p in range(3):
            if p > 0:
                for st in range(4):
                    slot(st, 3 * st + p)
            qc = jnp.concatenate([qkvt[0, 0, p], qkvl[0, 0]], axis=1)
            kc = jnp.concatenate([qkvt[0, 1, p], qkvl[0, 1]], axis=1)
            vtT = qkvt[0, 2, p].T
            for hh in range(2):
                h = 2 * p + hh
                mk = head_masks(h)[1]
                S = dot_nt(jnp.where(mk, kc, jnp.zeros_like(kc)), qc)
                m = jnp.max(S, axis=0, keepdims=True)
                e = jnp.exp(S - m)
                l = colsum(e)
                vT = jnp.concatenate([vtT[64 * hh:64 * hh + 64], vlT[16 * h:16 * h + 16]], axis=0)
                o = dot(vT, e.astype(bf16)) * (1.0 / l)
                cT[64 * hh:64 * hh + 64, :] = o[:64]
                clT[16 * h:16 * h + 16, :] = o[64:]
                lse_o[0, 0, h:h + 1, :] = m + jnp.log(l)
            cv = cT[...].T.astype(bf16)
            ctxt[0, :, 128 * p:128 * p + 128] = cv
            ctx_s[hf, rows, 128 * p:128 * p + 128] = cv
        clT[96:, :] = jnp.zeros((32, SEQ), f32)
        ctl[hf, rows, :] = clT[...].T.astype(bf16)
        lse_o[0, 0, 6:8, :] = jnp.zeros((2, SEQ), f32)

    slot(4, 12)
    slot(5, 14)

    @pl.when(k == 4)
    def _():
        arrived(5)
        arrived(6)

    @pl.when((k == 4) | (k == 5))
    def _():
        page = k - 4
        rows = pl.ds(pl.multiple_of(page * SEQ, SEQ), SEQ)
        ups, dns, bs_ = (lup, lup_v), (ldnT, ldnT_v), (blu, oblu)

        attn = dot(ctl[0, rows, :], lo_p[0]) + dot(ctl[1, rows, :], lo_p[1])
        n1, rstd1 = norm_stats(xl_s[page].astype(f32) + attn + lshifts[2:3])
        h1 = n1 * lgains[0:1] + lshifts[0:1]
        h1b = h1.astype(bf16)
        r2 = h1 + lshifts[3:4]
        for h in range(2):
            if h == 1:
                slot(4, 13)
                slot(5, 15)
            ga, gd = gelu_pair(dot(h1b, ups[h][...]) + row_of(bs_[h], 0, 384))
            ab = ga.astype(bf16)
            lact[h, rows, :] = ab
            lgp[h] = gd
            r2 = r2 + dot_nt(ab, dns[h][...])
        o, dr2, (s_g2, s_s2, s_r2) = second_norm(r2, lgains[...], lshifts[...], lcotT[...].T.astype(f32))
        outT[...] = o.T.astype(bf16)
        df = dr2.astype(bf16)
        dh1 = dr2
        for h in range(2):
            dp = (dot(df, dns[h][...]) * lgp[h]).astype(bf16)
            ldpre[h, rows, :] = dp
            lbsum[h] += colsum(dp.astype(f32))
            dh1 = dh1 + dot_nt(dp, ups[h][...])
        d1 = norm_back(dh1 * lgains[0:1], n1, rstd1)
        ldr1[...] = d1
        db = d1.astype(bf16)
        lh1[rows, :] = h1b
        ldf[rows, :] = df
        lda[rows, :] = db
        for h in range(2):
            dcl[h] = dot_nt(db, lo_p[h]).astype(bf16)
        lsums[...] += jnp.concatenate([colsum(dh1 * n1), s_g2, colsum(dh1), s_s2, colsum(d1), s_r2,
                                       jnp.zeros((2, 192), f32)], axis=0)

    @pl.when(k == 5)
    def _():
        hT = lh1[...].T
        fT = ldf[...].T
        aT = lda[...].T
        for h in range(2):
            lay1[h] = dot(hT, ldpre[h])
            lay2[h, :, 0:384] = dot(fT, lact[h])
            lay2[h, :, 384:512] = dot(aT, ctl[h])
            for c in range(3):
                lqp[h, c] = lq_p[h, c]

    for i in range(4):
        slot(TEXT + i, 16 + i)

    @pl.when(k == TEXT)
    def _():
        for c in load_own():
            c.wait()
        arrived(4)
        sums[...] = jnp.zeros_like(sums)

    def units(h1b, up, dn, b):
        r = None
        for c in range(2):
            cs = slice(768 * c, 768 * c + 768)
            ga, gd = gelu_pair(dot(h1b, up[:, cs]) + row_of(b, 768 * c, 768))
            ab = ga.astype(bf16)
            act[0, :, cs] = ab
            gp[0, :, cs] = gd.astype(bf16)
            t = dot(ab, dn[cs, :])
            r = t if r is None else r + t
        return r

    @pl.when((k >= TEXT) & (k < TEXT2))
    def _():
        rows = pl.ds(pl.multiple_of((k - TEXT) * 256, 256), 256)
        attn = dot(ctx_s[0, rows, :], wo_s[...]) + dot(ctx_s[1, rows, :], wo_v[...])
        n1, rstd1 = norm_stats(x2[...].astype(f32) + attn + shifts[2:3])
        n1o[...] = n1.astype(bf16)
        rso[...] = jnp.broadcast_to(rstd1, (256, 128))
        h1 = n1 * gains[0:1] + shifts[0:1]
        h1b = h1.astype(bf16)
        h1_s[rows, :] = h1b
        h1T[...] = h1b.T
        r2_s[rows, :] = h1 + shifts[3:4] + units(h1b, up_s, dn_s, bu)

    @pl.when(k == TEXT2)
    def _():
        for i in range(7, PIECES):
            arrived(i)
        for i in range(1, 4):
            keep(i).start()

    @pl.when(k >= TEXT2)
    def _():
        rows = pl.ds(pl.multiple_of((k - TEXT2) * 256, 256), 256)
        r2 = r2_s[rows, :] + units(h1_s[rows, :], up_v, dn_v, obu)
        o, dr2, (s_g2, s_s2, s_r2) = second_norm(r2, gains[...], shifts[...], cot[...].astype(f32))
        out[...] = o.astype(bf16)
        dfo[...] = dr2.astype(bf16)
        dr2o[...] = dr2
        sums[...] += jnp.concatenate([s_g2, s_s2, s_r2, jnp.zeros((5, 768), f32)], axis=0)

    @pl.when(k == FWD_STEPS - 1)
    def _():
        for i in range(PIECES):
            over_y(i).wait_send()
            over_x(i).wait_send()
            over_core(i).wait_send()
            over_core2(i).wait_send()
        for c in small():
            c.wait_send()
        for i in range(4):
            keep(i).wait()


def forward(cnt, xt, xlT, wq, lq, wo, lo, lup, ldnT, up, dn, bq, blq, bu, blu, lgains, lshifts, lcotT, gains, shifts, cot):
    T = xt.shape[0]
    n = T // SEQ
    hf = lambda k: clip(k, 0, 3) // 2
    pg = lambda k: clip(k, 0, 3) % 2
    lp = lambda k: clip(k - 4, 0, 1)
    tb = lambda k: clip(k - TEXT, 0, 3)
    anyspec = pl.BlockSpec(memory_space=pl.ANY)
    const = lambda s: pl.BlockSpec(s, lambda k, *_: (0,) * len(s))
    V = pltpu.VMEM
    D = pltpu.SemaphoreType.DMA
    sds = jax.ShapeDtypeStruct
    tb2 = lambda k: clip(k - TEXT2, 0, 3)
    tc = lambda k: clip(k - TEXT, 0, 7)
    trow = pl.BlockSpec((256, 768), lambda k, *_: (tb(k), 0))
    trow2 = pl.BlockSpec((256, 768), lambda k, *_: (tb2(k), 0))
    trow3 = pl.BlockSpec((1, 256, 1536), lambda k, *_: (tc(k) // 4, tc(k) % 4, 0))
    lcol = pl.BlockSpec((192, SEQ), lambda k, *_: (0, lp(k)))
    return pl.pallas_call(
        forward_kernel,
        grid_spec=pltpu.PrefetchScalarGridSpec(
            num_scalar_prefetch=1, grid=(FWD_STEPS,),
            in_specs=[pl.BlockSpec((SEQ, 768), lambda k, *_: (pg(k), 0)),
                      pl.BlockSpec((192, SEQ), lambda k, *_: (0, pg(k)))]
            + [whole(a) for a in (wq, lq, lo, lup, ldnT, bq, blq, bu, blu, lgains, lshifts)]
            + [lcol, trow, whole(gains), whole(shifts), trow2] + [anyspec] * 7,
            out_specs=[pl.BlockSpec((1, 3, 3, SEQ, 128), lambda k, *_: (hf(k), 0, 0, pg(k), 0)),
                       pl.BlockSpec((1, 3, SEQ, 128), lambda k, *_: (hf(k), 0, pg(k), 0)),
                       pl.BlockSpec((1, 1, 8, SEQ), lambda k, *_: (hf(k), pg(k), 0, 0)),
                       pl.BlockSpec((1, SEQ, 384), lambda k, *_: (hf(k), pg(k), 0)),
                       lcol, pl.BlockSpec((SEQ, 192), lambda k, *_: (lp(k), 0)),
                       pl.BlockSpec((2, SEQ, 128), lambda k, *_: (0, lp(k), 0)),
                       const((2, 192, 384)), const((2, 192, 512)), const((8, 192)), const((2, 1, 384)),
                       const((2, 3, 192, 128)),
                       trow2, trow3, trow3, pl.BlockSpec((768, 256), lambda k, *_: (0, tb(k))), trow2, trow2, trow,
                       pl.BlockSpec((256, 128), lambda k, *_: (tb(k), 0)), const((8, 768)),
                       anyspec, anyspec, anyspec, anyspec],
            scratch_shapes=[
                V((128, SEQ), f32), V((128, SEQ), f32), V((2, T, 384), bf16), V((2, T, 128), bf16),
                V((n, SEQ, 192), bf16), V((2, T, 384), bf16), V((2, SEQ, 384), f32), V((2, T, 384), bf16),
                V((T, 192), bf16), V((T, 192), bf16), V((T, 192), bf16),
                V((3, 768, 384), bf16), V((3, 192, 96), bf16), V((192, 384), bf16), V((192, 384), bf16),
                V((2, 128, 192), bf16), V((2, 3, 192, 128), bf16),
                V((384, 768), bf16), V((768, 1536), bf16), V((1536, 768), bf16),
                V((384, 768), bf16), V((768, 1536), bf16), V((1536, 768), bf16),
                V((T, 768), bf16), V((T, 768), f32), V((2, 384), f32), V((2, 96), f32), V((12, 128), f32), V((3, 128), f32)]
            + [D((PIECES,))] * 8 + [D((5,)), D((5,)), D((4,)), D((3,))]),
        out_shape=[sds((2, 3, 3, T, 128), bf16), sds((2, 3, T, 128), bf16), sds((2, n, 8, SEQ), f32),
                   sds((2, T, 384), bf16), sds((192, T), bf16), sds((T, 192), f32), sds((2, T, 128), bf16),
                   sds((2, 192, 384), f32), sds((2, 192, 512), f32), sds((8, 192), f32), sds((2, 1, 384), f32),
                   sds((2, 3, 192, 128), bf16),
                   sds((T, 768), bf16), sds((2, T, 1536), bf16), sds((2, T, 1536), bf16), sds((768, T), bf16),
                   sds((T, 768), bf16), sds((T, 768), f32), sds((T, 768), bf16), sds((T, 128), f32), sds((8, 768), f32),
                   sds((3, 768, 384), bf16), sds((384, 768), bf16), sds((768, 1536), bf16), sds((1536, 768), bf16)],
        compiler_params=pltpu.CompilerParams(collective_id=1, has_side_effects=True, vmem_limit_bytes=62 << 20),
        name="forward",
    )(cnt, xt, xlT, wq, lq, lo, lup, ldnT, bq, blq, bu, blu, lgains, lshifts, lcotT, xt, gains, shifts, cot,
      wq, lq, wo, lup, ldnT, up, dn)


FEED = 6
ATT = FEED + 12
OTHER = ATT - 5
GRADS = ATT + 4
BWD_STEPS = ATT + 12
N_FEED = 6
N_ATT = 8
FEED_STEPS = ((3, 5, 7, 9, 12, 15), (4, 6, 10, 12, 15, 18), (5, 9, 13, 15, 18, 20), (6, 12, 16, 18, 20, 22),
              (8, 15, 18, 20, 22, 24), (10, 17, 19, 21, 23, 25))
ATT_MET = (1, 1, 2, 2, 3, 4, 5, 6)


def by_table(table, k):
    return sum((k >= t).astype(jnp.int32) for t in table)


def feed_made(k):
    return clip(k + 1, 0, N_FEED)


def other_made(k):
    return clip(2 * (k - OTHER + 1), 0, N_ATT)


def own_made(k):
    return clip(2 * (k - ATT + 1), 0, N_ATT)


def each(count, k, run):
    now, before = count(k), count(k - 1)
    for d in (2, 1):
        @pl.when(now - before >= d)
        def _(d=d):
            run(now - d)


class Ring:
    def __init__(self, bufs, where):
        (self.RC, self.RY, self.RX, self.RZ, self.res, self.sends, self.rA, self.rO, self.rB, self.rC, self.rD, self.rE,
         self.rF, self.rH, self.loc) = bufs
        self.z, self.x, self.core, self.mp = where
        self.C = {"core": 1 - self.core}

    def cB(self, j):
        return remote(self.RC.at[j, 0], self.RY.at[j], self.sends.at[1, j], self.rB.at[j], {"mp": 1 - self.mp})

    def cC(self, j):
        return remote(self.RY.at[j, 1 - self.x], self.RX.at[j], self.sends.at[2, j], self.rC.at[j], {"x": 1 - self.x})

    def cD(self, j, d):
        t = (self.z + d) % 4
        return remote(self.RX.at[j, t], self.RZ.at[j, 3 - d], self.sends.at[2 + d, j], self.rD.at[j], {"z": t})

    def place(self, j):
        return self.res.at[j, self.core, self.x]

    def cE(self, j, d):
        t = (self.z + d) % 4
        return remote(self.RX.at[j, self.z], self.place(j).at[self.z], self.sends.at[5 + d, j], self.rE.at[j], {"z": t})

    def cF(self, j):
        return remote(self.place(j), self.place(j), self.sends.at[9, j], self.rF.at[j], {"x": 1 - self.x})

    def cH(self, j):
        return remote(self.res.at[j, self.core], self.res.at[j, self.core], self.sends.at[10, j], self.rH.at[j], self.C)

    def kept(self, j):
        return pltpu.make_async_copy(self.RX.at[j, self.z], self.place(j).at[self.z], self.loc.at[j])

    def add(self, j, i, part):
        self.RC[j, i] = (self.RC[j, i].astype(f32) + part.astype(f32)).astype(bf16)

    def stages(self, k, counts):
        z, x = self.z, self.x

        def meet(j):
            self.cB(j).wait_recv()
            self.RY[j] = (self.RY[j].astype(f32) + self.RC[j, 1].astype(f32)).astype(bf16)
            self.cC(j).start()

        def scatter(j):
            self.cC(j).wait_recv()
            self.RX[j] = (self.RX[j].astype(f32) + self.RY[j, x].astype(f32)).astype(bf16)
            for d in range(1, 4):
                self.cD(j, d).start()

        def gather(j):
            remote(self.RZ.at[j], self.RZ.at[j], self.sends.at[3, j], self.rD.at[j], {"z": (z + 1) % 4}).wait_recv()
            tot = self.RX[j, z].astype(f32)
            for d in range(3):
                tot = tot + self.RZ[j, d].astype(f32)
            self.RX[j, z] = tot.astype(bf16)
            for d in range(1, 4):
                self.cE(j, d).start()
            self.kept(j).start()

        def back_x(j):
            three = self.place(j).at[pl.ds(0, 3)]
            remote(three, three, self.sends.at[6, j], self.rE.at[j], {"z": (z + 1) % 4}).wait_recv()
            self.kept(j).wait()
            self.cF(j).start()

        def back_core(j):
            self.cF(j).wait_recv()
            self.cH(j).start()

        def done(j):
            self.cH(j).wait_recv()
            self.cB(j).wait_send()
            self.cC(j).wait_send()
            for d in range(1, 4):
                self.cD(j, d).wait_send()
                self.cE(j, d).wait_send()
            self.cF(j).wait_send()
            self.cH(j).wait_send()

        for count, run in zip(counts, (meet, scatter, gather, back_x, back_core, done)):
            each(count, k, run)


def backward_kernel(h1T, gp, act, df, dno, dnp, upo, upp, qkvt, qkvl, lse, gains, dcl, ldr1, wql, xlT, lay1, lay2,
                    sums, lsums, lbsum, dr2, a_n1, a_rs1, a_wout, a_woutp, a_wq, a_wqp, a_ctx, a_x,
                    res_f, res_a, gx, gxlT,
                    dh1, n1, rs1, wout, woutp, wq, wqp, ctx, xs, dab, bsum, sums1, DQ, DQL, dct_s, klT_s, avl, akl, dqT, dqlT,
                    small, PF, PO, PW, *ring_refs):
    k = pl.program_id(0)
    z, x, core, mp = (lax.axis_index(a) for a in ("z", "x", "core", "mp"))
    ini = ring_refs[-1]
    feed = Ring(ring_refs[0:4] + (res_f,) + ring_refs[8:18], (z, x, core, mp))
    att = Ring(ring_refs[4:8] + (res_a,) + ring_refs[18:28], (z, x, core, mp))

    def loads(i):
        a, b = ((dr2, dh1), (a_n1, n1), (a_rs1, rs1), (a_wout, wout), (a_woutp, woutp), (a_wq, wq), (a_wqp, wqp),
                (a_ctx, ctx), (a_x, xs))[i]
        return pltpu.make_async_copy(a, b, ini.at[i])

    @pl.when(k == 0)
    def _():
        for i in range(9):
            loads(i).start()
        bar = pltpu.get_barrier_semaphore()
        for who in ({"core": 1 - core}, {"mp": 1 - mp}, {"x": 1 - x}):
            pl.semaphore_signal(bar, inc=1, device_id=who, device_id_type=MESH)
        for d in range(1, 4):
            pl.semaphore_signal(bar, inc=1, device_id={"z": (z + d) % 4}, device_id_type=MESH)
        pl.semaphore_wait(bar, 6)
        loads(0).wait()

    @pl.when(k == FEED)
    def _():
        for i in range(1, 9):
            loads(i).wait()

    def feed_A(j):
        return remote(PF.at[1 - core], feed.RC.at[j], feed.sends.at[0, j], feed.rA.at[j], feed.C)

    def other_A(j):
        return remote(PO.at[j % 2, 1 - core], att.RC.at[j, 0], att.sends.at[0, j], att.rA.at[j], att.C)

    def own_A(j):
        return remote(PW.at[j % 2, 1 - core], att.RC.at[j, 1], att.sends.at[11, j], att.rO.at[j], att.C)

    def feed_B(j):
        feed_A(j).wait_recv()
        for i in range(2):
            feed.add(j, i, PF[core, i])
        feed.cB(j).start()
        feed_A(j).wait_send()

    def other_B(j):
        other_A(j).wait_recv()
        att.add(j, 0, PO[j % 2, core])
        att.cB(j).start()
        other_A(j).wait_send()

    def own_B(j):
        own_A(j).wait_recv()
        att.add(j, 1, PW[j % 2, core])
        own_A(j).wait_send()

    each(feed_made, k - 1, feed_B)
    each(other_made, k - 1, other_B)
    each(own_made, k - 1, own_B)

    def put(h, i, t):
        to = (PW, PO)[h]
        t = t.astype(bf16).reshape(2, 2, 4, 16, WIDE)
        to[i % 2, 0] = t[0]
        to[i % 2, 1] = t[1]

    dns, ups = (dno, dnp), (upo, upp)

    @pl.when(k < FEED)
    def _():
        for h in range(2):
            dp = (dot_nt(df[...], dns[h][...]) * gp[h].astype(f32)).astype(bf16)
            bsum[h, pl.ds(k, 1), :] = colsum(dp.astype(f32))
            t = dot(h1T[...], dp).astype(bf16)
            PF[0, 1 - h] = jnp.concatenate([t[0:256], t[256:512], t[512:768]], axis=1).reshape(2, 4, 32, WIDE)
            PF[1, 1 - h] = dot_tn(act[h], df[...]).astype(bf16).reshape(2, 4, 32, WIDE)
            for r in range(2):
                rs = slice(512 * r, 512 * r + 512)
                dh1[rs, :] = dh1[rs, :] + dot_nt(dp[rs, :], ups[h][...])

    cat3 = lambda h, c: jnp.concatenate([DQ[h, c, 0], DQ[h, c, 1], DQ[h, c, 2]], axis=1)

    def make(h, i):
        if i < 3:
            xT = xs[:, 256 * i:256 * i + 256].T
            put(h, i, jnp.concatenate([dot(xT, cat3(h, 0)), dot(xT, cat3(h, 1))], axis=1))
        elif i < 6:
            xT = xs[:, 256 * i - 768:256 * i - 512].T
            put(h, i, jnp.concatenate([dot(xT, cat3(h, 2)), dot(dab[i - 3].T, ctx[h])], axis=1))
        elif i == 6:
            xT = xlT[...]
            t = jnp.concatenate([dot(xT, DQL[h, 0]), dot(xT, DQL[h, 1]), dot(xT, DQL[h, 2]), lay1[h]], axis=1)
            small[...] = jnp.zeros_like(small)
            small[0:1, :] = sums1[0:1, :]
            small[1:2, :] = sums[0:1, :]
            small[2:3, :] = sums1[1:2, :]
            small[3:4, :] = sums[1:2, :]
            small[4:5, :] = sums1[2:3, :]
            small[5:6, :] = sums[2:3, :]
            small[6:12, 0:192] = lsums[0:6, :]
            for n, c in enumerate((0, 2)):
                for p in range(3):
                    at = 384 * n + 128 * p
                    small[12:13, at:at + 128] = colsum(DQ[h, c, p].astype(f32))
                small[13:14, 128 * n:128 * n + 128] = colsum(DQL[h, c].astype(f32))
            for b in range(6):
                small[14 + b // 3:15 + b // 3, 256 * (b % 3):256 * (b % 3) + 256] = bsum[h, b:b + 1, :]
            small[16:17, 0:384] = lbsum[h]
            put(h, i, jnp.concatenate([t, small[...]], axis=0))
        else:
            t = jnp.concatenate([lay2[h], jnp.zeros((192, 256), f32)], axis=1)
            put(h, i, jnp.concatenate([t, jnp.zeros((64, WIDE), f32)], axis=0))

    for h, at in ((1, OTHER), (0, ATT)):
        for p in range(4):
            @pl.when(k == at + p)
            def _(h=h, p=p):
                make(h, 2 * p)
                make(h, 2 * p + 1)

    each(feed_made, k, lambda j: feed_A(j).start())
    each(other_made, k, lambda j: other_A(j).start())
    each(own_made, k, lambda j: own_A(j).start())

    @pl.when(k == FEED)
    def _():
        s1 = s2 = s3 = None
        for r in range(4):
            rs = slice(256 * r, 256 * r + 256)
            g = dh1[rs, :]
            n = n1[rs, :].astype(f32)
            d = norm_back(g * gains[0:1], n, rs1[rs, 0:1])
            dh1[rs, :] = d
            db = d.astype(bf16)
            for i in range(3):
                dab[i, rs, :] = db[:, 256 * i:256 * i + 256]
            t1, t2, t3 = colsum(g * n), colsum(g), colsum(d)
            s1, s2, s3 = (t1, t2, t3) if s1 is None else (s1 + t1, s2 + t2, s3 + t3)
        sums1[...] = jnp.concatenate([s1, s2, s3, jnp.zeros((5, WIDE), f32)], axis=0)

    @pl.when((k >= FEED) & (k < ATT))
    def _():
        a = k - FEED
        hf = 1 - a // 6
        page = (a % 6) // 3
        pair = a % 3
        rs = pl.ds(pl.multiple_of(page * SEQ, SEQ), SEQ)

        @pl.when(pair == 0)
        def _():
            da = jnp.concatenate([dab[0, rs, :], dab[1, rs, :], dab[2, rs, :]], axis=1)
            for h, w in enumerate((wout, woutp)):
                @pl.when(hf == h)
                def _(w=w):
                    dct = dot_nt(da, w[...]).astype(bf16)
                    for p in range(3):
                        dct_s[p] = dct[:, 128 * p:128 * p + 128]

            klT_s[...] = qkvl[0, 1].T
            avl[...] = jnp.zeros_like(avl)
            akl[...] = jnp.zeros_like(akl)
            dqlT[...] = jnp.zeros_like(dqlT)

        qc = jnp.concatenate([qkvt[0, 0, 0], qkvl[0, 0]], axis=1)
        kc = jnp.concatenate([qkvt[0, 1, 0], qkvl[0, 1]], axis=1)
        vc = jnp.concatenate([qkvt[0, 2, 0], qkvl[0, 2]], axis=1)
        dc = jnp.concatenate([dct_s[pair], dcl[0]], axis=1)
        ktT = qkvt[0, 1, 0].T
        zero = jnp.zeros_like(kc)
        av = ak = None
        for hh in range(2):
            h = 2 * pair + hh
            lane = lax.broadcasted_iota(jnp.int32, (1, 256), 1)
            mv = ((lane >= 64 * hh) & (lane < 64 * hh + 64)) | ((lane >= 128 + 16 * h) & (lane < 144 + 16 * h))
            mk = mv | (lane == 224)
            E = jnp.exp(dot_nt(jnp.where(mk, kc, zero), qc) - lse[0, 0, pl.ds(h, 1), :])
            dP = dot_nt(jnp.where(mv, vc, zero), dc)
            X = E * dP
            dS = (X - E * colsum(X)).astype(bf16)
            ov = dot(E.astype(bf16), jnp.where(mv, dc, zero))
            ok = dot(dS, jnp.where(mv, qc, zero))
            av = ov[:, :128] if av is None else av + ov[:, :128]
            ak = ok[:, :128] if ak is None else ak + ok[:, :128]
            avl[...] += ov[:, 128:]
            akl[...] += ok[:, 128:]
            ls = pl.ds(pl.multiple_of(16 * h, 16), 16)
            kT = jnp.concatenate([ktT[64 * hh:64 * hh + 64], klT_s[ls, :]], axis=0)
            oq = dot(kT, dS)
            dqT[64 * hh:64 * hh + 64, :] = oq[:64] * 0.125
            dqlT[ls, :] = oq[64:] * 0.25
        DQ[hf, 0, pair, rs, :] = dqT[...].T.astype(bf16)
        DQ[hf, 1, pair, rs, :] = ak.astype(bf16)
        DQ[hf, 2, pair, rs, :] = av.astype(bf16)

        @pl.when(pair == 2)
        def _():
            DQL[hf, 0, rs, :] = dqlT[...].T.astype(bf16)
            DQL[hf, 1, rs, :] = akl[...].astype(bf16)
            DQL[hf, 2, rs, :] = avl[...].astype(bf16)

    @pl.when((k >= GRADS) & (k < GRADS + 4))
    def _():
        rs = pl.ds(pl.multiple_of((k - GRADS) * 256, 256), 256)
        g = dh1[rs, :]
        gl = ldr1[...]
        for h in range(2):
            for c in range(3):
                g = g + dot_nt(jnp.concatenate([DQ[h, c, p, rs, :] for p in range(3)], axis=1), (wq, wqp)[h][c])
                gl = gl + dot_nt(DQL[h, c, rs, :], wql[h, c])
        gx[...] = g
        gxlT[...] = gl.T

    feed.stages(k, [functools.partial(by_table, t) for t in FEED_STEPS])
    att.stages(k, [functools.partial(by_table, [ATT + t + lag for t in ATT_MET]) for lag in range(6)])


def backward(h1T, gp, act, df, dno, dnp, upo, upp, qkvt, qkvl, lse, x, n1, rs1, gains, dcl, ldr1, wout, woutp, wq, wqp, wql,
             ctx, xlT, lay1, lay2, sums, lsums, lbsum, dr2):
    T = x.shape[0]
    blk = lambda k: clip(k, 0, FEED - 1)
    att = lambda k: clip(k - FEED, 0, 11)
    head = lambda k: (1 - att(k) // 6, (att(k) % 6) // 3, att(k) % 3)
    D = pltpu.SemaphoreType.DMA
    V = pltpu.VMEM
    sd = jax.ShapeDtypeStruct
    hid = pl.BlockSpec((2, T, 256), lambda k: (0, 0, blk(k)))
    rowb = pl.BlockSpec((256, WIDE), lambda k: (blk(k), 0))
    colb = pl.BlockSpec((WIDE, 256), lambda k: (0, blk(k)))
    grow = lambda k: clip(k - GRADS, 0, 3)
    anyspec = pl.BlockSpec(memory_space=pl.ANY)
    in_specs = [
        whole(h1T), hid, hid, whole(df), rowb, rowb, colb, colb,
        pl.BlockSpec((1, 3, 1, SEQ, 128), lambda k: (head(k)[0], 0, head(k)[2], head(k)[1], 0)),
        pl.BlockSpec((1, 3, SEQ, 128), lambda k: (head(k)[0], 0, head(k)[1], 0)),
        pl.BlockSpec((1, 1, 8, SEQ), lambda k: (head(k)[0], head(k)[1], 0, 0)),
        whole(gains),
        pl.BlockSpec((1, SEQ, 128), lambda k: (head(k)[0], head(k)[1], 0)),
        pl.BlockSpec((256, 192), lambda k: (grow(k), 0)),
    ] + [whole(a) for a in (wql, xlT, lay1, lay2, sums, lsums, lbsum)] + [anyspec] * 9
    bufs = lambda n, r: [V((n, 2, 2, 4, r, WIDE), bf16), V((n, 2, 4, r, WIDE), bf16), V((n, 4, r, WIDE), bf16),
                         V((n, 3, r, WIDE), bf16)]
    sems = lambda n: [D((12, n))] + [D((n,))] * 9
    return pl.pallas_call(
        backward_kernel,
        grid=(BWD_STEPS,),
        in_specs=in_specs,
        out_specs=[anyspec, anyspec,
                   pl.BlockSpec((256, WIDE), lambda k: (grow(k), 0)),
                   pl.BlockSpec((192, 256), lambda k: (0, grow(k)))],
        out_shape=[sd((N_FEED, 2, 2, 4, 32, WIDE), bf16), sd((N_ATT, 2, 2, 4, 16, WIDE), bf16), sd((T, WIDE), f32),
                   sd((192, T), f32)],
        scratch_shapes=[
            V((T, WIDE), f32), V((T, WIDE), bf16), V((T, 128), f32), V((384, WIDE), bf16), V((384, WIDE), bf16),
            V((3, WIDE, 384), bf16), V((3, WIDE, 384), bf16), V((2, T, 384), bf16), V((T, WIDE), bf16),
            V((3, T, 256), bf16), V((2, 8, 256), f32), V((8, WIDE), f32),
            V((2, 3, 3, T, 128), bf16), V((2, 3, T, 128), bf16), V((3, SEQ, 128), bf16),
            V((128, SEQ), bf16), V((SEQ, 128), f32), V((SEQ, 128), f32), V((128, SEQ), f32), V((128, SEQ), f32),
            V((64, WIDE), f32),
            V((2, 2, 2, 4, 32, WIDE), bf16), V((2, 2, 2, 4, 16, WIDE), bf16), V((2, 2, 2, 4, 16, WIDE), bf16)]
        + bufs(N_FEED, 32) + bufs(N_ATT, 16) + sems(N_FEED) + sems(N_ATT) + [D((9,))],
        compiler_params=pltpu.CompilerParams(collective_id=0, has_side_effects=True, vmem_limit_bytes=63 << 20),
        name="backward",
    )(h1T, gp, act, df, dno, dnp, upo, upp, qkvt, qkvl, lse, gains, dcl, ldr1, wql, xlT, lay1, lay2, sums, lsums, lbsum, dr2,
      n1, rs1, wout, woutp, wq, wqp, ctx, x)


def unpack_kernel(rf, r, up, dn, qkv, out, lqkv, lup, ldnT, lout, qvb, upb, gain, shift, lqvb, lupb, lgain, lshift):
    k = pl.program_id(0)

    @pl.when(k < 6)
    def _():
        for i in range(3):
            up[256 * i:256 * i + 256, :] = rf[0:256, 256 * i:256 * i + 256].astype(f32)
        dn[...] = rf[256:512, :].astype(f32)

    for j in range(6):
        @pl.when(k == 6 + j // 2)
        def _(j=j):
            rows = slice(256 * (j % 3), 256 * (j % 3) + 256)
            a = r[256 * (j % 2):256 * (j % 2) + 256, :].astype(f32)
            if j < 3:
                qkv[0, rows, :] = a[:, 0:384]
                qkv[1, rows, :] = a[:, 384:768]
            else:
                qkv[2, rows, :] = a[:, 0:384]
                out[:, rows] = a[:, 384:768].T

    @pl.when(k == 9)
    def _():
        for c in range(3):
            lqkv[c] = r[0:192, 128 * c:128 * c + 96].astype(f32)
        lup[...] = r[0:192, 384:768].astype(f32)
        s = r[192:224, :].astype(f32)
        ldnT[...] = r[256:448, 0:384].astype(f32)
        lout[...] = r[256:448, 384:512].astype(f32).T[:96, :]
        gain[...] = s[0:2]
        shift[...] = s[2:6]
        lgain[...] = s[6:8, 0:192]
        lshift[...] = s[8:12, 0:192]
        for i in range(2):
            qvb[i:i + 1, :] = s[12:13, 384 * i:384 * i + 384]
            lqvb[i:i + 1, :] = s[13:14, 128 * i:128 * i + 96]
            for j in range(6):
                upb[6 * i + j:6 * i + j + 1, :] = s[14 + i:15 + i, 128 * j:128 * j + 128]
        for j in range(3):
            lupb[j:j + 1, :] = s[16:17, 128 * j:128 * j + 128]


def unpack(feed, att):
    const = lambda s: pl.BlockSpec(s, lambda k: (0,) * len(s))
    sd = jax.ShapeDtypeStruct
    shapes = [(768, 1536), (1536, 768), (3, 768, 384), (384, 768), (3, 192, 96), (192, 384), (192, 384), (96, 192),
              (2, 384), (12, 128), (2, 768), (4, 768), (2, 96), (3, 128), (2, 192), (4, 192)]
    specs = [const(s) for s in shapes]
    specs[0] = pl.BlockSpec((768, 256), lambda k: (0, clip(k, 0, 5)))
    specs[1] = pl.BlockSpec((256, 768), lambda k: (clip(k, 0, 5), 0))
    return pl.pallas_call(
        unpack_kernel, grid=(10,),
        in_specs=[pl.BlockSpec((512, 768), lambda k: (clip(k, 0, 5), 0)), pl.BlockSpec((512, 768), lambda k: (clip(k - 6, 0, 3), 0))],
        out_specs=specs, out_shape=[sd(s, f32) for s in shapes],
        compiler_params=pltpu.CompilerParams(vmem_limit_bytes=56 << 20), name="unpack_gradients",
    )(feed, att)


def body(n_group, text_states, layout_states, box_counts, text_qkv, text_qv_bias, text_out, text_up, text_up_bias,
         text_down, text_gains, text_shifts, layout_qkv, layout_qv_bias, layout_out, layout_up, layout_up_bias,
         layout_down, layout_gains, layout_shifts, cot_text, cot_layout):
    mp = lax.axis_index("mp")
    tq = jnp.transpose(text_qkv, (1, 0, 2))
    lq = jnp.transpose(layout_qkv, (1, 0, 2))
    xlT = layout_states.T
    counts = lax.dynamic_slice_in_dim(box_counts, mp * 2, 2, 0)
    (qkvt, qkvl, lse, ctx, out_lT, ldr1, dcl, lay1, lay2, lsums, lbsum, lqp, out_t, act, gp, h1T, df, dr2, n1, rs1, sums,
     wq, wo, wu, wd) = forward(
        counts, text_states, xlT, tq, lq, text_out, layout_out, layout_up, layout_down.T, text_up, text_down,
        text_qv_bias, layout_qv_bias, text_up_bias.reshape(12, 128), layout_up_bias.reshape(3, 128), layout_gains,
        layout_shifts, cot_layout.T, text_gains, text_shifts, cot_text)
    feed, att, gx, gxlT = backward(h1T, gp, act, df, text_down, wd, text_up, wu, qkvt, qkvl, lse, text_states, n1, rs1,
                             text_gains, dcl, ldr1, text_out, wo, tq, wq, lqp, ctx, xlT, lay1, lay2, sums, lsums, lbsum,
                             dr2)
    feed = feed.reshape(N_FEED * 512, WIDE)
    att = att.reshape(N_ATT * 256, WIDE)
    if n_group > 1:
        feed, att = lax.psum((feed, att), "group")
    (g_up, g_dn, g_qkv, g_o, gl_qkv, gl_up, gl_dnT, gl_o, qvb, upb, gain, shift, lqvb, lupb, lgain, lshift) = unpack(feed, att)
    swap = lambda a: jnp.transpose(a, (1, 0, 2))
    return (out_t, out_lT.T, gx, gxlT.T, swap(g_qkv), qvb, g_o, g_up, upb.reshape(1536), g_dn, gain, shift,
            swap(gl_qkv), lqvb, gl_o, gl_up, lupb.reshape(384), gl_dnT.T, lgain, lshift)


def solution(mesh):
    dp = mesh.shape["dp"]
    n_group = dp // 16
    fine = Mesh(mesh.devices.reshape(n_group, 4, 2, 2, 2), AXES)
    rows = P(AXES, None)
    half2 = P(None, "mp")
    half1 = P("mp", None)
    qkv = P(None, None, "mp")
    rep = P()
    return jax.shard_map(
        functools.partial(body, n_group),
        mesh=fine,
        in_specs=(rows, rows, P(AXES[:4]), qkv, half2, half1, half2, P("mp"), half1, rep, rep,
                  qkv, half2, half1, half2, P("mp"), half1, rep, rep, rows, rows),
        out_specs=(rows, rows, rows, rows, qkv, half2, half1, half2, P("mp"), half1, rep, rep,
                   qkv, half2, half1, half2, P("mp"), half1, rep, rep),
        check_vma=False,
    )
```

```python
import functools

import jax
import jax.numpy as jnp
from jax import lax
from jax.experimental import pallas as pl
from jax.experimental.pallas import tpu as pltpu
from jax.sharding import Mesh, PartitionSpec as P

f32 = jnp.float32
bf16 = jnp.bfloat16
SEQ = 512
NT = (((1,), (1,)), ((), ()))
TN = (((0,), (0,)), ((), ()))
AXES = ("group", "z", "x", "core", "mp")
MESH = pl.DeviceIdType.MESH
WIDE = 768


def dot(a, b):
    return jnp.dot(a, b, preferred_element_type=f32)


def dot_nt(a, b):
    return lax.dot_general(a, b, NT, preferred_element_type=f32)


def dot_tn(a, b):
    return lax.dot_general(a, b, TN, preferred_element_type=f32)


def colsum(v):
    return jnp.sum(v, axis=0, keepdims=True)


def whole(a):
    return pl.BlockSpec(a.shape, lambda *i: (0,) * a.ndim, pipeline_mode=pl.Buffered(1))


GC = [0.11609199498651965, 0.07018864201817518, 0.2621979336040309, -0.22868178430415115, 0.38476147983842124,
      -0.10455825070574547]
GP = 0.28


def gelu_pair(v):
    t = 1.0 / (1.0 + GP * jnp.abs(v))
    g = jnp.exp(v * v * -0.5)
    q = GC[5]
    for c in GC[4::-1]:
        q = q * t + c
    q = q * t * g
    phi = jnp.where(v < 0, q, 1.0 - q)
    return v * phi, phi + v * g * 0.3989422804014327


def norm_stats(r):
    cen = r - jnp.mean(r, -1, keepdims=True)
    rstd = lax.rsqrt(jnp.mean(cen * cen, -1, keepdims=True) + 1e-5)
    return cen * rstd, rstd


def norm_back(e, n, rstd):
    return (e - jnp.mean(e, -1, keepdims=True) - n * jnp.mean(e * n, -1, keepdims=True)) * rstd


def head_masks(h):
    lane = lax.broadcasted_iota(jnp.int32, (1, 256), 1)
    t = (lane >= 64 * (h % 2)) & (lane < 64 * (h % 2) + 64)
    l = (lane >= 128 + 16 * h) & (lane < 128 + 16 * h + 16)
    return t | l, t | l | (lane == 224)


def row_of(b, at, n):
    return jnp.concatenate([b[i:i + 1, :] for i in range(at // 128, (at + n) // 128)], axis=1)


def clip(v, a, b):
    return jnp.minimum(jnp.maximum(v, a), b)


def remote(src, dst, s, r, who):
    return pltpu.make_async_remote_copy(src_ref=src, dst_ref=dst, send_sem=s, recv_sem=r, device_id=who,
                                        device_id_type=MESH)


def second_norm(r2, gains, shifts, ct):
    n2, rstd2 = norm_stats(r2)
    dr2 = norm_back(ct * gains[1:2], n2, rstd2)
    return n2 * gains[1:2] + shifts[1:2], dr2, (colsum(ct * n2), colsum(ct), colsum(dr2))


PIECES = 15
START = [0, 0, 0, 0, 2, 3, 3, 4, 5, 6, 7, 8, 9, 10, 11]
RELAY = [2, 4, 5, 5, 6, 6, 6, 7, 8, 9, 10, 12, 14, 15, 16]
AHEAD = [5, 6, 6, 6, 9, 9, 9, 10, 11, 12, 14, 15, 17, 18, 19]
TEXT = 6
TEXT2 = 10
FWD_STEPS = 14


def forward_kernel(cnt, xt, xlT, wq, lq, lo, lup, ldnT, bq, blq, bu, blu, lgains, lshifts, lcotT, x2, gains, shifts, cot,
                   a_wq, a_lq, a_wo, a_lup, a_ldnT, a_up, a_dn,
                   qkvt, qkvl, lse_o, ctxt, outT, ldr1, dcl, lay1, lay2, lsums, lbsum, lqp,
                   out, act, gp, h1T, x_T, dfo, dr2o, n1o, rso, sums, o_wq, o_wo, o_up, o_dn,
                   cT, clT, ctx_s, ctl, xl_s, lact, lgp, ldpre, lh1, ldf, lda, wq_v, lq_v, lup_v, ldnT_v, lo_p, lq_p,
                   wo_v, up_v, dn_v, wo_s, up_s, dn_s, h1_s, r2_s, obq, oblq, obu, oblu,
                   sy, ry, sx, rx, sc, rc, sd, rd, ss, rs_, loc, own):
    k = pl.program_id(0)
    x, core, mp = (lax.axis_index(a) for a in ("x", "core", "mp"))
    Y, X, C = {"mp": 1 - mp}, {"x": 1 - x}, {"core": 1 - core}
    q_me = 2 * x + core
    q_x = 2 * (1 - x) + core

    def cut(ref, q, n, sub, nsub):
        m = n // 4 // nsub
        return ref.at[pl.ds(pl.multiple_of(q * (n // 4) + sub * m, 16), m), :]

    def piece(i, q, mine):
        if i < 3:
            return cut((a_wq if mine else wq_v).at[i], q, 768, 0, 1)
        if i == 3:
            return (a_lq if mine else lq_v).at[:, pl.ds(pl.multiple_of(q * 48, 16), 48), :]
        if i == 4:
            return cut(a_wo if mine else wo_v, q, 384, 0, 1)
        if i == 5:
            return cut(a_lup if mine else lup_v, q, 192, 0, 1)
        if i == 6:
            return cut(a_ldnT if mine else ldnT_v, q, 192, 0, 1)
        if i < 11:
            return cut(a_up if mine else up_v, q, 768, i - 7, 4)
        return cut(a_dn if mine else dn_v, q, 1536, i - 11, 4)

    def over_y(i):
        return remote(piece(i, q_me, True), piece(i, q_me, False), sy.at[i], ry.at[i], Y)

    def over_x(i):
        return remote(piece(i, q_me, False), piece(i, q_me, False), sx.at[i], rx.at[i], X)

    def over_core(i):
        return remote(piece(i, q_me, False), piece(i, q_me, False), sc.at[i], rc.at[i], C)

    def over_core2(i):
        return remote(piece(i, q_x, False), piece(i, q_x, False), sd.at[i], rd.at[i], C)

    def arrived(i):
        over_core(i).wait_recv()
        over_core2(i).wait_recv()

    def small():
        pairs = ((bq, obq), (blq, oblq), (bu, obu), (blu, oblu), (lo, lo_p.at[1, 0:96]))
        return [remote(a, b, ss.at[i], rs_.at[i], Y) for i, (a, b) in enumerate(pairs)]

    def keep(i):
        a, b = ((wq_v, o_wq), (wo_v, o_wo), (up_v, o_up), (dn_v, o_dn))[i]
        return pltpu.make_async_copy(a, b, loc.at[i])

    def load_own():
        return [pltpu.make_async_copy(a, b, own.at[i]) for i, (a, b) in enumerate(
            ((a_wo, wo_s), (a_up, up_s), (a_dn, dn_s)))]

    @pl.when(k == 0)
    def _():
        lo_p[...] = jnp.zeros_like(lo_p)
        bar = pltpu.get_barrier_semaphore()
        for who in (C, Y, X):
            pl.semaphore_signal(bar, inc=1, device_id=who, device_id_type=MESH)
        pl.semaphore_wait(bar, 3)
        for c in small():
            c.start()

    def slot(step, s):
        @pl.when(k == step)
        def _():
            for i in range(PIECES):
                if START[i] == s:
                    over_y(i).start()
            for i in range(PIECES):
                if RELAY[i] == s:
                    over_y(i).wait_recv()
                    over_x(i).start()
                    over_core(i).start()
            for i in range(PIECES):
                if AHEAD[i] == s:
                    over_x(i).wait_recv()
                    over_core2(i).start()

    for st in range(4):
        slot(st, 3 * st)

    @pl.when(k == 0)
    def _():
        for c in load_own():
            c.start()
        lq_p[...] = jnp.zeros_like(lq_p)
        lo_p[0, 0:96, :] = lo[...]
        for c in range(3):
            lq_p[0, c, :, 0:96] = lq[c]
        lsums[...] = jnp.zeros_like(lsums)
        lbsum[...] = jnp.zeros_like(lbsum)

    @pl.when(k == 2)
    def _():
        for c in small():
            c.wait_recv()
        for i in range(4):
            arrived(i)
        for c in range(3):
            lq_p[1, c, :, 0:96] = lq_v[c]
        keep(0).start()

    @pl.when(k < 4)
    def _():
        hf = k // 2
        page = k % 2

        def project(w, b, lb):
            n = cnt[2 * mp + page]
            lane = lax.broadcasted_iota(jnp.int32, (SEQ, 128), 1)
            row = lax.broadcasted_iota(jnp.int32, (SEQ, 128), 0)
            for c in range(3):
                r = dot(xt[...], w[c])
                s = dot(xl_s[page], lq_p[hf, c])
                if c != 1:
                    r = r + b[c // 2:c // 2 + 1]
                    s = s + jnp.concatenate([lb[c // 2:c // 2 + 1], jnp.zeros((1, 32), f32)], axis=1)
                if c == 0:
                    r = r * 0.125
                    s = jnp.where(lane == 96, 1.0, s * 0.25)
                if c == 1:
                    s = jnp.where((lane == 96) & (row >= n), -1e30, s)
                for p in range(3):
                    qkvt[0, c, p] = r[:, 128 * p:128 * p + 128].astype(bf16)
                qkvl[0, c] = s.astype(bf16)

        @pl.when(hf == 0)
        def _():
            xl_s[page] = xlT[...].T
            project(wq, bq, blq)

        @pl.when(hf == 1)
        def _():
            project(wq_v, obq, oblq)

        rows = pl.ds(pl.multiple_of(page * SEQ, SEQ), SEQ)
        vlT = qkvl[0, 2].T
        for p in range(3):
            if p > 0:
                for st in range(4):
                    slot(st, 3 * st + p)
            qc = jnp.concatenate([qkvt[0, 0, p], qkvl[0, 0]], axis=1)
            kc = jnp.concatenate([qkvt[0, 1, p], qkvl[0, 1]], axis=1)
            vtT = qkvt[0, 2, p].T
            for hh in range(2):
                h = 2 * p + hh
                mk = head_masks(h)[1]
                S = dot_nt(jnp.where(mk, kc, jnp.zeros_like(kc)), qc)
                m = jnp.max(S, axis=0, keepdims=True)
                e = jnp.exp(S - m)
                l = colsum(e)
                vT = jnp.concatenate([vtT[64 * hh:64 * hh + 64], vlT[16 * h:16 * h + 16]], axis=0)
                o = dot(vT, e.astype(bf16)) * (1.0 / l)
                cT[64 * hh:64 * hh + 64, :] = o[:64]
                clT[16 * h:16 * h + 16, :] = o[64:]
                lse_o[0, 0, h:h + 1, :] = m + jnp.log(l)
            cv = cT[...].T.astype(bf16)
            ctxt[0, :, 128 * p:128 * p + 128] = cv
            ctx_s[hf, rows, 128 * p:128 * p + 128] = cv
        clT[96:, :] = jnp.zeros((32, SEQ), f32)
        ctl[hf, rows, :] = clT[...].T.astype(bf16)
        lse_o[0, 0, 6:8, :] = jnp.zeros((2, SEQ), f32)

    slot(4, 12)
    slot(5, 14)

    @pl.when(k == 4)
    def _():
        arrived(5)
        arrived(6)

    @pl.when((k == 4) | (k == 5))
    def _():
        page = k - 4
        rows = pl.ds(pl.multiple_of(page * SEQ, SEQ), SEQ)
        ups, dns, bs_ = (lup, lup_v), (ldnT, ldnT_v), (blu, oblu)

        attn = dot(ctl[0, rows, :], lo_p[0]) + dot(ctl[1, rows, :], lo_p[1])
        n1, rstd1 = norm_stats(xl_s[page].astype(f32) + attn + lshifts[2:3])
        h1 = n1 * lgains[0:1] + lshifts[0:1]
        h1b = h1.astype(bf16)
        r2 = h1 + lshifts[3:4]
        for h in range(2):
            if h == 1:
                slot(4, 13)
                slot(5, 15)
            ga, gd = gelu_pair(dot(h1b, ups[h][...]) + row_of(bs_[h], 0, 384))
            ab = ga.astype(bf16)
            lact[h, rows, :] = ab
            lgp[h] = gd
            r2 = r2 + dot_nt(ab, dns[h][...])
        o, dr2, (s_g2, s_s2, s_r2) = second_norm(r2, lgains[...], lshifts[...], lcotT[...].T.astype(f32))
        outT[...] = o.T.astype(bf16)
        df = dr2.astype(bf16)
        dh1 = dr2
        for h in range(2):
            dp = (dot(df, dns[h][...]) * lgp[h]).astype(bf16)
            ldpre[h, rows, :] = dp
            lbsum[h] += colsum(dp.astype(f32))
            dh1 = dh1 + dot_nt(dp, ups[h][...])
        d1 = norm_back(dh1 * lgains[0:1], n1, rstd1)
        ldr1[...] = d1
        db = d1.astype(bf16)
        lh1[rows, :] = h1b
        ldf[rows, :] = df
        lda[rows, :] = db
        for h in range(2):
            dcl[h] = dot_nt(db, lo_p[h]).astype(bf16)
        lsums[...] += jnp.concatenate([colsum(dh1 * n1), s_g2, colsum(dh1), s_s2, colsum(d1), s_r2,
                                       jnp.zeros((2, 192), f32)], axis=0)

    @pl.when(k == 5)
    def _():
        hT = lh1[...].T
        fT = ldf[...].T
        aT = lda[...].T
        for h in range(2):
            lay1[h] = dot(hT, ldpre[h])
            lay2[h, :, 0:384] = dot(fT, lact[h])
            lay2[h, :, 384:512] = dot(aT, ctl[h])
            for c in range(3):
                lqp[h, c] = lq_p[h, c]

    for i in range(4):
        slot(TEXT + i, 16 + i)

    @pl.when(k == TEXT)
    def _():
        for c in load_own():
            c.wait()
        arrived(4)
        sums[...] = jnp.zeros_like(sums)

    def units(h1b, up, dn, b):
        r = None
        for c in range(2):
            cs = slice(768 * c, 768 * c + 768)
            ga, gd = gelu_pair(dot(h1b, up[:, cs]) + row_of(b, 768 * c, 768))
            ab = ga.astype(bf16)
            act[0, :, cs] = ab
            gp[0, :, cs] = gd.astype(bf16)
            t = dot(ab, dn[cs, :])
            r = t if r is None else r + t
        return r

    @pl.when((k >= TEXT) & (k < TEXT2))
    def _():
        rows = pl.ds(pl.multiple_of((k - TEXT) * 256, 256), 256)
        attn = dot(ctx_s[0, rows, :], wo_s[...]) + dot(ctx_s[1, rows, :], wo_v[...])
        n1, rstd1 = norm_stats(x2[...].astype(f32) + attn + shifts[2:3])
        n1o[...] = n1.astype(bf16)
        rso[...] = jnp.broadcast_to(rstd1, (256, 128))
        h1 = n1 * gains[0:1] + shifts[0:1]
        h1b = h1.astype(bf16)
        h1_s[rows, :] = h1b
        h1T[...] = h1b.T
        x_T[...] = x2[...].T
        r2_s[rows, :] = h1 + shifts[3:4] + units(h1b, up_s, dn_s, bu)

    @pl.when(k == TEXT2)
    def _():
        for i in range(7, PIECES):
            arrived(i)
        for i in range(1, 4):
            keep(i).start()

    @pl.when(k >= TEXT2)
    def _():
        rows = pl.ds(pl.multiple_of((k - TEXT2) * 256, 256), 256)
        r2 = r2_s[rows, :] + units(h1_s[rows, :], up_v, dn_v, obu)
        o, dr2, (s_g2, s_s2, s_r2) = second_norm(r2, gains[...], shifts[...], cot[...].astype(f32))
        out[...] = o.astype(bf16)
        dfo[...] = dr2.astype(bf16)
        dr2o[...] = dr2
        sums[...] += jnp.concatenate([s_g2, s_s2, s_r2, jnp.zeros((5, 768), f32)], axis=0)

    @pl.when(k == FWD_STEPS - 1)
    def _():
        for i in range(PIECES):
            over_y(i).wait_send()
            over_x(i).wait_send()
            over_core(i).wait_send()
            over_core2(i).wait_send()
        for c in small():
            c.wait_send()
        for i in range(4):
            keep(i).wait()


def forward(cnt, xt, xlT, wq, lq, wo, lo, lup, ldnT, up, dn, bq, blq, bu, blu, lgains, lshifts, lcotT, gains, shifts, cot):
    T = xt.shape[0]
    n = T // SEQ
    hf = lambda k: clip(k, 0, 3) // 2
    pg = lambda k: clip(k, 0, 3) % 2
    lp = lambda k: clip(k - 4, 0, 1)
    tb = lambda k: clip(k - TEXT, 0, 3)
    anyspec = pl.BlockSpec(memory_space=pl.ANY)
    const = lambda s: pl.BlockSpec(s, lambda k, *_: (0,) * len(s))
    V = pltpu.VMEM
    D = pltpu.SemaphoreType.DMA
    sds = jax.ShapeDtypeStruct
    tb2 = lambda k: clip(k - TEXT2, 0, 3)
    tc = lambda k: clip(k - TEXT, 0, 7)
    trow = pl.BlockSpec((256, 768), lambda k, *_: (tb(k), 0))
    trow2 = pl.BlockSpec((256, 768), lambda k, *_: (tb2(k), 0))
    trow3 = pl.BlockSpec((1, 256, 1536), lambda k, *_: (tc(k) // 4, tc(k) % 4, 0))
    lcol = pl.BlockSpec((192, SEQ), lambda k, *_: (0, lp(k)))
    return pl.pallas_call(
        forward_kernel,
        grid_spec=pltpu.PrefetchScalarGridSpec(
            num_scalar_prefetch=1, grid=(FWD_STEPS,),
            in_specs=[pl.BlockSpec((SEQ, 768), lambda k, *_: (pg(k), 0)),
                      pl.BlockSpec((192, SEQ), lambda k, *_: (0, pg(k)))]
            + [whole(a) for a in (wq, lq, lo, lup, ldnT, bq, blq, bu, blu, lgains, lshifts)]
            + [lcol, trow, whole(gains), whole(shifts), trow2] + [anyspec] * 7,
            out_specs=[pl.BlockSpec((1, 3, 3, SEQ, 128), lambda k, *_: (hf(k), 0, 0, pg(k), 0)),
                       pl.BlockSpec((1, 3, SEQ, 128), lambda k, *_: (hf(k), 0, pg(k), 0)),
                       pl.BlockSpec((1, 1, 8, SEQ), lambda k, *_: (hf(k), pg(k), 0, 0)),
                       pl.BlockSpec((1, SEQ, 384), lambda k, *_: (hf(k), pg(k), 0)),
                       lcol, pl.BlockSpec((SEQ, 192), lambda k, *_: (lp(k), 0)),
                       pl.BlockSpec((2, SEQ, 128), lambda k, *_: (0, lp(k), 0)),
                       const((2, 192, 384)), const((2, 192, 512)), const((8, 192)), const((2, 1, 384)),
                       const((2, 3, 192, 128)),
                       trow2, trow3, trow3, pl.BlockSpec((768, 256), lambda k, *_: (0, tb(k))), pl.BlockSpec((768, 256), lambda k, *_: (0, tb(k))),
                       trow2, trow2, trow,
                       pl.BlockSpec((256, 128), lambda k, *_: (tb(k), 0)), const((8, 768)),
                       anyspec, anyspec, anyspec, anyspec],
            scratch_shapes=[
                V((128, SEQ), f32), V((128, SEQ), f32), V((2, T, 384), bf16), V((2, T, 128), bf16),
                V((n, SEQ, 192), bf16), V((2, T, 384), bf16), V((2, SEQ, 384), f32), V((2, T, 384), bf16),
                V((T, 192), bf16), V((T, 192), bf16), V((T, 192), bf16),
                V((3, 768, 384), bf16), V((3, 192, 96), bf16), V((192, 384), bf16), V((192, 384), bf16),
                V((2, 128, 192), bf16), V((2, 3, 192, 128), bf16),
                V((384, 768), bf16), V((768, 1536), bf16), V((1536, 768), bf16),
                V((384, 768), bf16), V((768, 1536), bf16), V((1536, 768), bf16),
                V((T, 768), bf16), V((T, 768), f32), V((2, 384), f32), V((2, 96), f32), V((12, 128), f32), V((3, 128), f32)]
            + [D((PIECES,))] * 8 + [D((5,)), D((5,)), D((4,)), D((3,))]),
        out_shape=[sds((2, 3, 3, T, 128), bf16), sds((2, 3, T, 128), bf16), sds((2, n, 8, SEQ), f32),
                   sds((2, T, 384), bf16), sds((192, T), bf16), sds((T, 192), f32), sds((2, T, 128), bf16),
                   sds((2, 192, 384), f32), sds((2, 192, 512), f32), sds((8, 192), f32), sds((2, 1, 384), f32),
                   sds((2, 3, 192, 128), bf16),
                   sds((T, 768), bf16), sds((2, T, 1536), bf16), sds((2, T, 1536), bf16), sds((768, T), bf16), sds((768, T), bf16),
                   sds((T, 768), bf16), sds((T, 768), f32), sds((T, 768), bf16), sds((T, 128), f32), sds((8, 768), f32),
                   sds((3, 768, 384), bf16), sds((384, 768), bf16), sds((768, 1536), bf16), sds((1536, 768), bf16)],
        compiler_params=pltpu.CompilerParams(collective_id=1, has_side_effects=True, vmem_limit_bytes=62 << 20),
        name="forward",
    )(cnt, xt, xlT, wq, lq, lo, lup, ldnT, bq, blq, bu, blu, lgains, lshifts, lcotT, xt, gains, shifts, cot,
      wq, lq, wo, lup, ldnT, up, dn)


FEED = 6
T_PAGES = 2
ATT = FEED + 12
GRADS = ATT + 2
BWD_STEPS = ATT + 10
N_FEED = 6
T_PAGES = 2
N_ATT = 8
FEED_STEPS = ((3, 5, 7, 9, 11, 14), (4, 6, 9, 11, 14, 17), (5, 8, 12, 14, 17, 19), (6, 11, 15, 17, 19, 20),
              (8, 14, 17, 19, 20, 21), (10, 16, 18, 20, 21, 22))
ATT_MADE = (FEED + 1, FEED + 1, FEED + 4, FEED + 4, FEED + 8, ATT, ATT, ATT + 1)
ATT_STEPS = ((14, 15, 16, 17, 19, 20, 21, 22), (16, 17, 18, 19, 20, 21, 22, 23), (18, 19, 19, 20, 21, 22, 23, 24),
             (19, 20, 20, 21, 22, 23, 24, 25), (20, 21, 21, 22, 23, 24, 25, 26), (21, 22, 22, 23, 24, 25, 26, 27))


def by_table(table, k):
    return sum((k >= t).astype(jnp.int32) for t in table)


def feed_made(k):
    return clip(k + 1, 0, N_FEED)


def att_made(k):
    return by_table(ATT_MADE, k)


def each(count, k, run):
    now, before = count(k), count(k - 1)
    for d in (2, 1):
        @pl.when(now - before >= d)
        def _(d=d):
            run(now - d)


class Ring:
    def __init__(self, bufs, where):
        (self.RC, self.RY, self.RX, self.RZ, self.res, self.sends, self.rA, self.rO, self.rB, self.rC, self.rD, self.rE,
         self.rF, self.rH, self.loc) = bufs
        self.z, self.x, self.core, self.mp = where
        self.C = {"core": 1 - self.core}

    def cB(self, j):
        return remote(self.RC.at[j, 0], self.RY.at[j], self.sends.at[1, j], self.rB.at[j], {"mp": 1 - self.mp})

    def cC(self, j):
        return remote(self.RY.at[j, 1 - self.x], self.RX.at[j], self.sends.at[2, j], self.rC.at[j], {"x": 1 - self.x})

    def cD(self, j, d):
        t = (self.z + d) % 4
        return remote(self.RX.at[j, t], self.RZ.at[j, 3 - d], self.sends.at[2 + d, j], self.rD.at[j], {"z": t})

    def place(self, j):
        return self.res.at[j, self.core, self.x]

    def cE(self, j, d):
        t = (self.z + d) % 4
        return remote(self.RX.at[j, self.z], self.place(j).at[self.z], self.sends.at[5 + d, j], self.rE.at[j], {"z": t})

    def cF(self, j):
        return remote(self.place(j), self.place(j), self.sends.at[9, j], self.rF.at[j], {"x": 1 - self.x})

    def cH(self, j):
        return remote(self.res.at[j, self.core], self.res.at[j, self.core], self.sends.at[10, j], self.rH.at[j], self.C)

    def kept(self, j):
        return pltpu.make_async_copy(self.RX.at[j, self.z], self.place(j).at[self.z], self.loc.at[j])

    def add(self, j, i, part):
        self.RC[j, i] = self.RC[j, i] + part

    def stages(self, k, counts):
        z, x = self.z, self.x

        def meet(j):
            self.cB(j).wait_recv()
            self.RY[j] = self.RY[j] + self.RC[j, 1]
            self.cC(j).start()

        def scatter(j):
            self.cC(j).wait_recv()
            self.RX[j] = self.RX[j] + self.RY[j, x]
            for d in range(1, 4):
                self.cD(j, d).start()

        def gather(j):
            remote(self.RZ.at[j], self.RZ.at[j], self.sends.at[3, j], self.rD.at[j], {"z": (z + 1) % 4}).wait_recv()
            tot = self.RX[j, z].astype(f32)
            for d in range(3):
                tot = tot + self.RZ[j, d].astype(f32)
            self.RX[j, z] = tot.astype(bf16)
            for d in range(1, 4):
                self.cE(j, d).start()
            self.kept(j).start()

        def back_x(j):
            three = self.place(j).at[pl.ds(0, 3)]
            remote(three, three, self.sends.at[6, j], self.rE.at[j], {"z": (z + 1) % 4}).wait_recv()
            self.kept(j).wait()
            self.cF(j).start()

        def back_core(j):
            self.cF(j).wait_recv()
            self.cH(j).start()

        def done(j):
            self.cH(j).wait_recv()
            self.cB(j).wait_send()
            self.cC(j).wait_send()
            for d in range(1, 4):
                self.cD(j, d).wait_send()
                self.cE(j, d).wait_send()
            self.cF(j).wait_send()
            self.cH(j).wait_send()

        for count, run in zip(counts, (meet, scatter, gather, back_x, back_core, done)):
            each(count, k, run)


def backward_kernel(h1T, gp, act, df, dno, dnp, upo, upp, qkvt, qkvl, lse, gains, dcl, ldr1, wql, xlT, lay1, lay2,
                    sums, lsums, lbsum, dr2, a_n1, a_rs1, a_wout, a_woutp, a_wq, a_wqp, a_ctx, a_x,
                    res_f, res_a, gx, gxlT,
                    dh1, n1, rs1, wout, woutp, wq, wqp, ctx, xs, dab, daT, bsum, sums1, DQ, DQL, dct_s, klT_s, avl, akl, dqT, dqlT,
                    small, PF, PA, *ring_refs):
    k = pl.program_id(0)
    z, x, core, mp = (lax.axis_index(a) for a in ("z", "x", "core", "mp"))
    ini = ring_refs[-1]
    feed = Ring(ring_refs[0:4] + (res_f,) + ring_refs[8:18], (z, x, core, mp))
    att = Ring(ring_refs[4:8] + (res_a,) + ring_refs[18:28], (z, x, core, mp))

    def loads(i):
        a, b = ((dr2, dh1), (a_n1, n1), (a_rs1, rs1), (a_wout, wout), (a_woutp, woutp), (a_wq, wq), (a_wqp, wqp),
                (a_ctx, ctx), (a_x, xs))[i]
        return pltpu.make_async_copy(a, b, ini.at[i])

    @pl.when(k == 0)
    def _():
        for i in range(9):
            loads(i).start()
        bar = pltpu.get_barrier_semaphore()
        for who in ({"core": 1 - core}, {"mp": 1 - mp}, {"x": 1 - x}):
            pl.semaphore_signal(bar, inc=1, device_id=who, device_id_type=MESH)
        for d in range(1, 4):
            pl.semaphore_signal(bar, inc=1, device_id={"z": (z + d) % 4}, device_id_type=MESH)
        pl.semaphore_wait(bar, 6)
        loads(0).wait()

    @pl.when(k == FEED)
    def _():
        for i in range(1, 9):
            loads(i).wait()

    def feed_A(j):
        return remote(PF.at[1 - core], feed.RC.at[j], feed.sends.at[0, j], feed.rA.at[j], feed.C)

    def att_A(j):
        return remote(PA.at[j % 2, 1 - core], att.RC.at[j], att.sends.at[0, j], att.rA.at[j], att.C)

    def feed_B(j):
        feed_A(j).wait_recv()
        for i in range(2):
            feed.add(j, i, PF[core, i])
        feed.cB(j).start()
        feed_A(j).wait_send()

    def att_B(j):
        att_A(j).wait_recv()
        for i in range(2):
            att.add(j, i, PA[j % 2, core, i])
        att.cB(j).start()
        att_A(j).wait_send()

    each(feed_made, k - 1, feed_B)
    each(att_made, k - 1, att_B)

    def put(h, i, t):
        t = t.astype(bf16).reshape(2, 2, 4, 16, WIDE)
        PA[i % 2, 0, 1 - h] = t[0]
        PA[i % 2, 1, 1 - h] = t[1]

    dns, ups = (dno, dnp), (upo, upp)

    @pl.when(k < FEED)
    def _():
        dps = []
        for h in range(2):
            dp = (dot_nt(df[...], dns[h][...]) * gp[h].astype(f32)).astype(bf16)
            bsum[h, pl.ds(k, 1), :] = colsum(dp.astype(f32))
            t = dot(h1T[...], dp).astype(bf16)
            PF[0, 1 - h] = jnp.concatenate([t[0:256], t[256:512], t[512:768]], axis=1).reshape(2, 4, 32, WIDE)
            PF[1, 1 - h] = dot_tn(act[h], df[...]).astype(bf16).reshape(2, 4, 32, WIDE)
            dps.append(dp)
        dp = jnp.concatenate(dps, axis=1)
        up = jnp.concatenate([upo[...], upp[...]], axis=1)
        for r in range(2):
            rs = slice(512 * r, 512 * r + 512)
            dh1[rs, :] = dh1[rs, :] + dot_nt(dp[rs, :], up)

    def two(h, rows, cols, right):
        lo, hi = rows
        return jnp.concatenate([dot(cols[lo:hi, :], right), dot(cols[384 + lo:384 + hi, :], right)], axis=1)

    def pair_rows(h, p, lo, hi):
        return two(h, (lo, hi), xs, jnp.concatenate([DQ[h, 0, p], DQ[h, 1, p], DQ[h, 2, p]], axis=1))

    def make(h, i):
        stack = lambda *v: jnp.concatenate(v, axis=0)
        if i == 0:
            t = two(h, (0, 256), daT, ctx[h])
        elif i == 1:
            t = stack(two(h, (256, 384), daT, ctx[h]), jnp.concatenate([lay1[h, 0:128], lay2[h, 0:128, 0:384]], axis=1))
        elif i == 2:
            t = stack(jnp.concatenate([lay1[h, 128:192], lay2[h, 128:192, 0:384]], axis=1), jnp.zeros((64, WIDE), f32),
                      pair_rows(h, 0, 0, 128))
        elif i == 3:
            t = pair_rows(h, 0, 128, 384)
        elif i == 4:
            t = pair_rows(h, 1, 0, 256)
        elif i == 5:
            t = stack(pair_rows(h, 1, 256, 384), pair_rows(h, 2, 0, 128))
        elif i == 6:
            t = pair_rows(h, 2, 128, 384)
        else:
            for pg in range(T_PAGES):
                rs = slice(SEQ * pg, SEQ * pg + SEQ)
                DQL[h, 0, rs, :] = dqlT[2 * h + pg].T.astype(bf16)
                DQL[h, 1, rs, :] = akl[2 * h + pg].astype(bf16)
                DQL[h, 2, rs, :] = avl[2 * h + pg].astype(bf16)
            xT = xlT[...]
            t = jnp.concatenate([dot(xT, DQL[h, 0]), dot(xT, DQL[h, 1]), dot(xT, DQL[h, 2]), lay2[h, :, 384:512],
                                 jnp.zeros((192, 256), f32)], axis=1)
            small[...] = jnp.zeros_like(small)
            for r, v in enumerate((sums1[0:1, :], sums[0:1, :], sums1[1:2, :], sums[1:2, :], sums1[2:3, :], sums[2:3, :])):
                small[r:r + 1, :] = v
            small[6:12, 0:192] = lsums[0:6, :]
            for n, c in enumerate((0, 2)):
                for p in range(3):
                    at = 384 * n + 128 * p
                    small[12:13, at:at + 128] = colsum(DQ[h, c, p].astype(f32))
                small[13:14, 128 * n:128 * n + 128] = colsum(DQL[h, c].astype(f32))
            for b in range(6):
                small[14 + b // 3:15 + b // 3, 256 * (b % 3):256 * (b % 3) + 256] = bsum[h, b:b + 1, :]
            small[16:17, 0:384] = lbsum[h]
            t = stack(t, small[...])
        put(h, i, t)

    for at in sorted(set(ATT_MADE)):
        @pl.when(k == at)
        def _(at=at):
            for i in range(N_ATT):
                if ATT_MADE[i] == at:
                    for h in range(2):
                        make(h, i)

    each(feed_made, k, lambda j: feed_A(j).start())
    each(att_made, k, lambda j: att_A(j).start())

    @pl.when(k == FEED)
    def _():
        s1 = s2 = s3 = None
        for r in range(4):
            rs = slice(256 * r, 256 * r + 256)
            g = dh1[rs, :]
            n = n1[rs, :].astype(f32)
            d = norm_back(g * gains[0:1], n, rs1[rs, 0:1])
            dh1[rs, :] = d
            db = d.astype(bf16)
            dab[rs, :] = db
            daT[:, rs] = db.T
            t1, t2, t3 = colsum(g * n), colsum(g), colsum(d)
            s1, s2, s3 = (t1, t2, t3) if s1 is None else (s1 + t1, s2 + t2, s3 + t3)
        sums1[...] = jnp.concatenate([s1, s2, s3, jnp.zeros((5, WIDE), f32)], axis=0)

    @pl.when((k >= FEED) & (k < ATT))
    def _():
        a = k - FEED
        pair = a // 4
        hf = 1 - (a % 4) // 2
        page = a % 2
        at = 2 * hf + page
        rs = pl.ds(pl.multiple_of(page * SEQ, SEQ), SEQ)

        @pl.when(pair == 0)
        def _():
            avl[at] = jnp.zeros((SEQ, 128), f32)
            akl[at] = jnp.zeros((SEQ, 128), f32)
            dqlT[at] = jnp.zeros((128, SEQ), f32)

        ws = pl.ds(pl.multiple_of(pair * 128, 128), 128)
        for h, w in enumerate((wout, woutp)):
            @pl.when(hf == h)
            def _(w=w):
                dct_s[...] = dot_nt(dab[rs, :], w[ws, :]).astype(bf16)

        klT_s[...] = qkvl[0, 1].T
        qc = jnp.concatenate([qkvt[0, 0, 0], qkvl[0, 0]], axis=1)
        kc = jnp.concatenate([qkvt[0, 1, 0], qkvl[0, 1]], axis=1)
        vc = jnp.concatenate([qkvt[0, 2, 0], qkvl[0, 2]], axis=1)
        dc = jnp.concatenate([dct_s[...], dcl[0]], axis=1)
        ktT = qkvt[0, 1, 0].T
        zero = jnp.zeros_like(kc)
        av = ak = None
        for hh in range(2):
            h = 2 * pair + hh
            lane = lax.broadcasted_iota(jnp.int32, (1, 256), 1)
            mv = ((lane >= 64 * hh) & (lane < 64 * hh + 64)) | ((lane >= 128 + 16 * h) & (lane < 144 + 16 * h))
            mk = mv | (lane == 224)
            E = jnp.exp(dot_nt(jnp.where(mk, kc, zero), qc) - lse[0, 0, pl.ds(h, 1), :])
            dP = dot_nt(jnp.where(mv, vc, zero), dc)
            X = E * dP
            dS = (X - E * colsum(X)).astype(bf16)
            ov = dot(E.astype(bf16), jnp.where(mv, dc, zero))
            ok = dot(dS, jnp.where(mv, qc, zero))
            av = ov[:, :128] if av is None else av + ov[:, :128]
            ak = ok[:, :128] if ak is None else ak + ok[:, :128]
            avl[at] += ov[:, 128:]
            akl[at] += ok[:, 128:]
            ls = pl.ds(pl.multiple_of(16 * h, 16), 16)
            kT = jnp.concatenate([ktT[64 * hh:64 * hh + 64], klT_s[ls, :]], axis=0)
            oq = dot(kT, dS)
            dqT[64 * hh:64 * hh + 64, :] = oq[:64] * 0.125
            dqlT[at, ls, :] = oq[64:] * 0.25
        DQ[hf, 0, pair, rs, :] = dqT[...].T.astype(bf16)
        DQ[hf, 1, pair, rs, :] = ak.astype(bf16)
        DQ[hf, 2, pair, rs, :] = av.astype(bf16)

    @pl.when((k >= GRADS) & (k < GRADS + 4))
    def _():
        rs = pl.ds(pl.multiple_of((k - GRADS) * 256, 256), 256)
        g = dh1[rs, :]
        gl = ldr1[...]
        for h in range(2):
            for c in range(3):
                g = g + dot_nt(jnp.concatenate([DQ[h, c, p, rs, :] for p in range(3)], axis=1), (wq, wqp)[h][c])
                gl = gl + dot_nt(DQL[h, c, rs, :], wql[h, c])
        gx[...] = g
        gxlT[...] = gl.T

    feed.stages(k, [functools.partial(by_table, t) for t in FEED_STEPS])
    att.stages(k, [functools.partial(by_table, t) for t in ATT_STEPS])


def backward(h1T, gp, act, df, dno, dnp, upo, upp, qkvt, qkvl, lse, x, n1, rs1, gains, dcl, ldr1, wout, woutp, wq, wqp, wql,
             ctx, xlT, lay1, lay2, sums, lsums, lbsum, dr2):
    T = n1.shape[0]
    blk = lambda k: clip(k, 0, FEED - 1)
    att = lambda k: clip(k - FEED, 0, 11)
    head = lambda k: (1 - (att(k) % 4) // 2, att(k) % 2, att(k) // 4)
    D = pltpu.SemaphoreType.DMA
    V = pltpu.VMEM
    sd = jax.ShapeDtypeStruct
    hid = pl.BlockSpec((2, T, 256), lambda k: (0, 0, blk(k)))
    rowb = pl.BlockSpec((256, WIDE), lambda k: (blk(k), 0))
    colb = pl.BlockSpec((WIDE, 256), lambda k: (0, blk(k)))
    grow = lambda k: clip(k - GRADS, 0, 3)
    anyspec = pl.BlockSpec(memory_space=pl.ANY)
    in_specs = [
        whole(h1T), hid, hid, whole(df), rowb, rowb, colb, colb,
        pl.BlockSpec((1, 3, 1, SEQ, 128), lambda k: (head(k)[0], 0, head(k)[2], head(k)[1], 0)),
        pl.BlockSpec((1, 3, SEQ, 128), lambda k: (head(k)[0], 0, head(k)[1], 0)),
        pl.BlockSpec((1, 1, 8, SEQ), lambda k: (head(k)[0], head(k)[1], 0, 0)),
        whole(gains),
        pl.BlockSpec((1, SEQ, 128), lambda k: (head(k)[0], head(k)[1], 0)),
        pl.BlockSpec((256, 192), lambda k: (grow(k), 0)),
    ] + [whole(a) for a in (wql, xlT, lay1, lay2, sums, lsums, lbsum)] + [anyspec] * 9
    bufs = lambda n, r: [V((n, 2, 2, 4, r, WIDE), bf16), V((n, 2, 4, r, WIDE), bf16), V((n, 4, r, WIDE), bf16),
                         V((n, 3, r, WIDE), bf16)]
    sems = lambda n: [D((12, n))] + [D((n,))] * 9
    return pl.pallas_call(
        backward_kernel,
        grid=(BWD_STEPS,),
        in_specs=in_specs,
        out_specs=[anyspec, anyspec,
                   pl.BlockSpec((256, WIDE), lambda k: (grow(k), 0)),
                   pl.BlockSpec((192, 256), lambda k: (0, grow(k)))],
        out_shape=[sd((N_FEED, 2, 2, 4, 32, WIDE), bf16), sd((N_ATT, 2, 2, 4, 16, WIDE), bf16), sd((T, WIDE), f32),
                   sd((192, T), f32)],
        scratch_shapes=[
            V((T, WIDE), f32), V((T, WIDE), bf16), V((T, 128), f32), V((384, WIDE), bf16), V((384, WIDE), bf16),
            V((3, WIDE, 384), bf16), V((3, WIDE, 384), bf16), V((2, T, 384), bf16), V((WIDE, T), bf16),
            V((T, WIDE), bf16), V((WIDE, T), bf16), V((2, 8, 256), f32), V((8, WIDE), f32),
            V((2, 3, 3, T, 128), bf16), V((2, 3, T, 128), bf16), V((SEQ, 128), bf16),
            V((128, SEQ), bf16), V((4, SEQ, 128), f32), V((4, SEQ, 128), f32), V((128, SEQ), f32), V((4, 128, SEQ), f32),
            V((64, WIDE), f32),
            V((2, 2, 2, 4, 32, WIDE), bf16), V((2, 2, 2, 2, 4, 16, WIDE), bf16)]
        + bufs(N_FEED, 32) + bufs(N_ATT, 16) + sems(N_FEED) + sems(N_ATT) + [D((9,))],
        compiler_params=pltpu.CompilerParams(collective_id=0, has_side_effects=True, vmem_limit_bytes=63 << 20),
        name="backward",
    )(h1T, gp, act, df, dno, dnp, upo, upp, qkvt, qkvl, lse, gains, dcl, ldr1, wql, xlT, lay1, lay2, sums, lsums, lbsum, dr2,
      n1, rs1, wout, woutp, wq, wqp, ctx, x)


def unpack_kernel(rf, r, up, dn, qkv, out, lqkv, lup, ldnT, lout, qvb, upb, gain, shift, lqvb, lupb, lgain, lshift):
    k = pl.program_id(0)

    @pl.when(k < 6)
    def _():
        for i in range(3):
            up[256 * i:256 * i + 256, :] = rf[0:256, 256 * i:256 * i + 256].astype(f32)
        dn[...] = rf[256:512, :].astype(f32)

    def put_pair(p, lo, a):
        for i in range(2):
            rows = slice(384 * i + lo, 384 * i + lo + a.shape[0])
            for c in range(3):
                qkv[c, rows, 128 * p:128 * p + 128] = a[:, 384 * i + 128 * c:384 * i + 128 * c + 128].astype(f32)

    @pl.when(k == 6)
    def _():
        for i in range(2):
            out[:, 384 * i:384 * i + 384] = r[0:384, 384 * i:384 * i + 384].astype(f32).T
        lup[0:128, :] = r[384:512, 0:384].astype(f32)
        ldnT[0:128, :] = r[384:512, 384:768].astype(f32)

    @pl.when(k == 7)
    def _():
        lup[128:192, :] = r[0:64, 0:384].astype(f32)
        ldnT[128:192, :] = r[0:64, 384:768].astype(f32)
        put_pair(0, 0, r[128:512, :])

    @pl.when(k == 8)
    def _():
        put_pair(1, 0, r[0:384, :])
        put_pair(2, 0, r[384:512, :])

    @pl.when(k == 9)
    def _():
        put_pair(2, 128, r[0:256, :])
        for c in range(3):
            lqkv[c] = r[256:448, 128 * c:128 * c + 96].astype(f32)
        lout[...] = r[256:448, 384:512].astype(f32).T[:96, :]
        s = r[448:480, :].astype(f32)
        gain[...] = s[0:2]
        shift[...] = s[2:6]
        lgain[...] = s[6:8, 0:192]
        lshift[...] = s[8:12, 0:192]
        for i in range(2):
            qvb[i:i + 1, :] = s[12:13, 384 * i:384 * i + 384]
            lqvb[i:i + 1, :] = s[13:14, 128 * i:128 * i + 96]
            for j in range(6):
                upb[6 * i + j:6 * i + j + 1, :] = s[14 + i:15 + i, 128 * j:128 * j + 128]
        for j in range(3):
            lupb[j:j + 1, :] = s[16:17, 128 * j:128 * j + 128]


def unpack(feed, att):
    const = lambda s: pl.BlockSpec(s, lambda k: (0,) * len(s))
    sd = jax.ShapeDtypeStruct
    shapes = [(768, 1536), (1536, 768), (3, 768, 384), (384, 768), (3, 192, 96), (192, 384), (192, 384), (96, 192),
              (2, 384), (12, 128), (2, 768), (4, 768), (2, 96), (3, 128), (2, 192), (4, 192)]
    specs = [const(s) for s in shapes]
    specs[0] = pl.BlockSpec((768, 256), lambda k: (0, clip(k, 0, 5)))
    specs[1] = pl.BlockSpec((256, 768), lambda k: (clip(k, 0, 5), 0))
    return pl.pallas_call(
        unpack_kernel, grid=(10,),
        in_specs=[pl.BlockSpec((512, 768), lambda k: (clip(k, 0, 5), 0)), pl.BlockSpec((512, 768), lambda k: (clip(k - 6, 0, 3), 0))],
        out_specs=specs, out_shape=[sd(s, f32) for s in shapes],
        compiler_params=pltpu.CompilerParams(vmem_limit_bytes=56 << 20), name="unpack_gradients",
    )(feed, att)


def body(n_group, text_states, layout_states, box_counts, text_qkv, text_qv_bias, text_out, text_up, text_up_bias,
         text_down, text_gains, text_shifts, layout_qkv, layout_qv_bias, layout_out, layout_up, layout_up_bias,
         layout_down, layout_gains, layout_shifts, cot_text, cot_layout):
    tq = jnp.transpose(text_qkv, (1, 0, 2))
    lq = jnp.transpose(layout_qkv, (1, 0, 2))
    xlT = layout_states.T
    (qkvt, qkvl, lse, ctx, out_lT, ldr1, dcl, lay1, lay2, lsums, lbsum, lqp, out_t, act, gp, h1T, xT, df, dr2, n1, rs1, sums,
     wq, wo, wu, wd) = forward(
        box_counts, text_states, xlT, tq, lq, text_out, layout_out, layout_up, layout_down.T, text_up, text_down,
        text_qv_bias, layout_qv_bias, text_up_bias.reshape(12, 128), layout_up_bias.reshape(3, 128), layout_gains,
        layout_shifts, cot_layout.T, text_gains, text_shifts, cot_text)
    feed, att, gx, gxlT = backward(h1T, gp, act, df, text_down, wd, text_up, wu, qkvt, qkvl, lse, xT, n1, rs1,
                             text_gains, dcl, ldr1, text_out, wo, tq, wq, lqp, ctx, xlT, lay1, lay2, sums, lsums, lbsum,
                             dr2)
    feed = feed.reshape(N_FEED * 512, WIDE)
    att = att.reshape(N_ATT * 256, WIDE)
    if n_group > 1:
        feed, att = lax.psum((feed, att), "group")
    (g_up, g_dn, g_qkv, g_o, gl_qkv, gl_up, gl_dnT, gl_o, qvb, upb, gain, shift, lqvb, lupb, lgain, lshift) = unpack(feed, att)
    swap = lambda a: jnp.transpose(a, (1, 0, 2))
    return (out_t, out_lT.T, gx, gxlT.T, swap(g_qkv), qvb, g_o, g_up, upb.reshape(1536), g_dn, gain, shift,
            swap(gl_qkv), lqvb, gl_o, gl_up, lupb.reshape(384), gl_dnT.T, lgain, lshift)


def solution(mesh):
    dp = mesh.shape["dp"]
    n_group = dp // 16
    fine = Mesh(mesh.devices.reshape(n_group, 4, 2, 2, 2), AXES)
    rows = P(AXES, None)
    half2 = P(None, "mp")
    half1 = P("mp", None)
    qkv = P(None, None, "mp")
    rep = P()
    return jax.shard_map(
        functools.partial(body, n_group),
        mesh=fine,
        in_specs=(rows, rows, P(AXES[:4]), qkv, half2, half1, half2, P("mp"), half1, rep, rep,
                  qkv, half2, half1, half2, P("mp"), half1, rep, rep, rows, rows),
        out_specs=(rows, rows, rows, rows, qkv, half2, half1, half2, P("mp"), half1, rep, rep,
                   qkv, half2, half1, half2, P("mp"), half1, rep, rep),
        check_vma=False,
    )
```

```python
import functools

import jax
import jax.numpy as jnp
from jax import lax
from jax.experimental import pallas as pl
from jax.experimental.pallas import tpu as pltpu
from jax.sharding import Mesh, PartitionSpec as P

f32 = jnp.float32
bf16 = jnp.bfloat16
SEQ = 512
NT = (((1,), (1,)), ((), ()))
TN = (((0,), (0,)), ((), ()))
AXES = ("group", "z", "x", "core", "mp")
MESH = pl.DeviceIdType.MESH
WIDE = 768


def dot(a, b):
    return jnp.dot(a, b, preferred_element_type=f32)


def dot_nt(a, b):
    return lax.dot_general(a, b, NT, preferred_element_type=f32)


def dot_tn(a, b):
    return lax.dot_general(a, b, TN, preferred_element_type=f32)


def colsum(v):
    return jnp.sum(v, axis=0, keepdims=True)


def whole(a):
    return pl.BlockSpec(a.shape, lambda *i: (0,) * a.ndim, pipeline_mode=pl.Buffered(1))


GC = [0.11609199498651965, 0.07018864201817518, 0.2621979336040309, -0.22868178430415115, 0.38476147983842124,
      -0.10455825070574547]
GP = 0.28


def gelu_pair(v):
    t = 1.0 / (1.0 + GP * jnp.abs(v))
    g = jnp.exp(v * v * -0.5)
    q = GC[5]
    for c in GC[4::-1]:
        q = q * t + c
    q = q * t * g
    phi = jnp.where(v < 0, q, 1.0 - q)
    return v * phi, phi + v * g * 0.3989422804014327


def norm_stats(r):
    cen = r - jnp.mean(r, -1, keepdims=True)
    rstd = lax.rsqrt(jnp.mean(cen * cen, -1, keepdims=True) + 1e-5)
    return cen * rstd, rstd


def norm_back(e, n, rstd):
    return (e - jnp.mean(e, -1, keepdims=True) - n * jnp.mean(e * n, -1, keepdims=True)) * rstd


def head_masks(h):
    lane = lax.broadcasted_iota(jnp.int32, (1, 256), 1)
    t = (lane >= 64 * (h % 2)) & (lane < 64 * (h % 2) + 64)
    l = (lane >= 128 + 16 * h) & (lane < 128 + 16 * h + 16)
    return t | l, t | l | (lane == 224)


def row_of(b, at, n):
    return jnp.concatenate([b[i:i + 1, :] for i in range(at // 128, (at + n) // 128)], axis=1)


def clip(v, a, b):
    return jnp.minimum(jnp.maximum(v, a), b)


def remote(src, dst, s, r, who):
    return pltpu.make_async_remote_copy(src_ref=src, dst_ref=dst, send_sem=s, recv_sem=r, device_id=who,
                                        device_id_type=MESH)


def second_norm(r2, gains, shifts, ct):
    n2, rstd2 = norm_stats(r2)
    dr2 = norm_back(ct * gains[1:2], n2, rstd2)
    return n2 * gains[1:2] + shifts[1:2], dr2, (colsum(ct * n2), colsum(ct), colsum(dr2))


PIECES = 15
START = [0, 0, 0, 0, 2, 3, 3, 4, 5, 6, 7, 8, 9, 10, 11]
RELAY = [2, 4, 5, 5, 6, 6, 6, 7, 8, 9, 10, 12, 14, 15, 16]
AHEAD = [5, 6, 6, 6, 9, 9, 9, 10, 11, 12, 14, 15, 17, 18, 19]
TEXT = 6
TEXT2 = 10
FWD_STEPS = 14


def forward_kernel(cnt, xt, xlT, wq, lq, lo, lup, ldnT, bq, blq, bu, blu, lgains, lshifts, lcotT, x2, gains, shifts, cot,
                   a_wq, a_lq, a_wo, a_lup, a_ldnT, a_up, a_dn,
                   qkvt, qkvl, lse_o, ctxt, outT, ldr1, dcl, lay1, lay2, lsums, lbsum, lqp,
                   out, act, gp, h1T, x_T, dfo, dr2o, n1o, rso, sums, o_wq, o_wo, o_up, o_dn,
                   cT, clT, ctx_s, ctl, xl_s, lact, lgp, ldpre, lh1, ldf, lda, wq_v, lq_v, lup_v, ldnT_v, lo_p, lq_p,
                   wo_v, up_v, dn_v, wo_s, up_s, dn_s, h1_s, r2_s, obq, oblq, obu, oblu,
                   sy, ry, sx, rx, sc, rc, sd, rd, ss, rs_, loc, own):
    k = pl.program_id(0)
    x, core, mp = (lax.axis_index(a) for a in ("x", "core", "mp"))
    Y, X, C = {"mp": 1 - mp}, {"x": 1 - x}, {"core": 1 - core}
    q_me = 2 * x + core
    q_x = 2 * (1 - x) + core

    def cut(ref, q, n, sub, nsub):
        m = n // 4 // nsub
        return ref.at[pl.ds(pl.multiple_of(q * (n // 4) + sub * m, 16), m), :]

    def piece(i, q, mine):
        if i < 3:
            return cut((a_wq if mine else wq_v).at[i], q, 768, 0, 1)
        if i == 3:
            return (a_lq if mine else lq_v).at[:, pl.ds(pl.multiple_of(q * 48, 16), 48), :]
        if i == 4:
            return cut(a_wo if mine else wo_v, q, 384, 0, 1)
        if i == 5:
            return cut(a_lup if mine else lup_v, q, 192, 0, 1)
        if i == 6:
            return cut(a_ldnT if mine else ldnT_v, q, 192, 0, 1)
        if i < 11:
            return cut(a_up if mine else up_v, q, 768, i - 7, 4)
        return cut(a_dn if mine else dn_v, q, 1536, i - 11, 4)

    def over_y(i):
        return remote(piece(i, q_me, True), piece(i, q_me, False), sy.at[i], ry.at[i], Y)

    def over_x(i):
        return remote(piece(i, q_me, False), piece(i, q_me, False), sx.at[i], rx.at[i], X)

    def over_core(i):
        return remote(piece(i, q_me, False), piece(i, q_me, False), sc.at[i], rc.at[i], C)

    def over_core2(i):
        return remote(piece(i, q_x, False), piece(i, q_x, False), sd.at[i], rd.at[i], C)

    def arrived(i):
        over_core(i).wait_recv()
        over_core2(i).wait_recv()

    def small():
        pairs = ((bq, obq), (blq, oblq), (bu, obu), (blu, oblu), (lo, lo_p.at[1, 0:96]))
        return [remote(a, b, ss.at[i], rs_.at[i], Y) for i, (a, b) in enumerate(pairs)]

    def keep(i):
        a, b = ((wq_v, o_wq), (wo_v, o_wo), (up_v, o_up), (dn_v, o_dn))[i]
        return pltpu.make_async_copy(a, b, loc.at[i])

    def load_own():
        return [pltpu.make_async_copy(a, b, own.at[i]) for i, (a, b) in enumerate(
            ((a_wo, wo_s), (a_up, up_s), (a_dn, dn_s)))]

    @pl.when(k == 0)
    def _():
        lo_p[...] = jnp.zeros_like(lo_p)
        bar = pltpu.get_barrier_semaphore()
        for who in (C, Y, X):
            pl.semaphore_signal(bar, inc=1, device_id=who, device_id_type=MESH)
        pl.semaphore_wait(bar, 3)
        for c in small():
            c.start()

    def slot(step, s):
        @pl.when(k == step)
        def _():
            for i in range(PIECES):
                if START[i] == s:
                    over_y(i).start()
            for i in range(PIECES):
                if RELAY[i] == s:
                    over_y(i).wait_recv()
                    over_x(i).start()
                    over_core(i).start()
            for i in range(PIECES):
                if AHEAD[i] == s:
                    over_x(i).wait_recv()
                    over_core2(i).start()

    for st in range(4):
        slot(st, 3 * st)

    @pl.when(k == 0)
    def _():
        for c in load_own():
            c.start()
        lq_p[...] = jnp.zeros_like(lq_p)
        lo_p[0, 0:96, :] = lo[...]
        for c in range(3):
            lq_p[0, c, :, 0:96] = lq[c]
        lsums[...] = jnp.zeros_like(lsums)
        lbsum[...] = jnp.zeros_like(lbsum)

    @pl.when(k == 2)
    def _():
        for c in small():
            c.wait_recv()
        for i in range(4):
            arrived(i)
        for c in range(3):
            lq_p[1, c, :, 0:96] = lq_v[c]
        keep(0).start()

    @pl.when(k < 4)
    def _():
        hf = k // 2
        page = k % 2

        def project(w, b, lb):
            n = cnt[2 * mp + page]
            lane = lax.broadcasted_iota(jnp.int32, (SEQ, 128), 1)
            row = lax.broadcasted_iota(jnp.int32, (SEQ, 128), 0)
            for c in range(3):
                r = dot(xt[...], w[c])
                s = dot(xl_s[page], lq_p[hf, c])
                if c != 1:
                    r = r + b[c // 2:c // 2 + 1]
                    s = s + jnp.concatenate([lb[c // 2:c // 2 + 1], jnp.zeros((1, 32), f32)], axis=1)
                if c == 0:
                    r = r * 0.125
                    s = jnp.where(lane == 96, 1.0, s * 0.25)
                if c == 1:
                    s = jnp.where((lane == 96) & (row >= n), -1e30, s)
                for p in range(3):
                    qkvt[0, c, p] = r[:, 128 * p:128 * p + 128].astype(bf16)
                qkvl[0, c] = s.astype(bf16)

        @pl.when(hf == 0)
        def _():
            xl_s[page] = xlT[...].T
            project(wq, bq, blq)

        @pl.when(hf == 1)
        def _():
            project(wq_v, obq, oblq)

        rows = pl.ds(pl.multiple_of(page * SEQ, SEQ), SEQ)
        vlT = qkvl[0, 2].T
        for p in range(3):
            if p > 0:
                for st in range(4):
                    slot(st, 3 * st + p)
            qc = jnp.concatenate([qkvt[0, 0, p], qkvl[0, 0]], axis=1)
            kc = jnp.concatenate([qkvt[0, 1, p], qkvl[0, 1]], axis=1)
            vtT = qkvt[0, 2, p].T
            for hh in range(2):
                h = 2 * p + hh
                mk = head_masks(h)[1]
                S = dot_nt(jnp.where(mk, kc, jnp.zeros_like(kc)), qc)
                m = jnp.max(S, axis=0, keepdims=True)
                e = jnp.exp(S - m)
                l = colsum(e)
                vT = jnp.concatenate([vtT[64 * hh:64 * hh + 64], vlT[16 * h:16 * h + 16]], axis=0)
                o = dot(vT, e.astype(bf16)) * (1.0 / l)
                cT[64 * hh:64 * hh + 64, :] = o[:64]
                clT[16 * h:16 * h + 16, :] = o[64:]
                lse_o[0, 0, h:h + 1, :] = m + jnp.log(l)
            cv = cT[...].T.astype(bf16)
            ctxt[0, :, 128 * p:128 * p + 128] = cv
            ctx_s[hf, rows, 128 * p:128 * p + 128] = cv
        clT[96:, :] = jnp.zeros((32, SEQ), f32)
        ctl[hf, rows, :] = clT[...].T.astype(bf16)
        lse_o[0, 0, 6:8, :] = jnp.zeros((2, SEQ), f32)

    slot(4, 12)
    slot(5, 14)

    @pl.when(k == 4)
    def _():
        arrived(5)
        arrived(6)

    @pl.when((k == 4) | (k == 5))
    def _():
        page = k - 4
        rows = pl.ds(pl.multiple_of(page * SEQ, SEQ), SEQ)
        ups, dns, bs_ = (lup, lup_v), (ldnT, ldnT_v), (blu, oblu)

        attn = dot(ctl[0, rows, :], lo_p[0]) + dot(ctl[1, rows, :], lo_p[1])
        n1, rstd1 = norm_stats(xl_s[page].astype(f32) + attn + lshifts[2:3])
        h1 = n1 * lgains[0:1] + lshifts[0:1]
        h1b = h1.astype(bf16)
        r2 = h1 + lshifts[3:4]
        for h in range(2):
            if h == 1:
                slot(4, 13)
                slot(5, 15)
            ga, gd = gelu_pair(dot(h1b, ups[h][...]) + row_of(bs_[h], 0, 384))
            ab = ga.astype(bf16)
            lact[h, rows, :] = ab
            lgp[h] = gd
            r2 = r2 + dot_nt(ab, dns[h][...])
        o, dr2, (s_g2, s_s2, s_r2) = second_norm(r2, lgains[...], lshifts[...], lcotT[...].T.astype(f32))
        outT[...] = o.T.astype(bf16)
        df = dr2.astype(bf16)
        dh1 = dr2
        for h in range(2):
            dp = (dot(df, dns[h][...]) * lgp[h]).astype(bf16)
            ldpre[h, rows, :] = dp
            lbsum[h] += colsum(dp.astype(f32))
            dh1 = dh1 + dot_nt(dp, ups[h][...])
        d1 = norm_back(dh1 * lgains[0:1], n1, rstd1)
        ldr1[...] = d1
        db = d1.astype(bf16)
        lh1[rows, :] = h1b
        ldf[rows, :] = df
        lda[rows, :] = db
        for h in range(2):
            dcl[h] = dot_nt(db, lo_p[h]).astype(bf16)
        lsums[...] += jnp.concatenate([colsum(dh1 * n1), s_g2, colsum(dh1), s_s2, colsum(d1), s_r2,
                                       jnp.zeros((2, 192), f32)], axis=0)

    @pl.when(k == 5)
    def _():
        hT = lh1[...].T
        fT = ldf[...].T
        aT = lda[...].T
        for h in range(2):
            lay1[h] = dot(hT, ldpre[h])
            lay2[h, :, 0:384] = dot(fT, lact[h])
            lay2[h, :, 384:512] = dot(aT, ctl[h])
            for c in range(3):
                lqp[h, c] = lq_p[h, c]

    for i in range(4):
        slot(TEXT + i, 16 + i)

    @pl.when(k == TEXT)
    def _():
        for c in load_own():
            c.wait()
        arrived(4)
        sums[...] = jnp.zeros_like(sums)

    def units(h1b, up, dn, b):
        r = None
        for c in range(2):
            cs = slice(768 * c, 768 * c + 768)
            ga, gd = gelu_pair(dot(h1b, up[:, cs]) + row_of(b, 768 * c, 768))
            ab = ga.astype(bf16)
            act[0, :, cs] = ab
            gp[0, :, cs] = gd.astype(bf16)
            t = dot(ab, dn[cs, :])
            r = t if r is None else r + t
        return r

    @pl.when((k >= TEXT) & (k < TEXT2))
    def _():
        rows = pl.ds(pl.multiple_of((k - TEXT) * 256, 256), 256)
        attn = dot(ctx_s[0, rows, :], wo_s[...]) + dot(ctx_s[1, rows, :], wo_v[...])
        n1, rstd1 = norm_stats(x2[...].astype(f32) + attn + shifts[2:3])
        n1o[...] = n1.astype(bf16)
        rso[...] = jnp.broadcast_to(rstd1, (256, 128))
        h1 = n1 * gains[0:1] + shifts[0:1]
        h1b = h1.astype(bf16)
        h1_s[rows, :] = h1b
        h1T[...] = h1b.T
        x_T[...] = x2[...].T
        r2_s[rows, :] = h1 + shifts[3:4] + units(h1b, up_s, dn_s, bu)

    @pl.when(k == TEXT2)
    def _():
        for i in range(7, PIECES):
            arrived(i)
        for i in range(1, 4):
            keep(i).start()

    @pl.when(k >= TEXT2)
    def _():
        rows = pl.ds(pl.multiple_of((k - TEXT2) * 256, 256), 256)
        r2 = r2_s[rows, :] + units(h1_s[rows, :], up_v, dn_v, obu)
        o, dr2, (s_g2, s_s2, s_r2) = second_norm(r2, gains[...], shifts[...], cot[...].astype(f32))
        out[...] = o.astype(bf16)
        dfo[...] = dr2.astype(bf16)
        dr2o[...] = dr2
        sums[...] += jnp.concatenate([s_g2, s_s2, s_r2, jnp.zeros((5, 768), f32)], axis=0)

    @pl.when(k == FWD_STEPS - 1)
    def _():
        for i in range(PIECES):
            over_y(i).wait_send()
            over_x(i).wait_send()
            over_core(i).wait_send()
            over_core2(i).wait_send()
        for c in small():
            c.wait_send()
        for i in range(4):
            keep(i).wait()


def forward(cnt, xt, xlT, wq, lq, wo, lo, lup, ldnT, up, dn, bq, blq, bu, blu, lgains, lshifts, lcotT, gains, shifts, cot):
    T = xt.shape[0]
    n = T // SEQ
    hf = lambda k: clip(k, 0, 3) // 2
    pg = lambda k: clip(k, 0, 3) % 2
    lp = lambda k: clip(k - 4, 0, 1)
    tb = lambda k: clip(k - TEXT, 0, 3)
    anyspec = pl.BlockSpec(memory_space=pl.ANY)
    const = lambda s: pl.BlockSpec(s, lambda k, *_: (0,) * len(s))
    V = pltpu.VMEM
    D = pltpu.SemaphoreType.DMA
    sds = jax.ShapeDtypeStruct
    tb2 = lambda k: clip(k - TEXT2, 0, 3)
    tc = lambda k: clip(k - TEXT, 0, 7)
    trow = pl.BlockSpec((256, 768), lambda k, *_: (tb(k), 0))
    trow2 = pl.BlockSpec((256, 768), lambda k, *_: (tb2(k), 0))
    trow3 = pl.BlockSpec((1, 256, 1536), lambda k, *_: (tc(k) // 4, tc(k) % 4, 0))
    lcol = pl.BlockSpec((192, SEQ), lambda k, *_: (0, lp(k)))
    return pl.pallas_call(
        forward_kernel,
        grid_spec=pltpu.PrefetchScalarGridSpec(
            num_scalar_prefetch=1, grid=(FWD_STEPS,),
            in_specs=[pl.BlockSpec((SEQ, 768), lambda k, *_: (pg(k), 0)),
                      pl.BlockSpec((192, SEQ), lambda k, *_: (0, pg(k)))]
            + [whole(a) for a in (wq, lq, lo, lup, ldnT, bq, blq, bu, blu, lgains, lshifts)]
            + [lcol, trow, whole(gains), whole(shifts), trow2] + [anyspec] * 7,
            out_specs=[pl.BlockSpec((1, 3, 3, SEQ, 128), lambda k, *_: (hf(k), 0, 0, pg(k), 0)),
                       pl.BlockSpec((1, 3, SEQ, 128), lambda k, *_: (hf(k), 0, pg(k), 0)),
                       pl.BlockSpec((1, 1, 8, SEQ), lambda k, *_: (hf(k), pg(k), 0, 0)),
                       pl.BlockSpec((1, SEQ, 384), lambda k, *_: (hf(k), pg(k), 0)),
                       lcol, pl.BlockSpec((SEQ, 192), lambda k, *_: (lp(k), 0)),
                       pl.BlockSpec((2, SEQ, 128), lambda k, *_: (0, lp(k), 0)),
                       const((2, 192, 384)), const((2, 192, 512)), const((8, 192)), const((2, 1, 384)),
                       const((2, 3, 192, 128)),
                       trow2, trow3, trow3, pl.BlockSpec((768, 256), lambda k, *_: (0, tb(k))), pl.BlockSpec((768, 256), lambda k, *_: (0, tb(k))),
                       trow2, trow2, trow,
                       pl.BlockSpec((256, 128), lambda k, *_: (tb(k), 0)), const((8, 768)),
                       anyspec, anyspec, anyspec, anyspec],
            scratch_shapes=[
                V((128, SEQ), f32), V((128, SEQ), f32), V((2, T, 384), bf16), V((2, T, 128), bf16),
                V((n, SEQ, 192), bf16), V((2, T, 384), bf16), V((2, SEQ, 384), f32), V((2, T, 384), bf16),
                V((T, 192), bf16), V((T, 192), bf16), V((T, 192), bf16),
                V((3, 768, 384), bf16), V((3, 192, 96), bf16), V((192, 384), bf16), V((192, 384), bf16),
                V((2, 128, 192), bf16), V((2, 3, 192, 128), bf16),
                V((384, 768), bf16), V((768, 1536), bf16), V((1536, 768), bf16),
                V((384, 768), bf16), V((768, 1536), bf16), V((1536, 768), bf16),
                V((T, 768), bf16), V((T, 768), f32), V((2, 384), f32), V((2, 96), f32), V((12, 128), f32), V((3, 128), f32)]
            + [D((PIECES,))] * 8 + [D((5,)), D((5,)), D((4,)), D((3,))]),
        out_shape=[sds((2, 3, 3, T, 128), bf16), sds((2, 3, T, 128), bf16), sds((2, n, 8, SEQ), f32),
                   sds((2, T, 384), bf16), sds((192, T), bf16), sds((T, 192), f32), sds((2, T, 128), bf16),
                   sds((2, 192, 384), f32), sds((2, 192, 512), f32), sds((8, 192), f32), sds((2, 1, 384), f32),
                   sds((2, 3, 192, 128), bf16),
                   sds((T, 768), bf16), sds((2, T, 1536), bf16), sds((2, T, 1536), bf16), sds((768, T), bf16), sds((768, T), bf16),
                   sds((T, 768), bf16), sds((T, 768), f32), sds((T, 768), bf16), sds((T, 128), f32), sds((8, 768), f32),
                   sds((3, 768, 384), bf16), sds((384, 768), bf16), sds((768, 1536), bf16), sds((1536, 768), bf16)],
        compiler_params=pltpu.CompilerParams(collective_id=1, has_side_effects=True, vmem_limit_bytes=62 << 20),
        name="forward",
    )(cnt, xt, xlT, wq, lq, lo, lup, ldnT, bq, blq, bu, blu, lgains, lshifts, lcotT, xt, gains, shifts, cot,
      wq, lq, wo, lup, ldnT, up, dn)


FEED = 6
T_PAGES = 2
ATT = FEED + 12
GRADS = ATT + 2
BWD_STEPS = ATT + 11
N_FEED = 6
T_PAGES = 2
N_ATT = 8
FEED_STEPS = ((3, 5, 7, 9, 11, 14), (4, 6, 9, 11, 14, 17), (5, 8, 12, 14, 17, 19), (6, 11, 15, 17, 19, 20),
              (8, 14, 17, 19, 20, 21), (10, 16, 18, 20, 21, 22))
ATT_MADE = (FEED + 1, FEED + 1, FEED + 4, FEED + 4, FEED + 8, ATT, ATT, ATT + 1)
ATT_STEPS = ((14, 15, 16, 17, 19, 20, 21, 22), (16, 17, 18, 19, 20, 21, 22, 23), (18, 19, 20, 21, 22, 23, 24, 25),
             (19, 20, 21, 22, 23, 24, 25, 26), (20, 21, 22, 23, 24, 25, 26, 27), (21, 22, 23, 24, 25, 26, 27, 28))


def by_table(table, k):
    return sum((k >= t).astype(jnp.int32) for t in table)


def feed_made(k):
    return clip(k + 1, 0, N_FEED)


def att_made(k):
    return by_table(ATT_MADE, k)


def each(count, k, run, most=1):
    now, before = count(k), count(k - 1)
    for d in range(most, 0, -1):
        @pl.when(now - before >= d)
        def _(d=d):
            run(now - d)


class Ring:
    def __init__(self, bufs, where):
        (self.RC, self.RY, self.RX, self.RZ, self.res, self.sends, self.rA, self.rO, self.rB, self.rC, self.rD, self.rE,
         self.rF, self.rH, self.loc) = bufs
        self.z, self.x, self.core, self.mp = where
        self.C = {"core": 1 - self.core}

    def cB(self, j):
        return remote(self.RC.at[j, 0], self.RY.at[j], self.sends.at[1, j], self.rB.at[j], {"mp": 1 - self.mp})

    def cC(self, j):
        return remote(self.RY.at[j, 1 - self.x], self.RX.at[j], self.sends.at[2, j], self.rC.at[j], {"x": 1 - self.x})

    def cD(self, j, d):
        t = (self.z + d) % 4
        return remote(self.RX.at[j, t], self.RZ.at[j, 3 - d], self.sends.at[2 + d, j], self.rD.at[j], {"z": t})

    def place(self, j):
        return self.res.at[j, self.core, self.x]

    def cE(self, j, d):
        t = (self.z + d) % 4
        return remote(self.RX.at[j, self.z], self.place(j).at[self.z], self.sends.at[5 + d, j], self.rE.at[j], {"z": t})

    def cF(self, j):
        return remote(self.place(j), self.place(j), self.sends.at[9, j], self.rF.at[j], {"x": 1 - self.x})

    def cH(self, j):
        return remote(self.res.at[j, self.core], self.res.at[j, self.core], self.sends.at[10, j], self.rH.at[j], self.C)

    def kept(self, j):
        return pltpu.make_async_copy(self.RX.at[j, self.z], self.place(j).at[self.z], self.loc.at[j])

    def add(self, j, i, part):
        self.RC[j, i] = self.RC[j, i] + part

    def stages(self, k, counts):
        z, x = self.z, self.x

        def meet(j):
            self.cB(j).wait_recv()
            self.RY[j] = self.RY[j] + self.RC[j, 1]
            self.cC(j).start()

        def scatter(j):
            self.cC(j).wait_recv()
            self.RX[j] = self.RX[j] + self.RY[j, x]
            for d in range(1, 4):
                self.cD(j, d).start()

        def gather(j):
            remote(self.RZ.at[j], self.RZ.at[j], self.sends.at[3, j], self.rD.at[j], {"z": (z + 1) % 4}).wait_recv()
            tot = self.RX[j, z].astype(f32)
            for d in range(3):
                tot = tot + self.RZ[j, d].astype(f32)
            self.RX[j, z] = tot.astype(bf16)
            for d in range(1, 4):
                self.cE(j, d).start()
            self.kept(j).start()

        def back_x(j):
            three = self.place(j).at[pl.ds(0, 3)]
            remote(three, three, self.sends.at[6, j], self.rE.at[j], {"z": (z + 1) % 4}).wait_recv()
            self.kept(j).wait()
            self.cF(j).start()

        def back_core(j):
            self.cF(j).wait_recv()
            self.cH(j).start()

        def done(j):
            self.cH(j).wait_recv()
            self.cB(j).wait_send()
            self.cC(j).wait_send()
            for d in range(1, 4):
                self.cD(j, d).wait_send()
                self.cE(j, d).wait_send()
            self.cF(j).wait_send()
            self.cH(j).wait_send()

        for count, run in zip(counts, (meet, scatter, gather, back_x, back_core, done)):
            each(count, k, run)


def backward_kernel(h1T, gp, act, df, dno, dnp, upo, upp, qkvt, qkvl, lse, gains, dcl, ldr1, wql, xlT, lay1, lay2,
                    sums, lsums, lbsum, dr2, a_n1, a_rs1, a_wout, a_woutp, a_wq, a_wqp, a_ctx, a_x,
                    res_f, res_a, gx, gxlT,
                    dh1, n1, rs1, wout, woutp, wq, wqp, ctx, xs, dab, daT, bsum, sums1, DQ, DQL, dct_s, klT_s, avl, akl, dqT, dqlT,
                    small, PF, PA, *ring_refs):
    k = pl.program_id(0)
    z, x, core, mp = (lax.axis_index(a) for a in ("z", "x", "core", "mp"))
    ini = ring_refs[-1]
    feed = Ring(ring_refs[0:4] + (res_f,) + ring_refs[8:18], (z, x, core, mp))
    att = Ring(ring_refs[4:8] + (res_a,) + ring_refs[18:28], (z, x, core, mp))

    def loads(i):
        a, b = ((dr2, dh1), (a_n1, n1), (a_rs1, rs1), (a_wout, wout), (a_woutp, woutp), (a_wq, wq), (a_wqp, wqp),
                (a_ctx, ctx), (a_x, xs))[i]
        return pltpu.make_async_copy(a, b, ini.at[i])

    @pl.when(k == 0)
    def _():
        for i in range(9):
            loads(i).start()
        bar = pltpu.get_barrier_semaphore()
        for who in ({"core": 1 - core}, {"mp": 1 - mp}, {"x": 1 - x}):
            pl.semaphore_signal(bar, inc=1, device_id=who, device_id_type=MESH)
        for d in range(1, 4):
            pl.semaphore_signal(bar, inc=1, device_id={"z": (z + d) % 4}, device_id_type=MESH)
        pl.semaphore_wait(bar, 6)
        loads(0).wait()

    @pl.when(k == FEED)
    def _():
        for i in range(1, 9):
            loads(i).wait()

    def feed_A(j):
        return remote(PF.at[1 - core], feed.RC.at[j], feed.sends.at[0, j], feed.rA.at[j], feed.C)

    def att_A(j):
        return remote(PA.at[j % 2, 1 - core], att.RC.at[j], att.sends.at[0, j], att.rA.at[j], att.C)

    def feed_B(j):
        feed_A(j).wait_recv()
        for i in range(2):
            feed.add(j, i, PF[core, i])
        feed.cB(j).start()
        feed_A(j).wait_send()

    def att_B(j):
        att_A(j).wait_recv()
        for i in range(2):
            att.add(j, i, PA[j % 2, core, i])
        att.cB(j).start()
        att_A(j).wait_send()

    each(feed_made, k - 1, feed_B)
    each(att_made, k - 1, att_B, 2)

    def put(h, i, t):
        t = t.astype(bf16).reshape(2, 2, 4, 16, WIDE)
        PA[i % 2, 0, 1 - h] = t[0]
        PA[i % 2, 1, 1 - h] = t[1]

    dns, ups = (dno, dnp), (upo, upp)

    @pl.when(k < FEED)
    def _():
        dps = []
        for h in range(2):
            dp = (dot_nt(df[...], dns[h][...]) * gp[h].astype(f32)).astype(bf16)
            bsum[h, pl.ds(k, 1), :] = colsum(dp.astype(f32))
            t = dot(h1T[...], dp).astype(bf16)
            PF[0, 1 - h] = jnp.concatenate([t[0:256], t[256:512], t[512:768]], axis=1).reshape(2, 4, 32, WIDE)
            PF[1, 1 - h] = dot_tn(act[h], df[...]).astype(bf16).reshape(2, 4, 32, WIDE)
            dps.append(dp)
        dp = jnp.concatenate(dps, axis=1)
        up = jnp.concatenate([upo[...], upp[...]], axis=1)
        for r in range(2):
            rs = slice(512 * r, 512 * r + 512)
            dh1[rs, :] = dh1[rs, :] + dot_nt(dp[rs, :], up)

    def two(h, rows, cols, right):
        lo, hi = rows
        return jnp.concatenate([dot(cols[lo:hi, :], right), dot(cols[384 + lo:384 + hi, :], right)], axis=1)

    def pair_rows(h, p, lo, hi):
        return two(h, (lo, hi), xs, jnp.concatenate([DQ[h, 0, p], DQ[h, 1, p], DQ[h, 2, p]], axis=1))

    def make(h, i):
        stack = lambda *v: jnp.concatenate(v, axis=0)
        if i == 0:
            t = two(h, (0, 256), daT, ctx[h])
        elif i == 1:
            t = stack(two(h, (256, 384), daT, ctx[h]), jnp.concatenate([lay1[h, 0:128], lay2[h, 0:128, 0:384]], axis=1))
        elif i == 2:
            t = stack(jnp.concatenate([lay1[h, 128:192], lay2[h, 128:192, 0:384]], axis=1), jnp.zeros((64, WIDE), f32),
                      pair_rows(h, 0, 0, 128))
        elif i == 3:
            t = pair_rows(h, 0, 128, 384)
        elif i == 4:
            t = pair_rows(h, 1, 0, 256)
        elif i == 5:
            t = stack(pair_rows(h, 1, 256, 384), pair_rows(h, 2, 0, 128))
        elif i == 6:
            t = pair_rows(h, 2, 128, 384)
        else:
            for pg in range(T_PAGES):
                rs = slice(SEQ * pg, SEQ * pg + SEQ)
                DQL[h, 0, rs, :] = dqlT[2 * h + pg].T.astype(bf16)
                DQL[h, 1, rs, :] = akl[2 * h + pg].astype(bf16)
                DQL[h, 2, rs, :] = avl[2 * h + pg].astype(bf16)
            xT = xlT[...]
            t = jnp.concatenate([dot(xT, DQL[h, 0]), dot(xT, DQL[h, 1]), dot(xT, DQL[h, 2]), lay2[h, :, 384:512],
                                 jnp.zeros((192, 256), f32)], axis=1)
            small[...] = jnp.zeros_like(small)
            for r, v in enumerate((sums1[0:1, :], sums[0:1, :], sums1[1:2, :], sums[1:2, :], sums1[2:3, :], sums[2:3, :])):
                small[r:r + 1, :] = v
            small[6:12, 0:192] = lsums[0:6, :]
            for n, c in enumerate((0, 2)):
                for p in range(3):
                    at = 384 * n + 128 * p
                    small[12:13, at:at + 128] = colsum(DQ[h, c, p].astype(f32))
                small[13:14, 128 * n:128 * n + 128] = colsum(DQL[h, c].astype(f32))
            for b in range(6):
                small[14 + b // 3:15 + b // 3, 256 * (b % 3):256 * (b % 3) + 256] = bsum[h, b:b + 1, :]
            small[16:17, 0:384] = lbsum[h]
            t = stack(t, small[...])
        put(h, i, t)

    for at in sorted(set(ATT_MADE)):
        @pl.when(k == at)
        def _(at=at):
            for i in range(N_ATT):
                if ATT_MADE[i] == at:
                    @pl.loop(0, 2)
                    def _(h, i=i):
                        make(h, i)

    each(feed_made, k, lambda j: feed_A(j).start())
    each(att_made, k, lambda j: att_A(j).start(), 2)

    @pl.when(k == FEED)
    def _():
        s1 = s2 = s3 = None
        for r in range(4):
            rs = slice(256 * r, 256 * r + 256)
            g = dh1[rs, :]
            n = n1[rs, :].astype(f32)
            d = norm_back(g * gains[0:1], n, rs1[rs, 0:1])
            dh1[rs, :] = d
            db = d.astype(bf16)
            dab[rs, :] = db
            daT[:, rs] = db.T
            t1, t2, t3 = colsum(g * n), colsum(g), colsum(d)
            s1, s2, s3 = (t1, t2, t3) if s1 is None else (s1 + t1, s2 + t2, s3 + t3)
        sums1[...] = jnp.concatenate([s1, s2, s3, jnp.zeros((5, WIDE), f32)], axis=0)

    @pl.when((k >= FEED) & (k < ATT))
    def _():
        a = k - FEED
        pair = a // 4
        hf = 1 - (a % 4) // 2
        page = a % 2
        at = 2 * hf + page
        rs = pl.ds(pl.multiple_of(page * SEQ, SEQ), SEQ)

        @pl.when(pair == 0)
        def _():
            avl[at] = jnp.zeros((SEQ, 128), f32)
            akl[at] = jnp.zeros((SEQ, 128), f32)
            dqlT[at] = jnp.zeros((128, SEQ), f32)

        ws = pl.ds(pl.multiple_of(pair * 128, 128), 128)
        for h, w in enumerate((wout, woutp)):
            @pl.when(hf == h)
            def _(w=w):
                dct_s[...] = dot_nt(dab[rs, :], w[ws, :]).astype(bf16)

        klT_s[...] = qkvl[0, 1].T
        qc = jnp.concatenate([qkvt[0, 0, 0], qkvl[0, 0]], axis=1)
        kc = jnp.concatenate([qkvt[0, 1, 0], qkvl[0, 1]], axis=1)
        vc = jnp.concatenate([qkvt[0, 2, 0], qkvl[0, 2]], axis=1)
        dc = jnp.concatenate([dct_s[...], dcl[0]], axis=1)
        ktT = qkvt[0, 1, 0].T
        zero = jnp.zeros_like(kc)
        av = ak = None
        for hh in range(2):
            h = 2 * pair + hh
            lane = lax.broadcasted_iota(jnp.int32, (1, 256), 1)
            mv = ((lane >= 64 * hh) & (lane < 64 * hh + 64)) | ((lane >= 128 + 16 * h) & (lane < 144 + 16 * h))
            mk = mv | (lane == 224)
            E = jnp.exp(dot_nt(jnp.where(mk, kc, zero), qc) - lse[0, 0, pl.ds(h, 1), :])
            dP = dot_nt(jnp.where(mv, vc, zero), dc)
            X = E * dP
            dS = (X - E * colsum(X)).astype(bf16)
            ov = dot(E.astype(bf16), jnp.where(mv, dc, zero))
            ok = dot(dS, jnp.where(mv, qc, zero))
            av = ov[:, :128] if av is None else av + ov[:, :128]
            ak = ok[:, :128] if ak is None else ak + ok[:, :128]
            avl[at] += ov[:, 128:]
            akl[at] += ok[:, 128:]
            ls = pl.ds(pl.multiple_of(16 * h, 16), 16)
            kT = jnp.concatenate([ktT[64 * hh:64 * hh + 64], klT_s[ls, :]], axis=0)
            oq = dot(kT, dS)
            dqT[64 * hh:64 * hh + 64, :] = oq[:64] * 0.125
            dqlT[at, ls, :] = oq[64:] * 0.25
        DQ[hf, 0, pair, rs, :] = dqT[...].T.astype(bf16)
        DQ[hf, 1, pair, rs, :] = ak.astype(bf16)
        DQ[hf, 2, pair, rs, :] = av.astype(bf16)

    @pl.when((k >= GRADS) & (k < GRADS + 4))
    def _():
        rs = pl.ds(pl.multiple_of((k - GRADS) * 256, 256), 256)
        g = dh1[rs, :]
        gl = ldr1[...]
        for h in range(2):
            for c in range(3):
                g = g + dot_nt(jnp.concatenate([DQ[h, c, p, rs, :] for p in range(3)], axis=1), (wq, wqp)[h][c])
                gl = gl + dot_nt(DQL[h, c, rs, :], wql[h, c])
        gx[...] = g
        gxlT[...] = gl.T

    feed.stages(k, [functools.partial(by_table, t) for t in FEED_STEPS])
    att.stages(k, [functools.partial(by_table, t) for t in ATT_STEPS])


def backward(h1T, gp, act, df, dno, dnp, upo, upp, qkvt, qkvl, lse, x, n1, rs1, gains, dcl, ldr1, wout, woutp, wq, wqp, wql,
             ctx, xlT, lay1, lay2, sums, lsums, lbsum, dr2):
    T = n1.shape[0]
    blk = lambda k: clip(k, 0, FEED - 1)
    att = lambda k: clip(k - FEED, 0, 11)
    head = lambda k: (1 - (att(k) % 4) // 2, att(k) % 2, att(k) // 4)
    D = pltpu.SemaphoreType.DMA
    V = pltpu.VMEM
    sd = jax.ShapeDtypeStruct
    hid = pl.BlockSpec((2, T, 256), lambda k: (0, 0, blk(k)))
    rowb = pl.BlockSpec((256, WIDE), lambda k: (blk(k), 0))
    colb = pl.BlockSpec((WIDE, 256), lambda k: (0, blk(k)))
    grow = lambda k: clip(k - GRADS, 0, 3)
    anyspec = pl.BlockSpec(memory_space=pl.ANY)
    in_specs = [
        whole(h1T), hid, hid, whole(df), rowb, rowb, colb, colb,
        pl.BlockSpec((1, 3, 1, SEQ, 128), lambda k: (head(k)[0], 0, head(k)[2], head(k)[1], 0)),
        pl.BlockSpec((1, 3, SEQ, 128), lambda k: (head(k)[0], 0, head(k)[1], 0)),
        pl.BlockSpec((1, 1, 8, SEQ), lambda k: (head(k)[0], head(k)[1], 0, 0)),
        whole(gains),
        pl.BlockSpec((1, SEQ, 128), lambda k: (head(k)[0], head(k)[1], 0)),
        pl.BlockSpec((256, 192), lambda k: (grow(k), 0)),
    ] + [whole(a) for a in (wql, xlT, lay1, lay2, sums, lsums, lbsum)] + [anyspec] * 9
    bufs = lambda n, r: [V((n, 2, 2, 4, r, WIDE), bf16), V((n, 2, 4, r, WIDE), bf16), V((n, 4, r, WIDE), bf16),
                         V((n, 3, r, WIDE), bf16)]
    sems = lambda n: [D((12, n))] + [D((n,))] * 9
    return pl.pallas_call(
        backward_kernel,
        grid=(BWD_STEPS,),
        in_specs=in_specs,
        out_specs=[anyspec, anyspec,
                   pl.BlockSpec((256, WIDE), lambda k: (grow(k), 0)),
                   pl.BlockSpec((192, 256), lambda k: (0, grow(k)))],
        out_shape=[sd((N_FEED, 2, 2, 4, 32, WIDE), bf16), sd((N_ATT, 2, 2, 4, 16, WIDE), bf16), sd((T, WIDE), f32),
                   sd((192, T), f32)],
        scratch_shapes=[
            V((T, WIDE), f32), V((T, WIDE), bf16), V((T, 128), f32), V((384, WIDE), bf16), V((384, WIDE), bf16),
            V((3, WIDE, 384), bf16), V((3, WIDE, 384), bf16), V((2, T, 384), bf16), V((WIDE, T), bf16),
            V((T, WIDE), bf16), V((WIDE, T), bf16), V((2, 8, 256), f32), V((8, WIDE), f32),
            V((2, 3, 3, T, 128), bf16), V((2, 3, T, 128), bf16), V((SEQ, 128), bf16),
            V((128, SEQ), bf16), V((4, SEQ, 128), f32), V((4, SEQ, 128), f32), V((128, SEQ), f32), V((4, 128, SEQ), f32),
            V((64, WIDE), f32),
            V((2, 2, 2, 4, 32, WIDE), bf16), V((2, 2, 2, 2, 4, 16, WIDE), bf16)]
        + bufs(N_FEED, 32) + bufs(N_ATT, 16) + sems(N_FEED) + sems(N_ATT) + [D((9,))],
        compiler_params=pltpu.CompilerParams(collective_id=0, has_side_effects=True, vmem_limit_bytes=63 << 20),
        name="backward",
    )(h1T, gp, act, df, dno, dnp, upo, upp, qkvt, qkvl, lse, gains, dcl, ldr1, wql, xlT, lay1, lay2, sums, lsums, lbsum, dr2,
      n1, rs1, wout, woutp, wq, wqp, ctx, x)


def unpack_kernel(rf, r, up, dn, qkv, out, lqkv, lup, ldnT, lout, qvb, upb, gain, shift, lqvb, lupb, lgain, lshift):
    k = pl.program_id(0)

    @pl.when(k < 6)
    def _():
        for i in range(3):
            up[256 * i:256 * i + 256, :] = rf[0:256, 256 * i:256 * i + 256].astype(f32)
        dn[...] = rf[256:512, :].astype(f32)

    def put_pair(p, lo, a):
        for i in range(2):
            rows = slice(384 * i + lo, 384 * i + lo + a.shape[0])
            for c in range(3):
                qkv[c, rows, 128 * p:128 * p + 128] = a[:, 384 * i + 128 * c:384 * i + 128 * c + 128].astype(f32)

    @pl.when(k == 6)
    def _():
        for i in range(2):
            out[:, 384 * i:384 * i + 384] = r[0:384, 384 * i:384 * i + 384].astype(f32).T
        lup[0:128, :] = r[384:512, 0:384].astype(f32)
        ldnT[0:128, :] = r[384:512, 384:768].astype(f32)

    @pl.when(k == 7)
    def _():
        lup[128:192, :] = r[0:64, 0:384].astype(f32)
        ldnT[128:192, :] = r[0:64, 384:768].astype(f32)
        put_pair(0, 0, r[128:512, :])

    @pl.when(k == 8)
    def _():
        put_pair(1, 0, r[0:384, :])
        put_pair(2, 0, r[384:512, :])

    @pl.when(k == 9)
    def _():
        put_pair(2, 128, r[0:256, :])
        for c in range(3):
            lqkv[c] = r[256:448, 128 * c:128 * c + 96].astype(f32)
        lout[...] = r[256:448, 384:512].astype(f32).T[:96, :]
        s = r[448:480, :].astype(f32)
        gain[...] = s[0:2]
        shift[...] = s[2:6]
        lgain[...] = s[6:8, 0:192]
        lshift[...] = s[8:12, 0:192]
        for i in range(2):
            qvb[i:i + 1, :] = s[12:13, 384 * i:384 * i + 384]
            lqvb[i:i + 1, :] = s[13:14, 128 * i:128 * i + 96]
            for j in range(6):
                upb[6 * i + j:6 * i + j + 1, :] = s[14 + i:15 + i, 128 * j:128 * j + 128]
        for j in range(3):
            lupb[j:j + 1, :] = s[16:17, 128 * j:128 * j + 128]


def unpack(feed, att):
    const = lambda s: pl.BlockSpec(s, lambda k: (0,) * len(s))
    sd = jax.ShapeDtypeStruct
    shapes = [(768, 1536), (1536, 768), (3, 768, 384), (384, 768), (3, 192, 96), (192, 384), (192, 384), (96, 192),
              (2, 384), (12, 128), (2, 768), (4, 768), (2, 96), (3, 128), (2, 192), (4, 192)]
    specs = [const(s) for s in shapes]
    specs[0] = pl.BlockSpec((768, 256), lambda k: (0, clip(k, 0, 5)))
    specs[1] = pl.BlockSpec((256, 768), lambda k: (clip(k, 0, 5), 0))
    return pl.pallas_call(
        unpack_kernel, grid=(10,),
        in_specs=[pl.BlockSpec((512, 768), lambda k: (clip(k, 0, 5), 0)), pl.BlockSpec((512, 768), lambda k: (clip(k - 6, 0, 3), 0))],
        out_specs=specs, out_shape=[sd(s, f32) for s in shapes],
        compiler_params=pltpu.CompilerParams(vmem_limit_bytes=56 << 20), name="unpack_gradients",
    )(feed, att)


def body(n_group, text_states, layout_states, box_counts, text_qkv, text_qv_bias, text_out, text_up, text_up_bias,
         text_down, text_gains, text_shifts, layout_qkv, layout_qv_bias, layout_out, layout_up, layout_up_bias,
         layout_down, layout_gains, layout_shifts, cot_text, cot_layout):
    tq = jnp.transpose(text_qkv, (1, 0, 2))
    lq = jnp.transpose(layout_qkv, (1, 0, 2))
    xlT = layout_states.T
    (qkvt, qkvl, lse, ctx, out_lT, ldr1, dcl, lay1, lay2, lsums, lbsum, lqp, out_t, act, gp, h1T, xT, df, dr2, n1, rs1, sums,
     wq, wo, wu, wd) = forward(
        box_counts, text_states, xlT, tq, lq, text_out, layout_out, layout_up, layout_down.T, text_up, text_down,
        text_qv_bias, layout_qv_bias, text_up_bias.reshape(12, 128), layout_up_bias.reshape(3, 128), layout_gains,
        layout_shifts, cot_layout.T, text_gains, text_shifts, cot_text)
    feed, att, gx, gxlT = backward(h1T, gp, act, df, text_down, wd, text_up, wu, qkvt, qkvl, lse, xT, n1, rs1,
                             text_gains, dcl, ldr1, text_out, wo, tq, wq, lqp, ctx, xlT, lay1, lay2, sums, lsums, lbsum,
                             dr2)
    feed = feed.reshape(N_FEED * 512, WIDE)
    att = att.reshape(N_ATT * 256, WIDE)
    if n_group > 1:
        feed, att = lax.psum((feed, att), "group")
    (g_up, g_dn, g_qkv, g_o, gl_qkv, gl_up, gl_dnT, gl_o, qvb, upb, gain, shift, lqvb, lupb, lgain, lshift) = unpack(feed, att)
    swap = lambda a: jnp.transpose(a, (1, 0, 2))
    return (out_t, out_lT.T, gx, gxlT.T, swap(g_qkv), qvb, g_o, g_up, upb.reshape(1536), g_dn, gain, shift,
            swap(gl_qkv), lqvb, gl_o, gl_up, lupb.reshape(384), gl_dnT.T, lgain, lshift)


def solution(mesh):
    dp = mesh.shape["dp"]
    n_group = dp // 16
    fine = Mesh(mesh.devices.reshape(n_group, 4, 2, 2, 2), AXES)
    rows = P(AXES, None)
    half2 = P(None, "mp")
    half1 = P("mp", None)
    qkv = P(None, None, "mp")
    rep = P()
    return jax.shard_map(
        functools.partial(body, n_group),
        mesh=fine,
        in_specs=(rows, rows, P(AXES[:4]), qkv, half2, half1, half2, P("mp"), half1, rep, rep,
                  qkv, half2, half1, half2, P("mp"), half1, rep, rep, rows, rows),
        out_specs=(rows, rows, rows, rows, qkv, half2, half1, half2, P("mp"), half1, rep, rep,
                   qkv, half2, half1, half2, P("mp"), half1, rep, rep),
        check_vma=False,
    )
```

```python
import functools

import jax
import jax.numpy as jnp
from jax import lax
from jax.experimental import pallas as pl
from jax.experimental.pallas import tpu as pltpu
from jax.sharding import Mesh, PartitionSpec as P

f32 = jnp.float32
bf16 = jnp.bfloat16
SEQ = 512
NT = (((1,), (1,)), ((), ()))
TN = (((0,), (0,)), ((), ()))
AXES = ("group", "z", "x", "core", "mp")
MESH = pl.DeviceIdType.MESH
WIDE = 768


def dot(a, b):
    return jnp.dot(a, b, preferred_element_type=f32)


def dot_nt(a, b):
    return lax.dot_general(a, b, NT, preferred_element_type=f32)


def dot_tn(a, b):
    return lax.dot_general(a, b, TN, preferred_element_type=f32)


def colsum(v):
    return jnp.sum(v, axis=0, keepdims=True)


def whole(a):
    return pl.BlockSpec(a.shape, lambda *i: (0,) * a.ndim, pipeline_mode=pl.Buffered(1))


GC = [0.11609199498651965, 0.07018864201817518, 0.2621979336040309, -0.22868178430415115, 0.38476147983842124,
      -0.10455825070574547]
GP = 0.28


def gelu_pair(v):
    t = 1.0 / (1.0 + GP * jnp.abs(v))
    g = jnp.exp(v * v * -0.5)
    q = GC[5]
    for c in GC[4::-1]:
        q = q * t + c
    q = q * t * g
    phi = jnp.where(v < 0, q, 1.0 - q)
    return v * phi, phi + v * g * 0.3989422804014327


def norm_stats(r):
    cen = r - jnp.mean(r, -1, keepdims=True)
    rstd = lax.rsqrt(jnp.mean(cen * cen, -1, keepdims=True) + 1e-5)
    return cen * rstd, rstd


def norm_back(e, n, rstd):
    return (e - jnp.mean(e, -1, keepdims=True) - n * jnp.mean(e * n, -1, keepdims=True)) * rstd


def head_masks(h):
    lane = lax.broadcasted_iota(jnp.int32, (1, 256), 1)
    t = (lane >= 64 * (h % 2)) & (lane < 64 * (h % 2) + 64)
    l = (lane >= 128 + 16 * h) & (lane < 128 + 16 * h + 16)
    return t | l, t | l | (lane == 224)


def row_of(b, at, n):
    return jnp.concatenate([b[i:i + 1, :] for i in range(at // 128, (at + n) // 128)], axis=1)


def clip(v, a, b):
    return jnp.minimum(jnp.maximum(v, a), b)


def remote(src, dst, s, r, who):
    return pltpu.make_async_remote_copy(src_ref=src, dst_ref=dst, send_sem=s, recv_sem=r, device_id=who,
                                        device_id_type=MESH)


def second_norm(r2, gains, shifts, ct):
    n2, rstd2 = norm_stats(r2)
    dr2 = norm_back(ct * gains[1:2], n2, rstd2)
    return n2 * gains[1:2] + shifts[1:2], dr2, (colsum(ct * n2), colsum(ct), colsum(dr2))


PIECES = 15
START = [0, 0, 0, 0, 2, 3, 3, 4, 5, 6, 7, 8, 9, 10, 11]
RELAY = [2, 4, 5, 5, 6, 6, 6, 7, 8, 9, 10, 12, 14, 15, 16]
AHEAD = [5, 6, 6, 6, 9, 9, 9, 10, 11, 12, 14, 15, 17, 18, 19]
TEXT = 6
TEXT2 = 10
FWD_STEPS = 14


def forward_kernel(cnt, xt, xlT, wq, lq, lo, lup, ldnT, bq, blq, bu, blu, lgains, lshifts, lcotT, x2, gains, shifts, cot,
                   a_wq, a_lq, a_wo, a_lup, a_ldnT, a_up, a_dn,
                   qkvt, qkvl, lse_o, ctxt, outT, ldr1, dcl, lay1, lay2, lsums, lbsum, lqp,
                   out, act, gp, h1T, x_T, dfo, dr2o, n1o, rso, sums, o_wq, o_wo, o_up, o_dn,
                   cT, clT, ctx_s, ctl, xl_s, lact, lgp, ldpre, lh1, ldf, lda, wq_v, lq_v, lup_v, ldnT_v, lo_p, lq_p,
                   wo_v, up_v, dn_v, wo_s, up_s, dn_s, h1_s, r2_s, obq, oblq, obu, oblu,
                   sy, ry, sx, rx, sc, rc, sd, rd, ss, rs_, loc, own):
    k = pl.program_id(0)
    x, core, mp = (lax.axis_index(a) for a in ("x", "core", "mp"))
    Y, X, C = {"mp": 1 - mp}, {"x": 1 - x}, {"core": 1 - core}
    q_me = 2 * x + core
    q_x = 2 * (1 - x) + core

    def cut(ref, q, n, sub, nsub):
        m = n // 4 // nsub
        return ref.at[pl.ds(pl.multiple_of(q * (n // 4) + sub * m, 16), m), :]

    def piece(i, q, mine):
        if i < 3:
            return cut((a_wq if mine else wq_v).at[i], q, 768, 0, 1)
        if i == 3:
            return (a_lq if mine else lq_v).at[:, pl.ds(pl.multiple_of(q * 48, 16), 48), :]
        if i == 4:
            return cut(a_wo if mine else wo_v, q, 384, 0, 1)
        if i == 5:
            return cut(a_lup if mine else lup_v, q, 192, 0, 1)
        if i == 6:
            return cut(a_ldnT if mine else ldnT_v, q, 192, 0, 1)
        if i < 11:
            return cut(a_up if mine else up_v, q, 768, i - 7, 4)
        return cut(a_dn if mine else dn_v, q, 1536, i - 11, 4)

    def over_y(i):
        return remote(piece(i, q_me, True), piece(i, q_me, False), sy.at[i], ry.at[i], Y)

    def over_x(i):
        return remote(piece(i, q_me, False), piece(i, q_me, False), sx.at[i], rx.at[i], X)

    def over_core(i):
        return remote(piece(i, q_me, False), piece(i, q_me, False), sc.at[i], rc.at[i], C)

    def over_core2(i):
        return remote(piece(i, q_x, False), piece(i, q_x, False), sd.at[i], rd.at[i], C)

    def arrived(i):
        over_core(i).wait_recv()
        over_core2(i).wait_recv()

    def small():
        pairs = ((bq, obq), (blq, oblq), (bu, obu), (blu, oblu), (lo, lo_p.at[1, 0:96]))
        return [remote(a, b, ss.at[i], rs_.at[i], Y) for i, (a, b) in enumerate(pairs)]

    def keep(i):
        a, b = ((wq_v, o_wq), (wo_v, o_wo), (up_v, o_up), (dn_v, o_dn))[i]
        return pltpu.make_async_copy(a, b, loc.at[i])

    def load_own():
        return [pltpu.make_async_copy(a, b, own.at[i]) for i, (a, b) in enumerate(
            ((a_wo, wo_s), (a_up, up_s), (a_dn, dn_s)))]

    @pl.when(k == 0)
    def _():
        lo_p[...] = jnp.zeros_like(lo_p)
        bar = pltpu.get_barrier_semaphore()
        for who in (C, Y, X):
            pl.semaphore_signal(bar, inc=1, device_id=who, device_id_type=MESH)
        pl.semaphore_wait(bar, 3)
        for c in small():
            c.start()

    def slot(step, s):
        @pl.when(k == step)
        def _():
            for i in range(PIECES):
                if START[i] == s:
                    over_y(i).start()
            for i in range(PIECES):
                if RELAY[i] == s:
                    over_y(i).wait_recv()
                    over_x(i).start()
                    over_core(i).start()
            for i in range(PIECES):
                if AHEAD[i] == s:
                    over_x(i).wait_recv()
                    over_core2(i).start()

    for st in range(4):
        slot(st, 3 * st)

    @pl.when(k == 0)
    def _():
        for c in load_own():
            c.start()
        lq_p[...] = jnp.zeros_like(lq_p)
        lo_p[0, 0:96, :] = lo[...]
        for c in range(3):
            lq_p[0, c, :, 0:96] = lq[c]
        lsums[...] = jnp.zeros_like(lsums)
        lbsum[...] = jnp.zeros_like(lbsum)

    @pl.when(k == 2)
    def _():
        for c in small():
            c.wait_recv()
        for i in range(4):
            arrived(i)
        for c in range(3):
            lq_p[1, c, :, 0:96] = lq_v[c]
        keep(0).start()

    @pl.when(k < 4)
    def _():
        hf = k // 2
        page = k % 2

        def project(w, b, lb):
            n = cnt[2 * mp + page]
            lane = lax.broadcasted_iota(jnp.int32, (SEQ, 128), 1)
            row = lax.broadcasted_iota(jnp.int32, (SEQ, 128), 0)
            for c in range(3):
                r = dot(xt[...], w[c])
                s = dot(xl_s[page], lq_p[hf, c])
                if c != 1:
                    r = r + b[c // 2:c // 2 + 1]
                    s = s + jnp.concatenate([lb[c // 2:c // 2 + 1], jnp.zeros((1, 32), f32)], axis=1)
                if c == 0:
                    r = r * 0.125
                    s = jnp.where(lane == 96, 1.0, s * 0.25)
                if c == 1:
                    s = jnp.where((lane == 96) & (row >= n), -1e30, s)
                for p in range(3):
                    qkvt[0, c, p] = r[:, 128 * p:128 * p + 128].astype(bf16)
                qkvl[0, c] = s.astype(bf16)

        @pl.when(hf == 0)
        def _():
            xl_s[page] = xlT[...].T
            project(wq, bq, blq)

        @pl.when(hf == 1)
        def _():
            project(wq_v, obq, oblq)

        rows = pl.ds(pl.multiple_of(page * SEQ, SEQ), SEQ)
        vlT = qkvl[0, 2].T
        for p in range(3):
            if p > 0:
                for st in range(4):
                    slot(st, 3 * st + p)
            qc = jnp.concatenate([qkvt[0, 0, p], qkvl[0, 0]], axis=1)
            kc = jnp.concatenate([qkvt[0, 1, p], qkvl[0, 1]], axis=1)
            vtT = qkvt[0, 2, p].T
            for hh in range(2):
                h = 2 * p + hh
                mk = head_masks(h)[1]
                S = dot_nt(jnp.where(mk, kc, jnp.zeros_like(kc)), qc)
                m = jnp.max(S, axis=0, keepdims=True)
                e = jnp.exp(S - m)
                l = colsum(e)
                vT = jnp.concatenate([vtT[64 * hh:64 * hh + 64], vlT[16 * h:16 * h + 16]], axis=0)
                o = dot(vT, e.astype(bf16)) * (1.0 / l)
                cT[64 * hh:64 * hh + 64, :] = o[:64]
                clT[16 * h:16 * h + 16, :] = o[64:]
                lse_o[0, 0, h:h + 1, :] = m + jnp.log(l)
            cv = cT[...].T.astype(bf16)
            ctxt[0, :, 128 * p:128 * p + 128] = cv
            ctx_s[hf, rows, 128 * p:128 * p + 128] = cv
        clT[96:, :] = jnp.zeros((32, SEQ), f32)
        ctl[hf, rows, :] = clT[...].T.astype(bf16)
        lse_o[0, 0, 6:8, :] = jnp.zeros((2, SEQ), f32)

    slot(4, 12)
    slot(5, 14)

    @pl.when(k == 4)
    def _():
        arrived(5)
        arrived(6)

    @pl.when((k == 4) | (k == 5))
    def _():
        page = k - 4
        rows = pl.ds(pl.multiple_of(page * SEQ, SEQ), SEQ)
        ups, dns, bs_ = (lup, lup_v), (ldnT, ldnT_v), (blu, oblu)

        attn = dot(ctl[0, rows, :], lo_p[0]) + dot(ctl[1, rows, :], lo_p[1])
        n1, rstd1 = norm_stats(xl_s[page].astype(f32) + attn + lshifts[2:3])
        h1 = n1 * lgains[0:1] + lshifts[0:1]
        h1b = h1.astype(bf16)
        r2 = h1 + lshifts[3:4]
        for h in range(2):
            if h == 1:
                slot(4, 13)
                slot(5, 15)
            ga, gd = gelu_pair(dot(h1b, ups[h][...]) + row_of(bs_[h], 0, 384))
            ab = ga.astype(bf16)
            lact[h, rows, :] = ab
            lgp[h] = gd
            r2 = r2 + dot_nt(ab, dns[h][...])
        o, dr2, (s_g2, s_s2, s_r2) = second_norm(r2, lgains[...], lshifts[...], lcotT[...].T.astype(f32))
        outT[...] = o.T.astype(bf16)
        df = dr2.astype(bf16)
        dh1 = dr2
        for h in range(2):
            dp = (dot(df, dns[h][...]) * lgp[h]).astype(bf16)
            ldpre[h, rows, :] = dp
            lbsum[h] += colsum(dp.astype(f32))
            dh1 = dh1 + dot_nt(dp, ups[h][...])
        d1 = norm_back(dh1 * lgains[0:1], n1, rstd1)
        ldr1[...] = d1
        db = d1.astype(bf16)
        lh1[rows, :] = h1b
        ldf[rows, :] = df
        lda[rows, :] = db
        for h in range(2):
            dcl[h] = dot_nt(db, lo_p[h]).astype(bf16)
        lsums[...] += jnp.concatenate([colsum(dh1 * n1), s_g2, colsum(dh1), s_s2, colsum(d1), s_r2,
                                       jnp.zeros((2, 192), f32)], axis=0)

    @pl.when(k == 5)
    def _():
        hT = lh1[...].T
        fT = ldf[...].T
        aT = lda[...].T
        for h in range(2):
            lay1[h] = dot(hT, ldpre[h])
            lay2[h, :, 0:384] = dot(fT, lact[h])
            lay2[h, :, 384:512] = dot(aT, ctl[h])
            for c in range(3):
                lqp[h, c] = lq_p[h, c]

    for i in range(4):
        slot(TEXT + i, 16 + i)

    @pl.when(k == TEXT)
    def _():
        for c in load_own():
            c.wait()
        arrived(4)
        sums[...] = jnp.zeros_like(sums)

    def units(h1b, up, dn, b):
        r = None
        for c in range(2):
            cs = slice(768 * c, 768 * c + 768)
            ga, gd = gelu_pair(dot(h1b, up[:, cs]) + row_of(b, 768 * c, 768))
            ab = ga.astype(bf16)
            act[0, :, cs] = ab
            gp[0, :, cs] = gd.astype(bf16)
            t = dot(ab, dn[cs, :])
            r = t if r is None else r + t
        return r

    @pl.when((k >= TEXT) & (k < TEXT2))
    def _():
        rows = pl.ds(pl.multiple_of((k - TEXT) * 256, 256), 256)
        attn = dot(ctx_s[0, rows, :], wo_s[...]) + dot(ctx_s[1, rows, :], wo_v[...])
        n1, rstd1 = norm_stats(x2[...].astype(f32) + attn + shifts[2:3])
        n1o[...] = n1.astype(bf16)
        rso[...] = jnp.broadcast_to(rstd1, (256, 128))
        h1 = n1 * gains[0:1] + shifts[0:1]
        h1b = h1.astype(bf16)
        h1_s[rows, :] = h1b
        h1T[...] = h1b.T
        x_T[...] = x2[...].T
        r2_s[rows, :] = h1 + shifts[3:4] + units(h1b, up_s, dn_s, bu)

    @pl.when(k == TEXT2)
    def _():
        for i in range(7, PIECES):
            arrived(i)
        for i in range(1, 4):
            keep(i).start()

    @pl.when(k >= TEXT2)
    def _():
        rows = pl.ds(pl.multiple_of((k - TEXT2) * 256, 256), 256)
        r2 = r2_s[rows, :] + units(h1_s[rows, :], up_v, dn_v, obu)
        o, dr2, (s_g2, s_s2, s_r2) = second_norm(r2, gains[...], shifts[...], cot[...].astype(f32))
        out[...] = o.astype(bf16)
        dfo[...] = dr2.astype(bf16)
        dr2o[...] = dr2
        sums[...] += jnp.concatenate([s_g2, s_s2, s_r2, jnp.zeros((5, 768), f32)], axis=0)

    @pl.when(k == FWD_STEPS - 1)
    def _():
        for i in range(PIECES):
            over_y(i).wait_send()
            over_x(i).wait_send()
            over_core(i).wait_send()
            over_core2(i).wait_send()
        for c in small():
            c.wait_send()
        for i in range(4):
            keep(i).wait()


def forward(cnt, xt, xlT, wq, lq, wo, lo, lup, ldnT, up, dn, bq, blq, bu, blu, lgains, lshifts, lcotT, gains, shifts, cot):
    T = xt.shape[0]
    n = T // SEQ
    hf = lambda k: clip(k, 0, 3) // 2
    pg = lambda k: clip(k, 0, 3) % 2
    lp = lambda k: clip(k - 4, 0, 1)
    tb = lambda k: clip(k - TEXT, 0, 3)
    anyspec = pl.BlockSpec(memory_space=pl.ANY)
    const = lambda s: pl.BlockSpec(s, lambda k, *_: (0,) * len(s))
    V = pltpu.VMEM
    D = pltpu.SemaphoreType.DMA
    sds = jax.ShapeDtypeStruct
    tb2 = lambda k: clip(k - TEXT2, 0, 3)
    tc = lambda k: clip(k - TEXT, 0, 7)
    trow = pl.BlockSpec((256, 768), lambda k, *_: (tb(k), 0))
    trow2 = pl.BlockSpec((256, 768), lambda k, *_: (tb2(k), 0))
    trow3 = pl.BlockSpec((1, 256, 1536), lambda k, *_: (tc(k) // 4, tc(k) % 4, 0))
    lcol = pl.BlockSpec((192, SEQ), lambda k, *_: (0, lp(k)))
    return pl.pallas_call(
        forward_kernel,
        grid_spec=pltpu.PrefetchScalarGridSpec(
            num_scalar_prefetch=1, grid=(FWD_STEPS,),
            in_specs=[pl.BlockSpec((SEQ, 768), lambda k, *_: (pg(k), 0)),
                      pl.BlockSpec((192, SEQ), lambda k, *_: (0, pg(k)))]
            + [whole(a) for a in (wq, lq, lo, lup, ldnT, bq, blq, bu, blu, lgains, lshifts)]
            + [lcol, trow, whole(gains), whole(shifts), trow2] + [anyspec] * 7,
            out_specs=[pl.BlockSpec((1, 3, 3, SEQ, 128), lambda k, *_: (hf(k), 0, 0, pg(k), 0)),
                       pl.BlockSpec((1, 3, SEQ, 128), lambda k, *_: (hf(k), 0, pg(k), 0)),
                       pl.BlockSpec((1, 1, 8, SEQ), lambda k, *_: (hf(k), pg(k), 0, 0)),
                       pl.BlockSpec((1, SEQ, 384), lambda k, *_: (hf(k), pg(k), 0)),
                       lcol, pl.BlockSpec((SEQ, 192), lambda k, *_: (lp(k), 0)),
                       pl.BlockSpec((2, SEQ, 128), lambda k, *_: (0, lp(k), 0)),
                       const((2, 192, 384)), const((2, 192, 512)), const((8, 192)), const((2, 1, 384)),
                       const((2, 3, 192, 128)),
                       trow2, trow3, trow3, pl.BlockSpec((768, 256), lambda k, *_: (0, tb(k))), pl.BlockSpec((768, 256), lambda k, *_: (0, tb(k))),
                       trow2, trow2, trow,
                       pl.BlockSpec((256, 128), lambda k, *_: (tb(k), 0)), const((8, 768)),
                       anyspec, anyspec, anyspec, anyspec],
            scratch_shapes=[
                V((128, SEQ), f32), V((128, SEQ), f32), V((2, T, 384), bf16), V((2, T, 128), bf16),
                V((n, SEQ, 192), bf16), V((2, T, 384), bf16), V((2, SEQ, 384), f32), V((2, T, 384), bf16),
                V((T, 192), bf16), V((T, 192), bf16), V((T, 192), bf16),
                V((3, 768, 384), bf16), V((3, 192, 96), bf16), V((192, 384), bf16), V((192, 384), bf16),
                V((2, 128, 192), bf16), V((2, 3, 192, 128), bf16),
                V((384, 768), bf16), V((768, 1536), bf16), V((1536, 768), bf16),
                V((384, 768), bf16), V((768, 1536), bf16), V((1536, 768), bf16),
                V((T, 768), bf16), V((T, 768), f32), V((2, 384), f32), V((2, 96), f32), V((12, 128), f32), V((3, 128), f32)]
            + [D((PIECES,))] * 8 + [D((5,)), D((5,)), D((4,)), D((3,))]),
        out_shape=[sds((2, 3, 3, T, 128), bf16), sds((2, 3, T, 128), bf16), sds((2, n, 8, SEQ), f32),
                   sds((2, T, 384), bf16), sds((192, T), bf16), sds((T, 192), f32), sds((2, T, 128), bf16),
                   sds((2, 192, 384), f32), sds((2, 192, 512), f32), sds((8, 192), f32), sds((2, 1, 384), f32),
                   sds((2, 3, 192, 128), bf16),
                   sds((T, 768), bf16), sds((2, T, 1536), bf16), sds((2, T, 1536), bf16), sds((768, T), bf16), sds((768, T), bf16),
                   sds((T, 768), bf16), sds((T, 768), f32), sds((T, 768), bf16), sds((T, 128), f32), sds((8, 768), f32),
                   sds((3, 768, 384), bf16), sds((384, 768), bf16), sds((768, 1536), bf16), sds((1536, 768), bf16)],
        compiler_params=pltpu.CompilerParams(collective_id=1, has_side_effects=True, vmem_limit_bytes=62 << 20),
        name="forward",
    )(cnt, xt, xlT, wq, lq, lo, lup, ldnT, bq, blq, bu, blu, lgains, lshifts, lcotT, xt, gains, shifts, cot,
      wq, lq, wo, lup, ldnT, up, dn)


FEED = 6
T_PAGES = 2
ATT = FEED + 12
GRADS = ATT + 2
BWD_STEPS = ATT + 11
N_FEED = 6
T_PAGES = 2
N_ATT = 8
FEED_STEPS = ((3, 5, 7, 9, 11, 14), (4, 6, 9, 11, 14, 17), (5, 8, 12, 14, 17, 19), (6, 11, 15, 17, 19, 20),
              (8, 14, 17, 19, 20, 21), (10, 16, 18, 20, 21, 22))
ATT_MADE = (FEED + 1, FEED + 1, FEED + 4, FEED + 4, FEED + 8, ATT, ATT, ATT + 1)
ATT_STEPS = ((14, 15, 16, 17, 19, 20, 21, 22), (16, 17, 18, 19, 20, 21, 22, 23), (18, 19, 20, 21, 22, 23, 24, 25),
             (19, 20, 21, 22, 23, 24, 25, 26), (20, 21, 22, 23, 24, 25, 26, 27), (21, 22, 23, 24, 25, 26, 27, 28))


def by_table(table, k):
    return sum((k >= t).astype(jnp.int32) for t in table)


def feed_made(k):
    return clip(k + 1, 0, N_FEED)


def att_made(k):
    return by_table(ATT_MADE, k)


def each(count, k, run, most=1):
    now, before = count(k), count(k - 1)
    for d in range(most, 0, -1):
        @pl.when(now - before >= d)
        def _(d=d):
            run(now - d)


class Ring:
    def __init__(self, bufs, where):
        (self.RC, self.RY, self.RX, self.RZ, self.res, self.sends, self.rA, self.rO, self.rB, self.rC, self.rD, self.rE,
         self.rF, self.rH, self.loc) = bufs
        self.z, self.x, self.core, self.mp = where
        self.C = {"core": 1 - self.core}

    def cB(self, j):
        return remote(self.RC.at[j, 0], self.RY.at[j], self.sends.at[1, j], self.rB.at[j], {"mp": 1 - self.mp})

    def cC(self, j):
        return remote(self.RY.at[j, 1 - self.x], self.RX.at[j], self.sends.at[2, j], self.rC.at[j], {"x": 1 - self.x})

    def cD(self, j, d):
        t = (self.z + d) % 4
        return remote(self.RX.at[j, t], self.RZ.at[j, 3 - d], self.sends.at[2 + d, j], self.rD.at[j], {"z": t})

    def place(self, j):
        return self.res.at[j, self.core, self.x]

    def cE(self, j, d):
        t = (self.z + d) % 4
        return remote(self.RX.at[j, self.z], self.place(j).at[self.z], self.sends.at[5 + d, j], self.rE.at[j], {"z": t})

    def cF(self, j):
        return remote(self.place(j), self.place(j), self.sends.at[9, j], self.rF.at[j], {"x": 1 - self.x})

    def cH(self, j):
        return remote(self.res.at[j, self.core], self.res.at[j, self.core], self.sends.at[10, j], self.rH.at[j], self.C)

    def kept(self, j):
        return pltpu.make_async_copy(self.RX.at[j, self.z], self.place(j).at[self.z], self.loc.at[j])

    def add(self, j, i, part):
        self.RC[j, i] = self.RC[j, i] + part

    def stages(self, k, counts):
        z, x = self.z, self.x

        def meet(j):
            self.cB(j).wait_recv()
            self.RY[j] = self.RY[j] + self.RC[j, 1]
            self.cC(j).start()

        def scatter(j):
            self.cC(j).wait_recv()
            self.RX[j] = self.RX[j] + self.RY[j, x]
            for d in range(1, 4):
                self.cD(j, d).start()

        def gather(j):
            remote(self.RZ.at[j], self.RZ.at[j], self.sends.at[3, j], self.rD.at[j], {"z": (z + 1) % 4}).wait_recv()
            tot = self.RX[j, z].astype(f32)
            for d in range(3):
                tot = tot + self.RZ[j, d].astype(f32)
            self.RX[j, z] = tot.astype(bf16)
            for d in range(1, 4):
                self.cE(j, d).start()
            self.kept(j).start()

        def back_x(j):
            three = self.place(j).at[pl.ds(0, 3)]
            remote(three, three, self.sends.at[6, j], self.rE.at[j], {"z": (z + 1) % 4}).wait_recv()
            self.kept(j).wait()
            self.cF(j).start()

        def back_core(j):
            self.cF(j).wait_recv()
            self.cH(j).start()

        def done(j):
            self.cH(j).wait_recv()
            self.cB(j).wait_send()
            self.cC(j).wait_send()
            for d in range(1, 4):
                self.cD(j, d).wait_send()
                self.cE(j, d).wait_send()
            self.cF(j).wait_send()
            self.cH(j).wait_send()

        for count, run in zip(counts, (meet, scatter, gather, back_x, back_core, done)):
            each(count, k, run)


def backward_kernel(h1T, gp, act, df, dno, dnp, upo, upp, qkvt, qkvl, lse, gains, dcl, ldr1, wql, xlT, lay1, lay2,
                    sums, lsums, lbsum, dr2, a_n1, a_rs1, a_wout, a_woutp, a_wq, a_wqp, a_ctx, a_x,
                    res_f, res_a, gx, gxlT,
                    dh1, rs1, wout, woutp, wq, wqp, ctx, xs, dab, daT, bsum, sums1, DQ, DQL, dct_s, klT_s, avl, akl, dqT, dqlT,
                    small, WS, PF, PA, *ring_refs):
    k = pl.program_id(0)
    z, x, core, mp = (lax.axis_index(a) for a in ("z", "x", "core", "mp"))
    ini = ring_refs[-1]
    feed = Ring(ring_refs[0:4] + (res_f,) + ring_refs[8:18], (z, x, core, mp))
    att = Ring(ring_refs[4:8] + (res_a,) + ring_refs[18:28], (z, x, core, mp))

    def loads(i):
        a, b = ((dr2, dh1), (a_n1, dab), (a_rs1, rs1), (a_wout, wout), (a_woutp, woutp), (a_wq, wq), (a_wqp, wqp),
                (a_ctx, ctx), (a_x, xs))[i]
        return pltpu.make_async_copy(a, b, ini.at[i])

    @pl.when(k == 0)
    def _():
        loads(0).start()
        bar = pltpu.get_barrier_semaphore()
        for who in ({"core": 1 - core}, {"mp": 1 - mp}, {"x": 1 - x}):
            pl.semaphore_signal(bar, inc=1, device_id=who, device_id_type=MESH)
        for d in range(1, 4):
            pl.semaphore_signal(bar, inc=1, device_id={"z": (z + d) % 4}, device_id_type=MESH)
        pl.semaphore_wait(bar, 6)

    @pl.when(k == 1)
    def _():
        for i in range(1, 9):
            loads(i).start()

    @pl.when(k == FEED)
    def _():
        for i in range(1, 9):
            loads(i).wait()

    def feed_A(j):
        return remote(PF.at[1 - core], feed.RC.at[j], feed.sends.at[0, j], feed.rA.at[j], feed.C)

    def att_A(j):
        return remote(PA.at[j % 2, 1 - core], att.RC.at[j], att.sends.at[0, j], att.rA.at[j], att.C)

    def feed_B(j):
        feed_A(j).wait_recv()
        for i in range(2):
            feed.add(j, i, PF[core, i])
        feed.cB(j).start()
        feed_A(j).wait_send()

    def att_B(j):
        att_A(j).wait_recv()
        for i in range(2):
            att.add(j, i, PA[j % 2, core, i])
        att.cB(j).start()
        att_A(j).wait_send()

    each(feed_made, k - 1, feed_B)
    each(att_made, k - 1, att_B, 2)

    def put_half(h, i, c, t):
        PA[i % 2, c, 1 - h] = t.astype(bf16).reshape(2, 4, 16, WIDE)

    def put(h, i, t):
        put_half(h, i, 0, t[0:128])
        put_half(h, i, 1, t[128:256])

    dns, ups = (dno, dnp), (upo, upp)

    @pl.when(k < FEED)
    def _():
        dps = []
        for h in range(2):
            dp = (dot_nt(df[...], dns[h][...]) * gp[h].astype(f32)).astype(bf16)
            bsum[h, pl.ds(k, 1), :] = colsum(dp.astype(f32))
            t = dot(h1T[...], dp).astype(bf16)
            PF[0, 1 - h] = jnp.concatenate([t[0:256], t[256:512], t[512:768]], axis=1).reshape(2, 4, 32, WIDE)
            PF[1, 1 - h] = dot_tn(act[h], df[...]).astype(bf16).reshape(2, 4, 32, WIDE)
            dps.append(dp)

        @pl.when(k == 0)
        def _():
            loads(0).wait()

        dp = jnp.concatenate(dps, axis=1)
        up = jnp.concatenate([upo[...], upp[...]], axis=1)
        for r in range(2):
            rs = slice(512 * r, 512 * r + 512)
            dh1[rs, :] = dh1[rs, :] + dot_nt(dp[rs, :], up)

    def weigh(h, cols, *right):
        WS[h] = dot(cols[...], jnp.concatenate(right, axis=1)).astype(bf16)

    def two(h, lo, hi):
        return jnp.concatenate([WS[h, lo:hi, :], WS[h, 384 + lo:384 + hi, :]], axis=1)

    def pair(h, p):
        weigh(h, xs, DQ[h, 0, p], DQ[h, 1, p], DQ[h, 2, p])

    def layout_rows(h, lo, hi):
        return jnp.concatenate([lay1[h, lo:hi], lay2[h, lo:hi, 0:384]], axis=1).astype(bf16)

    def make(h, i):
        stack = lambda *v: jnp.concatenate(v, axis=0)
        if i == 0:
            weigh(h, daT, ctx[h])
            t = two(h, 0, 256)
        elif i == 1:
            t = stack(two(h, 256, 384), layout_rows(h, 0, 128))
        elif i == 2:
            pair(h, 0)
            t = stack(layout_rows(h, 128, 192), jnp.zeros((64, WIDE), bf16), two(h, 0, 128))
        elif i == 3:
            t = two(h, 128, 384)
        elif i == 4:
            pair(h, 1)
            t = two(h, 0, 256)
            put_half(h, 5, 0, two(h, 256, 384))
        elif i == 5:
            pair(h, 2)
            put_half(h, 5, 1, two(h, 0, 128))
            return
        elif i == 6:
            t = two(h, 128, 384)
        else:
            for pg in range(T_PAGES):
                rs = slice(SEQ * pg, SEQ * pg + SEQ)
                DQL[h, 0, rs, :] = dqlT[2 * h + pg].T.astype(bf16)
                DQL[h, 1, rs, :] = akl[2 * h + pg].astype(bf16)
                DQL[h, 2, rs, :] = avl[2 * h + pg].astype(bf16)
            xT = xlT[...]
            t = jnp.concatenate([dot(xT, DQL[h, 0]), dot(xT, DQL[h, 1]), dot(xT, DQL[h, 2]), lay2[h, :, 384:512],
                                 jnp.zeros((192, 256), f32)], axis=1)
            small[...] = jnp.zeros_like(small)
            for r, v in enumerate((sums1[0:1, :], sums[0:1, :], sums1[1:2, :], sums[1:2, :], sums1[2:3, :], sums[2:3, :])):
                small[r:r + 1, :] = v
            small[6:12, 0:192] = lsums[0:6, :]
            for n, c in enumerate((0, 2)):
                for p in range(3):
                    at = 384 * n + 128 * p
                    small[12:13, at:at + 128] = colsum(DQ[h, c, p].astype(f32))
                small[13:14, 128 * n:128 * n + 128] = colsum(DQL[h, c].astype(f32))
            for b in range(6):
                small[14 + b // 3:15 + b // 3, 256 * (b % 3):256 * (b % 3) + 256] = bsum[h, b:b + 1, :]
            small[16:17, 0:384] = lbsum[h]
            t = stack(t, small[...])
        put(h, i, t)

    for at in sorted(set(ATT_MADE)):
        @pl.when(k == at)
        def _(at=at):
            for i in range(N_ATT):
                if ATT_MADE[i] == at:
                    @pl.loop(0, 2)
                    def _(h, i=i):
                        make(h, i)

    each(feed_made, k, lambda j: feed_A(j).start())
    each(att_made, k, lambda j: att_A(j).start(), 2)

    @pl.when(k == FEED)
    def _():
        s1 = s2 = s3 = None
        for r in range(4):
            rs = slice(256 * r, 256 * r + 256)
            g = dh1[rs, :]
            n = dab[rs, :].astype(f32)
            d = norm_back(g * gains[0:1], n, rs1[rs, 0:1])
            dh1[rs, :] = d
            db = d.astype(bf16)
            dab[rs, :] = db
            daT[:, rs] = db.T
            t1, t2, t3 = colsum(g * n), colsum(g), colsum(d)
            s1, s2, s3 = (t1, t2, t3) if s1 is None else (s1 + t1, s2 + t2, s3 + t3)
        sums1[...] = jnp.concatenate([s1, s2, s3, jnp.zeros((5, WIDE), f32)], axis=0)

    @pl.when((k >= FEED) & (k < ATT))
    def _():
        a = k - FEED
        pair = a // 4
        hf = 1 - (a % 4) // 2
        page = a % 2
        at = 2 * hf + page
        rs = pl.ds(pl.multiple_of(page * SEQ, SEQ), SEQ)

        @pl.when(pair == 0)
        def _():
            avl[at] = jnp.zeros((SEQ, 128), f32)
            akl[at] = jnp.zeros((SEQ, 128), f32)
            dqlT[at] = jnp.zeros((128, SEQ), f32)

        ws = pl.ds(pl.multiple_of(pair * 128, 128), 128)
        for h, w in enumerate((wout, woutp)):
            @pl.when(hf == h)
            def _(w=w):
                dct_s[...] = dot_nt(dab[rs, :], w[ws, :]).astype(bf16)

        klT_s[...] = qkvl[0, 1].T
        qc = jnp.concatenate([qkvt[0, 0, 0], qkvl[0, 0]], axis=1)
        kc = jnp.concatenate([qkvt[0, 1, 0], qkvl[0, 1]], axis=1)
        vc = jnp.concatenate([qkvt[0, 2, 0], qkvl[0, 2]], axis=1)
        dc = jnp.concatenate([dct_s[...], dcl[0]], axis=1)
        ktT = qkvt[0, 1, 0].T
        zero = jnp.zeros_like(kc)
        av = ak = None
        for hh in range(2):
            h = 2 * pair + hh
            lane = lax.broadcasted_iota(jnp.int32, (1, 256), 1)
            mv = ((lane >= 64 * hh) & (lane < 64 * hh + 64)) | ((lane >= 128 + 16 * h) & (lane < 144 + 16 * h))
            mk = mv | (lane == 224)
            E = jnp.exp(dot_nt(jnp.where(mk, kc, zero), qc) - lse[0, 0, pl.ds(h, 1), :])
            dP = dot_nt(jnp.where(mv, vc, zero), dc)
            X = E * dP
            dS = (X - E * colsum(X)).astype(bf16)
            ov = dot(E.astype(bf16), jnp.where(mv, dc, zero))
            ok = dot(dS, jnp.where(mv, qc, zero))
            av = ov[:, :128] if av is None else av + ov[:, :128]
            ak = ok[:, :128] if ak is None else ak + ok[:, :128]
            avl[at] += ov[:, 128:]
            akl[at] += ok[:, 128:]
            ls = pl.ds(pl.multiple_of(16 * h, 16), 16)
            kT = jnp.concatenate([ktT[64 * hh:64 * hh + 64], klT_s[ls, :]], axis=0)
            oq = dot(kT, dS)
            dqT[64 * hh:64 * hh + 64, :] = oq[:64] * 0.125
            dqlT[at, ls, :] = oq[64:] * 0.25
        DQ[hf, 0, pair, rs, :] = dqT[...].T.astype(bf16)
        DQ[hf, 1, pair, rs, :] = ak.astype(bf16)
        DQ[hf, 2, pair, rs, :] = av.astype(bf16)

    @pl.when((k >= GRADS) & (k < GRADS + 4))
    def _():
        rs = pl.ds(pl.multiple_of((k - GRADS) * 256, 256), 256)
        g = dh1[rs, :]
        gl = ldr1[...]
        for h in range(2):
            for c in range(3):
                g = g + dot_nt(jnp.concatenate([DQ[h, c, p, rs, :] for p in range(3)], axis=1), (wq, wqp)[h][c])
                gl = gl + dot_nt(DQL[h, c, rs, :], wql[h, c])
        gx[...] = g
        gxlT[...] = gl.T

    feed.stages(k, [functools.partial(by_table, t) for t in FEED_STEPS])
    att.stages(k, [functools.partial(by_table, t) for t in ATT_STEPS])


def backward(h1T, gp, act, df, dno, dnp, upo, upp, qkvt, qkvl, lse, x, n1, rs1, gains, dcl, ldr1, wout, woutp, wq, wqp, wql,
             ctx, xlT, lay1, lay2, sums, lsums, lbsum, dr2):
    T = n1.shape[0]
    blk = lambda k: clip(k, 0, FEED - 1)
    att = lambda k: clip(k - FEED, 0, 11)
    head = lambda k: (1 - (att(k) % 4) // 2, att(k) % 2, att(k) // 4)
    D = pltpu.SemaphoreType.DMA
    V = pltpu.VMEM
    sd = jax.ShapeDtypeStruct
    hid = pl.BlockSpec((2, T, 256), lambda k: (0, 0, blk(k)))
    rowb = pl.BlockSpec((256, WIDE), lambda k: (blk(k), 0))
    colb = pl.BlockSpec((WIDE, 256), lambda k: (0, blk(k)))
    grow = lambda k: clip(k - GRADS, 0, 3)
    anyspec = pl.BlockSpec(memory_space=pl.ANY)
    in_specs = [
        whole(h1T), hid, hid, whole(df), rowb, rowb, colb, colb,
        pl.BlockSpec((1, 3, 1, SEQ, 128), lambda k: (head(k)[0], 0, head(k)[2], head(k)[1], 0)),
        pl.BlockSpec((1, 3, SEQ, 128), lambda k: (head(k)[0], 0, head(k)[1], 0)),
        pl.BlockSpec((1, 1, 8, SEQ), lambda k: (head(k)[0], head(k)[1], 0, 0)),
        whole(gains),
        pl.BlockSpec((1, SEQ, 128), lambda k: (head(k)[0], head(k)[1], 0)),
        pl.BlockSpec((256, 192), lambda k: (grow(k), 0)),
    ] + [whole(a) for a in (wql, xlT, lay1, lay2, sums, lsums, lbsum)] + [anyspec] * 9
    bufs = lambda n, r: [V((n, 2, 2, 4, r, WIDE), bf16), V((n, 2, 4, r, WIDE), bf16), V((n, 4, r, WIDE), bf16),
                         V((n, 3, r, WIDE), bf16)]
    sems = lambda n: [D((12, n))] + [D((n,))] * 9
    return pl.pallas_call(
        backward_kernel,
        grid=(BWD_STEPS,),
        in_specs=in_specs,
        out_specs=[anyspec, anyspec,
                   pl.BlockSpec((256, WIDE), lambda k: (grow(k), 0)),
                   pl.BlockSpec((192, 256), lambda k: (0, grow(k)))],
        out_shape=[sd((N_FEED, 2, 2, 4, 32, WIDE), bf16), sd((N_ATT, 2, 2, 4, 16, WIDE), bf16), sd((T, WIDE), f32),
                   sd((192, T), f32)],
        scratch_shapes=[
            V((T, WIDE), f32), V((T, 128), f32), V((384, WIDE), bf16), V((384, WIDE), bf16),
            V((3, WIDE, 384), bf16), V((3, WIDE, 384), bf16), V((2, T, 384), bf16), V((WIDE, T), bf16),
            V((T, WIDE), bf16), V((WIDE, T), bf16), V((2, 8, 256), f32), V((8, WIDE), f32),
            V((2, 3, 3, T, 128), bf16), V((2, 3, T, 128), bf16), V((SEQ, 128), bf16),
            V((128, SEQ), bf16), V((4, SEQ, 128), f32), V((4, SEQ, 128), f32), V((128, SEQ), f32), V((4, 128, SEQ), f32),
            V((64, WIDE), f32), V((2, WIDE, 384), bf16),
            V((2, 2, 2, 4, 32, WIDE), bf16), V((2, 2, 2, 2, 4, 16, WIDE), bf16)]
        + bufs(N_FEED, 32) + bufs(N_ATT, 16) + sems(N_FEED) + sems(N_ATT) + [D((9,))],
        compiler_params=pltpu.CompilerParams(collective_id=0, has_side_effects=True, vmem_limit_bytes=63 << 20),
        name="backward",
    )(h1T, gp, act, df, dno, dnp, upo, upp, qkvt, qkvl, lse, gains, dcl, ldr1, wql, xlT, lay1, lay2, sums, lsums, lbsum, dr2,
      n1, rs1, wout, woutp, wq, wqp, ctx, x)


def unpack_kernel(rf, a_ra, up, dn, qkv, out, lqkv, lup, ldnT, lout, qvb, upb, gain, shift, lqvb, lupb, lgain, lshift,
                  ra, sem):
    k = pl.program_id(0)
    load = pltpu.make_async_copy(a_ra, ra, sem)

    @pl.when(k == 0)
    def _():
        load.start()

    @pl.when(k < 6)
    def _():
        for i in range(3):
            up[256 * i:256 * i + 256, :] = rf[0:256, 256 * i:256 * i + 256].astype(f32)
        dn[...] = rf[256:512, :].astype(f32)

    @pl.when(k == 6)
    def _():
        load.wait()

    for p in range(3):
        @pl.when(k == 6 + p)
        def _(p=p):
            a = 640 + 384 * p
            for i in range(2):
                for c in range(3):
                    at = 384 * i + 128 * c
                    qkv[c, 384 * i:384 * i + 384, :] = ra[a:a + 384, at:at + 128].astype(f32)

    @pl.when(k == 6)
    def _():
        for i in range(2):
            out[:, 384 * i:384 * i + 384] = ra[0:384, 384 * i:384 * i + 384].astype(f32).T
        lup[...] = ra[384:576, 0:384].astype(f32)
        ldnT[...] = ra[384:576, 384:768].astype(f32)
        for c in range(3):
            lqkv[c] = ra[1792:1984, 128 * c:128 * c + 96].astype(f32)
        lout[...] = ra[1792:1984, 384:512].astype(f32).T[:96, :]
        s = ra[1984:2016, :].astype(f32)
        gain[...] = s[0:2]
        shift[...] = s[2:6]
        lgain[...] = s[6:8, 0:192]
        lshift[...] = s[8:12, 0:192]
        for i in range(2):
            qvb[i:i + 1, :] = s[12:13, 384 * i:384 * i + 384]
            lqvb[i:i + 1, :] = s[13:14, 128 * i:128 * i + 96]
            for j in range(6):
                upb[6 * i + j:6 * i + j + 1, :] = s[14 + i:15 + i, 128 * j:128 * j + 128]
        for j in range(3):
            lupb[j:j + 1, :] = s[16:17, 128 * j:128 * j + 128]


def unpack(feed, att):
    const = lambda s: pl.BlockSpec(s, lambda k: (0,) * len(s))
    sd = jax.ShapeDtypeStruct
    shapes = [(768, 1536), (1536, 768), (3, 768, 384), (384, 768), (3, 192, 96), (192, 384), (192, 384), (96, 192),
              (2, 384), (12, 128), (2, 768), (4, 768), (2, 96), (3, 128), (2, 192), (4, 192)]
    specs = [const(s) for s in shapes]
    specs[0] = pl.BlockSpec((768, 256), lambda k: (0, clip(k, 0, 5)))
    specs[1] = pl.BlockSpec((256, 768), lambda k: (clip(k, 0, 5), 0))
    specs[2] = pl.BlockSpec((3, 768, 128), lambda k: (0, 0, clip(k - 6, 0, 2)))
    return pl.pallas_call(
        unpack_kernel, grid=(9,),
        in_specs=[pl.BlockSpec((512, 768), lambda k: (clip(k, 0, 5), 0)), pl.BlockSpec(memory_space=pl.ANY)],
        out_specs=specs, out_shape=[sd(s, f32) for s in shapes],
        scratch_shapes=[pltpu.VMEM((N_ATT * 256, WIDE), bf16), pltpu.SemaphoreType.DMA],
        compiler_params=pltpu.CompilerParams(vmem_limit_bytes=56 << 20), name="unpack_gradients",
    )(feed, att)


def body(n_group, text_states, layout_states, box_counts, text_qkv, text_qv_bias, text_out, text_up, text_up_bias,
         text_down, text_gains, text_shifts, layout_qkv, layout_qv_bias, layout_out, layout_up, layout_up_bias,
         layout_down, layout_gains, layout_shifts, cot_text, cot_layout):
    tq = jnp.transpose(text_qkv, (1, 0, 2))
    lq = jnp.transpose(layout_qkv, (1, 0, 2))
    xlT = layout_states.T
    (qkvt, qkvl, lse, ctx, out_lT, ldr1, dcl, lay1, lay2, lsums, lbsum, lqp, out_t, act, gp, h1T, xT, df, dr2, n1, rs1, sums,
     wq, wo, wu, wd) = forward(
        box_counts, text_states, xlT, tq, lq, text_out, layout_out, layout_up, layout_down.T, text_up, text_down,
        text_qv_bias, layout_qv_bias, text_up_bias.reshape(12, 128), layout_up_bias.reshape(3, 128), layout_gains,
        layout_shifts, cot_layout.T, text_gains, text_shifts, cot_text)
    feed, att, gx, gxlT = backward(h1T, gp, act, df, text_down, wd, text_up, wu, qkvt, qkvl, lse, xT, n1, rs1,
                             text_gains, dcl, ldr1, text_out, wo, tq, wq, lqp, ctx, xlT, lay1, lay2, sums, lsums, lbsum,
                             dr2)
    feed = feed.reshape(N_FEED * 512, WIDE)
    att = att.reshape(N_ATT * 256, WIDE)
    if n_group > 1:
        feed, att = lax.psum((feed, att), "group")
    (g_up, g_dn, g_qkv, g_o, gl_qkv, gl_up, gl_dnT, gl_o, qvb, upb, gain, shift, lqvb, lupb, lgain, lshift) = unpack(feed, att)
    swap = lambda a: jnp.transpose(a, (1, 0, 2))
    return (out_t, out_lT.T, gx, gxlT.T, swap(g_qkv), qvb, g_o, g_up, upb.reshape(1536), g_dn, gain, shift,
            swap(gl_qkv), lqvb, gl_o, gl_up, lupb.reshape(384), gl_dnT.T, lgain, lshift)


def solution(mesh):
    dp = mesh.shape["dp"]
    n_group = dp // 16
    fine = Mesh(mesh.devices.reshape(n_group, 4, 2, 2, 2), AXES)
    rows = P(AXES, None)
    half2 = P(None, "mp")
    half1 = P("mp", None)
    qkv = P(None, None, "mp")
    rep = P()
    return jax.shard_map(
        functools.partial(body, n_group),
        mesh=fine,
        in_specs=(rows, rows, P(AXES[:4]), qkv, half2, half1, half2, P("mp"), half1, rep, rep,
                  qkv, half2, half1, half2, P("mp"), half1, rep, rep, rows, rows),
        out_specs=(rows, rows, rows, rows, qkv, half2, half1, half2, P("mp"), half1, rep, rep,
                   qkv, half2, half1, half2, P("mp"), half1, rep, rep),
        check_vma=False,
    )
```
